128 devices in a mesh: vintage: 2 (over core), tile: 64 (over x, y, z).
Axes of the slice: x: 4, y: 4, z: 4, core: 2. Of those that a mesh axis runs over, the one named last changes fastest.
Arguments:
- patches: bfloat16 [2, 32768, 768], P('vintage', 'tile'), may hold values from -16 to 16, as said below
- out_grad: bfloat16 [2, 32768, 768], P('vintage', 'tile'), may hold values from -6 to 6
- w_query: bfloat16 [768, 768], replicated, may hold values from -0.21875 to 0.21875
- w_key: bfloat16 [768, 256], replicated, may hold values from -0.21875 to 0.21875
- w_value: bfloat16 [768, 256], replicated, may hold values from -0.21875 to 0.21875
- w_out: bfloat16 [768, 768], replicated, may hold values from -0.21875 to 0.21875
- key_tiles: int32 [2, 256, 16], P('vintage'), may hold values from 0 to 63, all different within a row; in each aligned block of 4 rows (0 to 3, 4 to 7, ..., all dimensions but the last counted through in order) at most 2 rows name the same one
- key_blocks: int32 [2, 256, 16], P('vintage'), may hold values from 0 to 3
Outputs:
- layer_out: bfloat16 [2, 32768, 768], P('vintage', 'tile')
- input_grad: bfloat16 [2, 32768, 768], P('vintage', 'tile')
The draws below stay inside these ranges and needn't reach their ends.
Inputs may be any that keep to these rules, and one draw needn't show every extreme that they name: `patches`: patch features of order one, rows of differing scale possible. `key_tiles`: the 16 tiles of one query block's list differ; over the 4 query blocks of one tile no key tile is named more than 2 times, and in every draw some tile is named exactly 2 times by some tile's blocks.
All inputs are finite; a program needn't handle non-finite values.
Results may differ from the reference program's by a relative error of at most 0.012.
The reference program's roundings to bfloat16 on the way count: a program that leaves them out, or rounds other values in their place, can miss the bound.
Values may be sent and summed in bfloat16 or wider, within the bound.
A program may use at most 128 MiB of HBM per device.

```python
import math
import jax
import jax.numpy as jnp
import numpy as np
from jax import lax

D = 768
HEADS = 12
KV_HEADS = 4
HEAD_DIM = 64
BLK = 128
CAP = 2
QB = 4
LIST_LEN = 16
PATCHES = 32768
QBLOCKS = 256
N_TILE = 64


def draw_patches(key, part):
    first_key = jax.random.fold_in(jax.random.fold_in(key, 17), 0)
    base = jax.random.normal(first_key, (2, PATCHES, D), jnp.float32)
    return jnp.clip(base, -6.0, 6.0).astype(jnp.bfloat16)


def touch_ends(drawn, rng, low, top_value):
    spot = [jax.random.randint(jax.random.fold_in(rng, axis), (), 0, length) for axis, length in enumerate(drawn.shape)]
    main_axis = drawn.shape.index(max(drawn.shape))
    beside = spot[:main_axis] + [(spot[main_axis] + 1) % drawn.shape[main_axis]] + spot[main_axis + 1:]
    return drawn.at[tuple(spot)].set(low).at[tuple(beside)].set(top_value)


def levels(rng, shape, shards, smallest, largest):
    level = 1.0
    for position, blocks in shards:
        draws = jax.random.uniform(jax.random.fold_in(jax.random.fold_in(rng, 6), position), (blocks,), jnp.float32, smallest / len(shards), largest / len(shards))
        level = level * jnp.repeat(jnp.exp(draws), shape[position] // blocks).reshape((-1,) + (1,) * (len(shape) - 1 - position))
    return level


def deal_out(key, own, number, rows, number_of, top, reach, lean):
    order = jax.random.permutation(key, number_of)
    heavy_load, usual = load_shares(number_of, rows * top, reach, lean, True), load_shares(number_of, rows * top, reach, lean, False)
    places = jnp.arange(number_of)

    def named(sizes, rotation):
        used = int((sizes > 0).sum())
        fixed = max(1, used // 4)
        shifted = fixed + (places - fixed + rotation * (used - fixed)) % max(1, number_of - fixed)
        return jnp.zeros((number_of,), jnp.int32).at[order[jnp.where(places < fixed, places, shifted)]].set(jnp.asarray(sizes, jnp.int32))

    sizes = jnp.where(number % 4 == 0, named(heavy_load, number // 4), named(usual, number - number // 4 - 1))
    mixed = jax.random.permutation(jax.random.fold_in(own, 3), number_of)
    source_of, taker = mixed[0:number_of // 2 * 2:2], mixed[1:number_of // 2 * 2:2]
    margin = jnp.minimum(sizes[source_of] - 1, reach - sizes[taker]) // 2
    margin = jnp.where((source_of == order[0]) | (taker == order[0]) | (sizes[taker] == 0), 0, jnp.maximum(margin, 0))
    shifted = jax.random.randint(jax.random.fold_in(own, 4), (number_of // 2,), 0, 1 << 20) % (margin + 1)
    sizes = sizes.at[source_of].add(-shifted).at[taker].add(shifted)
    labels = jnp.searchsorted(jnp.cumsum(sizes), jnp.arange(rows * top), side="right").astype(jnp.int32)
    table = labels.reshape(top, rows).T
    table = table[jax.random.permutation(jax.random.fold_in(own, 1), rows)]
    rotation = jax.random.randint(jax.random.fold_in(own, 2), (rows, 1), 0, top)
    return jnp.take_along_axis(table, (jnp.arange(top)[None, :] + rotation) % top, axis=1)


def load_shares(number_of, total, reach, skew, full):
    loads = [(1 << 20) // math.isqrt(rank ** skew) + 1 for rank in range(1, number_of + 1)]
    largest = reach if full else min(reach, max(-(-total // number_of), total * loads[0] // sum(loads)))
    least = 1 if total - largest >= number_of - 1 else 0
    holding, rest = [largest] + [least] * (number_of - 1), total - largest - least * (number_of - 1)
    while rest > 0:
        free = [i for i in range(1, number_of) if holding[i] < largest] or [i for i in range(1, number_of) if holding[i] < reach]
        mass, remaining = sum([loads[i] for i in free]), rest
        for i in free:
            extra = min(reach - holding[i], max(1, remaining * loads[i] // mass), rest)
            holding[i] = holding[i] + extra
            rest = rest - extra
    return np.array(holding)


def centred(key, dims, scale, bound, shards=(), kind=jnp.bfloat16):
    result = jax.random.normal(key, dims, jnp.float32) * scale
    if len(shards) > 0:
        result = levels(key, dims, shards, -0.22, 0.18) * result
    return jnp.clip(result, min=-bound, max=bound).astype(kind)


def setup_inputs(seed: int = 0) -> dict:
    key_of = jax.random.split(jax.random.key(seed), 9)
    patches = draw_patches(jax.random.fold_in(key_of[8], 71), 0)
    out_grad = centred(key_of[1], (2, PATCHES, D), 1.0, 6.0, ((0, 2), (1, 64)))
    w_query = centred(key_of[2], (D, HEADS * HEAD_DIM), D ** -0.5, 0.21875)
    w_key = centred(key_of[3], (D, KV_HEADS * HEAD_DIM), D ** -0.5, 0.21875)
    w_value = centred(key_of[4], (D, KV_HEADS * HEAD_DIM), D ** -0.5, 0.21875)
    w_out = centred(key_of[5], (HEADS * HEAD_DIM, D), (HEADS * HEAD_DIM) ** -0.5, 0.21875)
    key_tiles_keys = jax.random.split(jax.random.fold_in(key_of[6], 1), 2 * QBLOCKS // QB)
    key_tiles_turns = jax.random.permutation(jax.random.fold_in(key_of[6], 3), 2 * QBLOCKS // QB)
    key_tiles = jax.vmap(lambda own, number: deal_out(jax.random.fold_in(key_of[6], 2), own, number, QB, N_TILE, LIST_LEN, CAP, 2))(key_tiles_keys, key_tiles_turns).reshape((2, QBLOCKS, LIST_LEN))
    key_blocks = touch_ends(jax.random.randint(key_of[7], (2, QBLOCKS, LIST_LEN), 0, QB), jax.random.fold_in(key_of[7], 1), 0, QB - 1).astype(jnp.int32)
    return dict(patches=patches, out_grad=out_grad, w_query=w_query, w_key=w_key, w_value=w_value, w_out=w_out, key_tiles=key_tiles, key_blocks=key_blocks)


EPSILON = 1e-06

def attend_block(query_rows, grad_rows, key_value, w_out):
    kv_width = KV_HEADS * HEAD_DIM
    group_size = HEADS // KV_HEADS
    temper = HEAD_DIM ** (-0.5)
    row_count = query_rows.shape[0]
    keys_f = key_value[:, :kv_width].astype(jnp.float32).reshape(-1, KV_HEADS, HEAD_DIM)
    values_f = key_value[:, kv_width:].astype(jnp.float32).reshape(-1, KV_HEADS, HEAD_DIM)
    query_f = query_rows.astype(jnp.float32).reshape(row_count, KV_HEADS, group_size, HEAD_DIM)
    scores = jnp.einsum('igrd,ngd->grin', query_f, keys_f) * temper
    peak = lax.optimization_barrier(jnp.max(scores, axis=-1, keepdims=True))
    expo = jnp.exp(scores - peak)
    probs = expo / lax.optimization_barrier(jnp.sum(expo, axis=-1, keepdims=True))
    probs_low = lax.optimization_barrier(probs.astype(jnp.bfloat16))
    probs_lf = probs_low.astype(jnp.float32)
    attended = jnp.einsum('grin,ngd->igrd', probs_lf, values_f).reshape(row_count, HEADS * HEAD_DIM)
    attended = lax.optimization_barrier(attended.astype(jnp.bfloat16))
    attended_f = attended.astype(jnp.float32)
    root_mean = jnp.sqrt(lax.optimization_barrier(jnp.mean(attended_f * attended_f, axis=-1, keepdims=True)) + EPSILON)
    normed = attended_f / root_mean
    layer_rows = jnp.dot(normed.astype(jnp.bfloat16), w_out, preferred_element_type=jnp.float32).astype(jnp.bfloat16)
    normed_grad = jnp.dot(grad_rows, w_out.T, preferred_element_type=jnp.float32)
    attended_grad = (normed_grad - normed * lax.optimization_barrier(jnp.mean(normed_grad * normed, axis=-1, keepdims=True))) / root_mean
    attended_grad = lax.optimization_barrier(attended_grad.astype(jnp.bfloat16))
    grad_f = attended_grad.astype(jnp.float32).reshape(row_count, KV_HEADS, group_size, HEAD_DIM)
    prob_grad = jnp.einsum('igrd,ngd->grin', grad_f, values_f)
    row_dot = lax.optimization_barrier(jnp.sum(probs * prob_grad, axis=-1, keepdims=True))
    score_grad = lax.optimization_barrier((probs * (prob_grad - row_dot) * temper).astype(jnp.bfloat16))
    score_f = score_grad.astype(jnp.float32)
    query_grad = jnp.einsum('grin,ngd->igrd', score_f, keys_f).reshape(row_count, HEADS * HEAD_DIM).astype(jnp.bfloat16)
    key_part = jnp.einsum('grin,igrd->ngd', score_f, query_f).reshape(-1, kv_width)
    value_part = jnp.einsum('grin,igrd->ngd', probs_lf, grad_f).reshape(-1, kv_width)
    parts = jnp.concatenate([key_part, value_part], axis=-1).astype(jnp.bfloat16)
    return (layer_rows, query_grad, parts.reshape(-1, row_count, 2 * kv_width))

def reference(patches, out_grad, w_query, w_key, w_value, w_out, key_tiles, key_blocks):
    kv_width = KV_HEADS * HEAD_DIM
    kv_cubes = []
    for vintage in range(2):
        keys = jnp.dot(patches[vintage], w_key, preferred_element_type=jnp.float32).astype(jnp.bfloat16)
        values = jnp.dot(patches[vintage], w_value, preferred_element_type=jnp.float32).astype(jnp.bfloat16)
        kv_cubes.append(jnp.concatenate([keys, values], axis=-1).reshape(QBLOCKS, BLK, 2 * kv_width))
    kv_terms = [None, None]
    layer_outs = []
    query_grads = []
    for vintage in range(2):
        other = 1 - vintage
        queries = jnp.dot(patches[vintage], w_query, preferred_element_type=jnp.float32).astype(jnp.bfloat16)
        queries = queries.reshape(QBLOCKS, BLK, HEADS * HEAD_DIM)
        grads = out_grad[vintage].reshape(QBLOCKS, BLK, D)
        block_ids = (key_tiles[vintage].astype(jnp.int32) * QB + key_blocks[vintage].astype(jnp.int32)).astype(jnp.int32)
        source = kv_cubes[other]

        def step(summed, item):
            query_rows, grad_rows, entry_ids = item
            key_value = source[entry_ids].reshape(-1, 2 * kv_width)
            layer_rows, query_grad, parts = attend_block(query_rows, grad_rows, key_value, w_out)
            summed = summed.at[entry_ids].add(parts.astype(jnp.float32))
            return (summed, (layer_rows, query_grad))
        start = jnp.zeros((QBLOCKS, BLK, 2 * kv_width), jnp.float32)
        summed, (layer_rows, query_grad) = lax.scan(step, start, (queries, grads, block_ids))
        kv_grad = summed.astype(jnp.bfloat16).reshape(PATCHES, 2 * kv_width)
        kv_terms[other] = jnp.dot(kv_grad[:, :kv_width], w_key.T, preferred_element_type=jnp.float32) + jnp.dot(kv_grad[:, kv_width:], w_value.T, preferred_element_type=jnp.float32)
        layer_outs.append(layer_rows.reshape(PATCHES, D))
        query_grads.append(query_grad.reshape(PATCHES, HEADS * HEAD_DIM))
    input_grads = []
    for vintage in range(2):
        total = jnp.dot(query_grads[vintage], w_query.T, preferred_element_type=jnp.float32) + kv_terms[vintage]
        input_grads.append(total.astype(jnp.bfloat16))
    return (jnp.stack(layer_outs), jnp.stack(input_grads))
```

```python
import functools

import jax
import jax.numpy as jnp
from jax import lax
from jax.experimental import pallas as pl
from jax.experimental.pallas import tpu as pltpu
from jax.sharding import PartitionSpec as P

CAP = 2
LOG2E = 1.4426950408889634
EPSILON = 1e-06
F32, BF16 = jnp.float32, jnp.bfloat16

def swap_halves(x):
    return jnp.concatenate([x[:, 64:], x[:, :64]], axis=1)

def dot(a, b, ca=1, cb=0):
    return lax.dot_general(a, b, (((ca,), (cb,)), ((), ())), preferred_element_type=F32)

def attend_kernel(slots, q_ref, go_ref, wo_ref, arr_ref, lay_ref, dq_ref, out_ref,
                  kv, stage, qp, dop, p, t, acc, stat, att, in_sem, out_sem, *, NC1, NC2):
    b = pl.program_id(0)
    nb = pl.num_programs(0)
    L = kv.shape[1]

    def fetch(blk, slot):
        return [pltpu.make_async_copy(arr_ref.at[slots[blk * L + l]], kv.at[slot, l], in_sem.at[slot, l]) for l in range(L)]

    def put(blk, slot):
        return [pltpu.make_async_copy(stage.at[slot, l], out_ref.at[slots[blk * L + l]], out_sem.at[slot, l]) for l in range(L)]

    cur = lax.rem(b, 2)

    @pl.when(b == 0)
    def _():
        for c in fetch(0, 0):
            c.start()

    @pl.when(b + 1 < nb)
    def _():
        for c in fetch(b + 1, 1 - cur):
            c.start()

    low = lax.broadcasted_iota(jnp.int32, (128, 128), 1) < 64

    def pad_heads(src, dst):
        for h in range(12):
            g = h // 3
            tile = src[:, (h // 2) * 128:(h // 2) * 128 + 128]
            if h % 2 != g % 2:
                tile = swap_halves(tile)
            tile = jnp.where(low if g % 2 == 0 else ~low, tile, jnp.zeros_like(tile))
            dst[g // 2, ((g % 2) * 3 + h % 3) * 128:((g % 2) * 3 + h % 3) * 128 + 128, :] = tile.astype(BF16)

    def unpad(src, j):
        parts = []
        for h in (2 * j, 2 * j + 1):
            g = h // 3
            rows = ((g % 2) * 3 + h % 3) * 128
            tile = src[g // 2, rows:rows + 128, :]
            if h % 2 != g % 2:
                tile = swap_halves(tile)
            parts.append(tile)
        return jnp.where(low, parts[0], parts[1])

    pad_heads(q_ref[...].astype(F32), qp)
    for c in fetch(b, cur):
        c.wait()

    scale = 0.125 * LOG2E
    R = 768
    for c in range(2):
        def scores(n, m):
            e0 = n * (NC1 // 128)
            k = kv[cur, pl.ds(e0, NC1 // 128), c * 128:c * 128 + 128, :].reshape(NC1, 128)
            s = dot(qp[c], k, 1, 1)
            p[c, :, pl.ds(pl.multiple_of(n * NC1, 128), NC1)] = s
            for i in range(NC1 // 128):
                m = jnp.maximum(m, s[:, i * 128:i * 128 + 128])
            return m
        m = lax.fori_loop(0, 2048 // NC1, scores, jnp.full((R, 128), -jnp.inf, F32))
        stat[...] = jnp.broadcast_to(jnp.max(m, axis=1, keepdims=True), (R, 128))

        def expo(n, tot):
            cols = pl.ds(pl.multiple_of(n * NC1, 128), NC1)
            mm = stat[...]
            for i in range(NC1 // 128):
                cols = pl.ds(pl.multiple_of(n * NC1 + i * 128, 128), 128)
                e = jnp.exp2((p[c, :, cols] - mm) * scale)
                p[c, :, cols] = e
                tot = tot + e
            return tot
        tot = lax.fori_loop(0, 2048 // NC1, expo, jnp.zeros((R, 128), F32))
        stat[...] = jnp.broadcast_to(1.0 / jnp.sum(tot, axis=1, keepdims=True), (R, 128))
        acc[c] = jnp.zeros((R, 128), F32)

        def attend(n, _):
            inv = stat[...]
            e0 = n * (NC1 // 128)
            v = kv[cur, pl.ds(e0, NC1 // 128), 256 + c * 128:256 + c * 128 + 128, :].reshape(NC1, 128)
            pl_ = []
            for i in range(NC1 // 128):
                cols = pl.ds(pl.multiple_of(n * NC1 + i * 128, 128), 128)
                pr = p[c, :, cols] * inv
                p[c, :, cols] = pr
                pl_.append(pr.astype(BF16))
            acc[c] += dot(jnp.concatenate(pl_, axis=1), v)
            return 0
        lax.fori_loop(0, 2048 // NC1, attend, 0)

    ss = jnp.zeros((128, 128), F32)
    for j in range(6):
        a = unpad(acc, j).astype(BF16).astype(F32)
        att[:, j * 128:j * 128 + 128] = a
        ss = ss + a * a
    root = jnp.sqrt(jnp.sum(ss, axis=1, keepdims=True) * (1.0 / 768) + EPSILON)
    normed = att[...] / root
    lay_ref[...] = dot(normed.astype(BF16), wo_ref[...]).astype(BF16)
    ng = dot(go_ref[...], wo_ref[...], 1, 1)
    ag = (ng - normed * (jnp.sum(ng * normed, axis=1, keepdims=True) * (1.0 / 768))) / root
    pad_heads(ag.astype(BF16).astype(F32), dop)

    @pl.when(b >= 2)
    def _():
        for cp in put(b - 2, cur):
            cp.wait()

    for c in range(2):
        dos = (dop[c].astype(F32) * 0.125).astype(BF16)

        def pgrad(n, rd):
            e0 = n * (NC1 // 128)
            v = kv[cur, pl.ds(e0, NC1 // 128), 256 + c * 128:256 + c * 128 + 128, :].reshape(NC1, 128)
            dp = dot(dos, v, 1, 1)
            for i in range(NC1 // 128):
                cols = pl.ds(pl.multiple_of(n * NC1 + i * 128, 128), 128)
                x = dp[:, i * 128:i * 128 + 128] * p[c, :, cols]
                t[:, cols] = x
                rd = rd + x
            return rd
        rd = lax.fori_loop(0, 2048 // NC1, pgrad, jnp.zeros((R, 128), F32))
        stat[...] = jnp.broadcast_to(jnp.sum(rd, axis=1, keepdims=True), (R, 128))
        acc[c] = jnp.zeros((R, 128), F32)

        def grads(n, _):
            rdb = stat[...]
            e0 = n * (NC2 // 128)
            ne = NC2 // 128
            k = kv[cur, pl.ds(e0, ne), c * 128:c * 128 + 128, :].reshape(NC2, 128)
            ds_, pl_ = [], []
            for i in range(ne):
                cols = pl.ds(pl.multiple_of(n * NC2 + i * 128, 128), 128)
                pr = p[c, :, cols]
                ds_.append((t[:, cols] - pr * rdb).astype(BF16))
                pl_.append(pr.astype(BF16))
            ds_ = jnp.concatenate(ds_, axis=1)
            pl_ = jnp.concatenate(pl_, axis=1)
            acc[c] += dot(ds_, k)
            dk = dot(ds_, qp[c], 0, 0)
            dv = dot(pl_, dop[c], 0, 0)
            stage[cur, pl.ds(e0, ne), c * 128:c * 128 + 128, :] = dk.astype(BF16).reshape(ne, 128, 128)
            stage[cur, pl.ds(e0, ne), 256 + c * 128:256 + c * 128 + 128, :] = dv.astype(BF16).reshape(ne, 128, 128)
            return 0
        lax.fori_loop(0, 2048 // NC2, grads, 0)

    for j in range(6):
        dq_ref[:, j * 128:j * 128 + 128] = unpad(acc, j).astype(BF16)

    for cp in put(b, cur):
        cp.start()

    @pl.when(b == nb - 1)
    def _():
        for cp in put(b - 1, 1 - cur):
            cp.wait()
        for cp in put(b, cur):
            cp.wait()

def attention(slots, queries, grads, w_out, arr, NC1=256, NC2=256):
    rows, D = queries.shape
    nb = rows // 128
    L = slots.shape[0] // nb
    ns = arr.shape[0]
    row = lambda b, s: (b, 0)
    return pl.pallas_call(
        functools.partial(attend_kernel, NC1=NC1, NC2=NC2),
        grid_spec=pltpu.PrefetchScalarGridSpec(
            num_scalar_prefetch=1, grid=(nb,),
            in_specs=[pl.BlockSpec((128, D), row), pl.BlockSpec((128, D), row),
                      pl.BlockSpec((D, D), lambda b, s: (0, 0), pipeline_mode=pl.Buffered(1)),
                      pl.BlockSpec(memory_space=pl.ANY)],
            out_specs=[pl.BlockSpec((128, D), row), pl.BlockSpec((128, D), row), pl.BlockSpec(memory_space=pl.ANY)],
            scratch_shapes=[
                pltpu.VMEM((2, L, 512, 128), BF16), pltpu.VMEM((2, L, 512, 128), BF16),
                pltpu.VMEM((2, 768, 128), BF16), pltpu.VMEM((2, 768, 128), BF16),
                pltpu.VMEM((2, 768, 2048), F32), pltpu.VMEM((768, 2048), F32),
                pltpu.VMEM((2, 768, 128), F32), pltpu.VMEM((768, 128), F32), pltpu.VMEM((128, 768), F32),
                pltpu.SemaphoreType.DMA((2, L)), pltpu.SemaphoreType.DMA((2, L))]),
        out_shape=[jax.ShapeDtypeStruct((rows, D), BF16), jax.ShapeDtypeStruct((rows, D), BF16),
                   jax.ShapeDtypeStruct((ns, 512, 128), BF16)],
        compiler_params=pltpu.CompilerParams(dimension_semantics=("arbitrary",), vmem_limit_bytes=60 * 2**20),
        name="attend",
    )(slots, queries, grads, w_out, arr)


MESH = pl.DeviceIdType.MESH
SIDE = 4
ORDERS = ((0, 1, 2), (1, 2, 0), (2, 0, 1))
PIECES = ((0, 176), (176, 176), (352, 160))
STRIDE = (16, 4, 1)


def place():
    tile = lax.axis_index("tile")
    return [lax.rem(lax.div(tile, s), SIDE) for s in STRIDE]


def shifted(pos, axis, by):
    moved = list(pos)
    moved[axis] = lax.rem(pos[axis] + by, SIDE)
    return moved


def tile_of(pos):
    return pos[0] * 16 + pos[1] * 4 + pos[2]


def greet(pos, core):
    barrier = pltpu.get_barrier_semaphore()
    count = 0
    for axis in range(3):
        for by in (1, 3):
            pl.semaphore_signal(barrier, inc=1, device_id=(core, tile_of(shifted(pos, axis, by))), device_id_type=MESH)
            count += 1
    pl.semaphore_signal(barrier, inc=1, device_id=(1 - core, tile_of(pos)), device_id_type=MESH)
    pl.semaphore_wait(barrier, count + 1)


class Sender:
    def __init__(self, pos, core, send_sem, recv_sem):
        self.pos, self.core, self.send_sem, self.recv_sem = pos, core, send_sem, recv_sem
        self.done = []

    def copy(self, src, dst, sem, axis, by):
        c = pltpu.make_async_remote_copy(
            src_ref=src, dst_ref=dst, send_sem=self.send_sem.at[sem], recv_sem=self.recv_sem.at[sem],
            device_id=(self.core, tile_of(shifted(self.pos, axis, by))), device_id_type=MESH)
        c.start()
        self.done.append(c)
        return c


def at_axis(ref, dims, index, axis, *rest):
    return ref.at[tuple(index if d == axis else slice(None) for d in dims) + rest]


def spread_kernel(wanted, mine_ref, out_ref, own, plane0, plane1, plane2, st0, st1, st2, rl0, rl1, rl2,
                  send_sem, recv_sem, swap_sem, local_sem):
    pos, core = place(), lax.axis_index("vintage")
    planes, stages, relays = (plane0, plane1, plane2), (st0, st1, st2), (rl0, rl1, rl2)
    greet(pos, core)
    swap = pltpu.make_async_remote_copy(
        src_ref=mine_ref, dst_ref=own, send_sem=swap_sem.at[0], recv_sem=swap_sem.at[1],
        device_id=(1 - core, tile_of(pos)), device_id_type=MESH)
    swap.start()
    swap.wait()
    send = Sender(pos, core, send_sem, recv_sem)
    dims = [tuple(sorted(o[:2])) for o in ORDERS]
    local = []

    def line(p, axis):
        return at_axis(planes[p], dims[p], pos[axis], axis)

    def cell(p, a1, i1, a2, i2, *rest):
        return planes[p].at[tuple(i1 if d == a1 else i2 for d in dims[p]) + rest]

    for p, (r0, rows) in enumerate(PIECES):
        a1, a2, a3 = ORDERS[p]
        c = pltpu.make_async_copy(own.at[:, pl.ds(r0, rows), :], cell(p, a1, pos[a1], a2, pos[a2]), local_sem.at[p])
        c.start()
        local.append(c)
    first = []
    for p in range(3):
        a1, a2, a3 = ORDERS[p]
        local[p].wait()
        here = cell(p, a1, pos[a1], a2, pos[a2])
        first.append([send.copy(here, here, p * 12 + i, a1, by) for i, by in enumerate((1, 3))])
    second = []
    for p in range(3):
        a1, a2, a3 = ORDERS[p]
        got = []
        for i, by in enumerate((1, 3)):
            first[p][i].wait_recv()
            part = cell(p, a1, lax.rem(pos[a1] + SIDE - by, SIDE), a2, pos[a2], pl.ds(2 * i, 2))
            got.append(send.copy(part, part, p * 12 + 2 + i, a1, by))
        second.append(got)
    third = []
    for p in range(3):
        a1, a2, a3 = ORDERS[p]
        for c in second[p]:
            c.wait_recv()
        here = line(p, a2)
        third.append([send.copy(here, here, p * 12 + 4 + i, a2, by) for i, by in enumerate((1, 3))])
    fourth = []
    for p in range(3):
        a1, a2, a3 = ORDERS[p]
        got = []
        for i, by in enumerate((1, 3)):
            third[p][i].wait_recv()
            other = lax.rem(pos[a2] + SIDE - by, SIDE)
            part = planes[p].at[tuple(other if d == a2 else pl.ds(2 * i, 2) for d in dims[p])]
            got.append(send.copy(part, part, p * 12 + 6 + i, a2, by))
        fourth.append(got)

    def landing(p, source, half=None):
        a3 = ORDERS[p][2]
        r0, rows = PIECES[p]
        idx = []
        for d in range(3):
            if d == a3:
                idx.append(source)
            elif half is not None and d == dims[p][0]:
                idx.append(pl.ds(2 * half, 2))
            else:
                idx.append(slice(None))
        return out_ref.at[tuple(idx) + (slice(None), pl.ds(r0, rows), slice(None))]

    fifth = []
    for p in range(3):
        a1, a2, a3 = ORDERS[p]
        r0, rows = PIECES[p]
        for c in fourth[p]:
            c.wait_recv()

        def pick(k, by, p=p, a3=a3):
            dest = tile_of(shifted(pos, a3, by))

            def one(j, _):
                hi, lo = lax.div(j, SIDE), lax.rem(j, SIDE)
                source = pos[a3] * STRIDE[a3] + hi * STRIDE[dims[p][0]] + lo * STRIDE[dims[p][1]]
                for s in range(2):
                    blk = jnp.maximum(wanted[dest * 128 + s * 64 + source], 0)
                    stages[p][k, hi, lo, s] = planes[p][hi, lo, blk]
                return 0
            lax.fori_loop(0, SIDE * SIDE, one, 0)

        got = []
        pick(2, 2)
        for i, by in enumerate((1, 3)):
            got.append(send.copy(stages[p].at[2, pl.ds(2 * i, 2)], relays[p].at[i], p * 12 + 8 + i, a3, by))
        for i, by in enumerate((1, 3)):
            pick(i, by)
            send.copy(stages[p].at[i], landing(p, pos[a3]), 36 + p * 2 + i, a3, by)
        pick(3, 0)
        c = pltpu.make_async_copy(stages[p].at[3], landing(p, pos[a3]), local_sem.at[3 + p])
        c.start()
        local.append(c)
        fifth.append(got)
    for p in range(3):
        a3 = ORDERS[p][2]
        for i, by in enumerate((1, 3)):
            fifth[p][i].wait_recv()
            send.copy(relays[p].at[i], landing(p, lax.rem(pos[a3] + SIDE - by, SIDE), i), p * 12 + 10 + i, a3, by)
    for c in local[3:]:
        c.wait()
    for c in send.done:
        c.wait_send()
    waited = set(id(c) for group in (first, second, third, fourth, fifth) for cs in group for c in cs)
    for c in send.done:
        if id(c) not in waited:
            c.wait_recv()


def spread(wanted, mine):
    scratch = [pltpu.VMEM((4, 512, 128), BF16)]
    for make in (lambda r: (4, 4, 4, r, 128), lambda r: (4, 4, 4, 2, r, 128), lambda r: (2, 2, 4, 2, r, 128)):
        scratch += [pltpu.VMEM(make(rows), BF16) for _, rows in PIECES]
    scratch += [pltpu.SemaphoreType.DMA((42,)), pltpu.SemaphoreType.DMA((42,)), pltpu.SemaphoreType.DMA((2,)),
                pltpu.SemaphoreType.DMA((6,))]
    return pl.pallas_call(
        spread_kernel,
        in_specs=[pl.BlockSpec(memory_space=pltpu.SMEM), pl.BlockSpec(memory_space=pl.ANY)],
        out_specs=pl.BlockSpec(memory_space=pl.ANY),
        out_shape=jax.ShapeDtypeStruct((4, 4, 4, 2, 512, 128), BF16),
        scratch_shapes=scratch,
        compiler_params=pltpu.CompilerParams(collective_id=0, has_side_effects=True, vmem_limit_bytes=56 * 2**20),
        name="spread",
    )(wanted, mine)


def gather_back_kernel(wanted, back_ref, out_ref, rz0, rz1, rz2, rl0, rl1, rl2, s0, s1, s2, g0, g1, g2,
                       y0, y1, y2, yl0, yl1, yl2, h0, h1, h2, x0, x1, x2, xl0, xl1, xl2, total,
                       send_sem, recv_sem, swap_sem, local_sem):
    pos, core = place(), lax.axis_index("vintage")
    rz, rl, sums, gs = (rz0, rz1, rz2), (rl0, rl1, rl2), (s0, s1, s2), (g0, g1, g2)
    ys, yl, hs, xs, xl = (y0, y1, y2), (yl0, yl1, yl2), (h0, h1, h2), (x0, x1, x2), (xl0, xl1, xl2)
    dims = [tuple(sorted(o[:2])) for o in ORDERS]
    own = []
    send = Sender(pos, core, send_sem, recv_sem)

    def slots_of(p, level, half=None):
        a3 = ORDERS[p][2]
        r0, rows = PIECES[p]
        idx = []
        for d in range(3):
            if d == a3:
                idx.append(level)
            elif half is not None and d == dims[p][0]:
                idx.append(pl.ds(2 * half, 2))
            else:
                idx.append(slice(None))
        return back_ref.at[tuple(idx) + (slice(None), pl.ds(r0, rows), slice(None))]

    for p in range(3):
        c = pltpu.make_async_copy(slots_of(p, pos[ORDERS[p][2]]), rz[p].at[3], local_sem.at[p])
        c.start()
        own.append(c)
    greet(pos, core)

    def turn(axis, by):
        return lax.rem(pos[axis] + by, SIDE)

    zr, zd = [], []
    for p in range(3):
        a3 = ORDERS[p][2]
        zr.append([send.copy(slots_of(p, turn(a3, 2), i), rl[p].at[i], p * 18 + i, a3, by) for i, by in enumerate((1, 3))])
        zd.append([send.copy(slots_of(p, turn(a3, by)), rz[p].at[i], p * 18 + 2 + i, a3, by) for i, by in enumerate((1, 3))])
    zf = []
    for p in range(3):
        a3 = ORDERS[p][2]
        got = []
        for i, by in enumerate((1, 3)):
            zr[p][i].wait_recv()
            got.append(send.copy(rl[p].at[i], rz[p].at[2, pl.ds(2 * i, 2)], p * 18 + 4 + i, a3, by))
        zf.append(got)

    def collect(p, k, by, how):
        a3 = ORDERS[p][2]
        rows = PIECES[p][1]
        source = tile_of(shifted(pos, a3, by))

        def one(j, _):
            hi, lo = lax.div(j, SIDE), lax.rem(j, SIDE)
            holder = pos[a3] * STRIDE[a3] + hi * STRIDE[dims[p][0]] + lo * STRIDE[dims[p][1]]
            want = [wanted[source * 128 + s * 64 + holder] for s in range(2)]

            def chunk(q, _):
                at = pl.ds(pl.multiple_of(q * 16, 16), 16)
                vals = [rz[p][k, hi, lo, s, at, :].astype(F32) for s in range(2)]
                for b in range(4):
                    x = jnp.where(want[0] == b, vals[0], 0.0) + jnp.where(want[1] == b, vals[1], 0.0)
                    if how > 0:
                        x = x + sums[p][hi, lo, b, at, :]
                    if how < 2:
                        sums[p][hi, lo, b, at, :] = x
                    else:
                        gs[p][hi, lo, b, at, :] = x.astype(BF16)
                return 0
            lax.fori_loop(0, rows // 16, chunk, 0)
            return 0
        lax.fori_loop(0, SIDE * SIDE, one, 0)

    for p in range(3):
        own[p].wait()
        collect(p, 3, 0, 0)
    for i, by in enumerate((3, 1)):
        for p in range(3):
            zd[p][i].wait_recv()
            collect(p, i, by, 1)
    yr, yd = [], []

    def lines(ref, p, axis, index, half=None):
        idx = []
        for d in dims[p]:
            if d == axis:
                idx.append(index)
            else:
                idx.append(slice(None) if half is None else pl.ds(2 * half, 2))
        return ref.at[tuple(idx)]

    for p in range(3):
        a1, a2, a3 = ORDERS[p]
        for c in zf[p]:
            c.wait_recv()
        collect(p, 2, 2, 2)
        yr.append([send.copy(lines(gs[p], p, a2, turn(a2, 2), i), yl[p].at[i], p * 18 + 6 + i, a2, by) for i, by in enumerate((1, 3))])
        yd.append([send.copy(lines(gs[p], p, a2, turn(a2, by)), ys[p].at[i], p * 18 + 8 + i, a2, by) for i, by in enumerate((1, 3))])
    yf = []
    for p in range(3):
        a2 = ORDERS[p][1]
        got = []
        for i, by in enumerate((1, 3)):
            yr[p][i].wait_recv()
            got.append(send.copy(yl[p].at[i], ys[p].at[2, pl.ds(2 * i, 2)], p * 18 + 10 + i, a2, by))
        yf.append(got)
    xr, xd = [], []
    for p in range(3):
        a1, a2, a3 = ORDERS[p]
        rows = PIECES[p][1]
        for c in yd[p] + yf[p]:
            c.wait_recv()

        def add_row(j, _, p=p, a1=a1, a2=a2, rows=rows):
            i1, b = lax.div(j, 4), lax.rem(j, 4)
            mine = gs[p][tuple(i1 if d == a1 else pos[a2] for d in dims[p]) + (b,)].astype(F32)
            for k in range(3):
                mine = mine + ys[p][k, i1, b].astype(F32)
            hs[p][i1, b] = mine.astype(BF16)
            return 0
        lax.fori_loop(0, 16, add_row, 0)
        xr.append([send.copy(hs[p].at[turn(a1, 2), pl.ds(2 * i, 2)], xl[p].at[i], p * 18 + 12 + i, a1, by) for i, by in enumerate((1, 3))])
        xd.append([send.copy(hs[p].at[turn(a1, by)], xs[p].at[i], p * 18 + 14 + i, a1, by) for i, by in enumerate((1, 3))])
    xf = []
    for p in range(3):
        a1 = ORDERS[p][0]
        got = []
        for i, by in enumerate((1, 3)):
            xr[p][i].wait_recv()
            got.append(send.copy(xl[p].at[i], xs[p].at[2, pl.ds(2 * i, 2)], p * 18 + 16 + i, a1, by))
        xf.append(got)
    for p in range(3):
        a1 = ORDERS[p][0]
        r0, rows = PIECES[p]
        for c in xd[p] + xf[p]:
            c.wait_recv()
        for b in range(4):
            mine = hs[p][pos[a1], b].astype(F32)
            for k in range(3):
                mine = mine + xs[p][k, b].astype(F32)
            total[b, r0:r0 + rows, :] = mine.astype(BF16)
    swap = pltpu.make_async_remote_copy(
        src_ref=total, dst_ref=out_ref, send_sem=swap_sem.at[0], recv_sem=swap_sem.at[1],
        device_id=(1 - core, tile_of(pos)), device_id_type=MESH)
    swap.start()
    swap.wait()
    for c in send.done:
        c.wait_send()


def gather_back(wanted, back):
    scratch = []
    for make, kind in ((lambda r: (4, 4, 4, 2, r, 128), BF16), (lambda r: (2, 2, 4, 2, r, 128), BF16),
                       (lambda r: (4, 4, 4, r, 128), F32), (lambda r: (4, 4, 4, r, 128), BF16),
                       (lambda r: (3, 4, 4, r, 128), BF16), (lambda r: (2, 2, 4, r, 128), BF16),
                       (lambda r: (4, 4, r, 128), BF16),
                       (lambda r: (3, 4, r, 128), BF16), (lambda r: (2, 2, r, 128), BF16)):
        scratch += [pltpu.VMEM(make(rows), kind) for _, rows in PIECES]
    scratch += [pltpu.VMEM((4, 512, 128), BF16)]
    scratch += [pltpu.SemaphoreType.DMA((54,)), pltpu.SemaphoreType.DMA((54,)), pltpu.SemaphoreType.DMA((2,)),
                pltpu.SemaphoreType.DMA((3,))]
    return pl.pallas_call(
        gather_back_kernel,
        in_specs=[pl.BlockSpec(memory_space=pltpu.SMEM), pl.BlockSpec(memory_space=pl.ANY)],
        out_specs=pl.BlockSpec(memory_space=pl.ANY),
        out_shape=jax.ShapeDtypeStruct((4, 512, 128), BF16),
        scratch_shapes=scratch,
        compiler_params=pltpu.CompilerParams(collective_id=1, has_side_effects=True, vmem_limit_bytes=60 * 2**20),
        name="collect",
    )(wanted, back)


def shards(patches, out_grad, w_query, w_key, w_value, w_out, key_tiles, key_blocks):
    tokens, grads_in = patches[0], out_grad[0]
    my_tile = lax.axis_index("tile")
    tiles = lax.axis_size("tile")
    named = key_tiles[0].reshape(tiles, -1)
    blocks = key_blocks[0].reshape(tiles, -1)
    entries = named.shape[1]
    earlier = jnp.arange(entries)[None, :] < jnp.arange(entries)[:, None]
    rank = jnp.sum(((named[:, :, None] == named[:, None, :]) & earlier[None]).astype(jnp.int32), axis=2)
    place_of = rank * tiles + named
    hits = place_of[:, :, None] == jnp.arange(CAP * tiles, dtype=jnp.int32)[None, None, :]
    wanted = jnp.max(jnp.where(hits, blocks[:, :, None], -1), axis=1).reshape(-1)
    slots = lax.dynamic_slice_in_dim(named * CAP + rank, my_tile, 1, 0).reshape(-1)

    kv = jnp.dot(tokens, jnp.concatenate([w_key, w_value], axis=1), preferred_element_type=jnp.float32).astype(jnp.bfloat16)
    mine = kv.reshape(4, 128, 4, 128).transpose(0, 2, 1, 3).reshape(4, 512, 128)
    queries = jnp.dot(tokens, w_query, preferred_element_type=jnp.float32).astype(jnp.bfloat16)
    arrived = spread(wanted, mine)
    layer, query_grad, back = attention(slots, queries, grads_in, w_out, arrived.reshape(tiles * CAP, 512, 128), 2048, 2048)
    kv_grad = gather_back(wanted, back.reshape(4, 4, 4, CAP, 512, 128))
    kv_grad = kv_grad.reshape(4, 4, 128, 128).transpose(0, 2, 1, 3).reshape(512, 512)
    lhs = jnp.concatenate([query_grad, kv_grad], axis=1)
    rhs = jnp.concatenate([w_query, w_key, w_value], axis=1)
    total = lax.dot_general(lhs, rhs, (((1,), (1,)), ((), ())), preferred_element_type=jnp.float32)
    return layer[None], total.astype(jnp.bfloat16)[None]


def solution(mesh):
    cubes = P("vintage", "tile", None)
    lists = P("vintage", None, None)
    return jax.shard_map(shards, mesh=mesh, in_specs=(cubes, cubes, P(), P(), P(), P(), lists, lists),
                         out_specs=(cubes, cubes), check_vma=False)
```

```python
import functools

import jax
import jax.numpy as jnp
from jax import lax
from jax.experimental import pallas as pl
from jax.experimental.pallas import tpu as pltpu
from jax.sharding import PartitionSpec as P

CAP = 2
LOG2E = 1.4426950408889634
EPSILON = 1e-06
F32, BF16 = jnp.float32, jnp.bfloat16


def dot(a, b, ca=1, cb=0):
    return lax.dot_general(a, b, (((ca,), (cb,)), ((), ())), preferred_element_type=F32)


def attend_kernel(slots, q_ref, go_ref, wo_ref, arr_ref, lay_ref, qp_ref, dop_ref, stat_ref, inv_ref, ent_ref,
                  kv, e, acc, att, in_sem, out_sem):
    b, nb = pl.program_id(0), pl.num_programs(0)
    L = kv.shape[1]
    cur = lax.rem(b, 2)

    def fetch(blk, slot):
        return [pltpu.make_async_copy(arr_ref.at[slots[blk * L + l]], kv.at[slot, l], in_sem.at[slot, l]) for l in range(L)]

    def keep(blk, slot):
        return [pltpu.make_async_copy(kv.at[slot, :, g], ent_ref.at[g, pl.ds(blk * L, L)], out_sem.at[slot, g]) for g in range(4)]

    @pl.when(b == 0)
    def _():
        for c in fetch(0, 0):
            c.start()

    @pl.when(b >= 1)
    def _():
        for c in keep(b - 1, 1 - cur):
            c.wait()

    @pl.when(b + 1 < nb)
    def _():
        for c in fetch(b + 1, 1 - cur):
            c.start()

    @pl.when(b == 0)
    def _():
        def clear(i, _):
            inv_ref[i] = 0
            return 0
        lax.fori_loop(0, inv_ref.shape[0], clear, 0)

        def put(i, _):
            inv_ref[slots[i]] = i
            return 0
        lax.fori_loop(0, nb * L, put, 0)

    zero = jnp.zeros((128, 64), BF16)
    for h in range(12):
        x = q_ref[:, (h // 2) * 128:(h // 2) * 128 + 128][:, (h % 2) * 64:(h % 2) * 64 + 64]
        qp_ref[h // 3, (h % 3) * 128:(h % 3) * 128 + 128, :] = jnp.concatenate([x, zero], axis=1)
    for c in fetch(b, cur):
        c.wait()
    for c in keep(b, cur):
        c.start()

    for g in range(4):
        m, inv, out = attend_rows(qp_ref[g], kv[cur, :, g].reshape(L * 128, 128), e)
        stat_ref[g] = jnp.concatenate([m[:, :64], inv[:, 64:]], axis=1)
        acc[g] = out

    ss = jnp.zeros((128, 128), F32)
    for j in range(6):
        a = jnp.concatenate([acc[h // 3, (h % 3) * 128:(h % 3) * 128 + 128, :][:, 64:] for h in (2 * j, 2 * j + 1)], axis=1)
        a = a.astype(BF16).astype(F32)
        att[:, j * 128:j * 128 + 128] = a
        ss = ss + a * a
    root = jnp.sqrt(jnp.sum(ss, axis=1, keepdims=True) * (1.0 / 768) + EPSILON)
    normed = att[...] / root
    lay_ref[...] = dot(normed.astype(BF16), wo_ref[...]).astype(BF16)
    ng = dot(go_ref[...], wo_ref[...], 1, 1)
    att[...] = (ng - normed * (jnp.sum(ng * normed, axis=1, keepdims=True) * (1.0 / 768))) / root
    for h in range(12):
        x = att[:, (h // 2) * 128:(h // 2) * 128 + 128][:, (h % 2) * 64:(h % 2) * 64 + 64].astype(BF16)
        dop_ref[h // 3, (h % 3) * 128:(h % 3) * 128 + 128, :] = jnp.concatenate([zero, x], axis=1)

    @pl.when(b == nb - 1)
    def _():
        for c in keep(b, cur):
            c.wait()


SCALE = 0.125 * LOG2E


def attend_rows(q, kv, e):
    rows, n = q.shape[0], kv.shape[0] // 128
    s = dot(q, kv, 1, 1)
    m = s[:, :128]
    for i in range(1, n):
        m = jnp.maximum(m, s[:, i * 128:i * 128 + 128])
    m = jnp.broadcast_to(jnp.max(m, axis=1, keepdims=True), (rows, 128))
    total = jnp.zeros((rows, 128), F32)
    for i in range(n):
        x = jnp.exp2((s[:, i * 128:i * 128 + 128] - m) * SCALE)
        e[:, i * 128:i * 128 + 128] = x
        total = total + x
    inv = jnp.broadcast_to(1.0 / jnp.sum(total, axis=1, keepdims=True), (rows, 128))
    low = jnp.concatenate([(e[:, i * 128:i * 128 + 128] * inv).astype(BF16) for i in range(n)], axis=1)
    return m, inv, dot(low, kv)


def attention(slots, queries, grads, w_out, arr):
    rows, D = queries.shape
    nb = rows // 128
    L = slots.shape[0] // nb
    ns = arr.shape[0]
    row = lambda b, s: (b, 0)
    padded = lambda b, s: (b, 0, 0, 0)
    return pl.pallas_call(
        attend_kernel,
        grid_spec=pltpu.PrefetchScalarGridSpec(
            num_scalar_prefetch=1, grid=(nb,),
            in_specs=[pl.BlockSpec((128, D), row), pl.BlockSpec((128, D), row),
                      pl.BlockSpec((D, D), lambda b, s: (0, 0), pipeline_mode=pl.Buffered(1)),
                      pl.BlockSpec(memory_space=pl.ANY)],
            out_specs=[pl.BlockSpec((128, D), row)] + [pl.BlockSpec((None, 4, 384, 128), padded)] * 3
                      + [pl.BlockSpec(memory_space=pltpu.SMEM), pl.BlockSpec(memory_space=pl.ANY)],
            scratch_shapes=[
                pltpu.VMEM((2, L, 4, 128, 128), BF16), pltpu.VMEM((384, 2048), F32),
                pltpu.VMEM((4, 384, 128), F32), pltpu.VMEM((128, 768), F32),
                pltpu.SemaphoreType.DMA((2, L)), pltpu.SemaphoreType.DMA((2, 4))]),
        out_shape=[jax.ShapeDtypeStruct((rows, D), BF16), jax.ShapeDtypeStruct((nb, 4, 384, 128), BF16),
                   jax.ShapeDtypeStruct((nb, 4, 384, 128), BF16), jax.ShapeDtypeStruct((nb, 4, 384, 128), F32),
                   jax.ShapeDtypeStruct((ns,), jnp.int32), jax.ShapeDtypeStruct((4, nb * L, 128, 128), BF16)],
        compiler_params=pltpu.CompilerParams(dimension_semantics=("arbitrary",), vmem_limit_bytes=60 * 2**20),
        name="attend",
    )(slots, queries, grads, w_out, arr.reshape(ns, 4, 128, 128))


MESH = pl.DeviceIdType.MESH
SIDE = 4
ORDERS = ((0, 1, 2), (1, 2, 0), (2, 0, 1))
PIECES = ((0, 176), (176, 176), (352, 160))
STRIDE = (16, 4, 1)


def place():
    tile = lax.axis_index("tile")
    return [lax.rem(lax.div(tile, s), SIDE) for s in STRIDE]


def shifted(pos, axis, by):
    moved = list(pos)
    moved[axis] = lax.rem(pos[axis] + by, SIDE)
    return moved


def tile_of(pos):
    return pos[0] * 16 + pos[1] * 4 + pos[2]


def greet(pos, core, wait=True):
    barrier = pltpu.get_barrier_semaphore()
    for axis in range(3):
        for by in (1, 3):
            pl.semaphore_signal(barrier, inc=1, device_id=(core, tile_of(shifted(pos, axis, by))), device_id_type=MESH)
    pl.semaphore_signal(barrier, inc=1, device_id=(1 - core, tile_of(pos)), device_id_type=MESH)
    if wait:
        greet_wait()


def greet_wait():
    pl.semaphore_wait(pltpu.get_barrier_semaphore(), 7)


class Sender:
    def __init__(self, pos, core, send_sem, recv_sem):
        self.pos, self.core, self.send_sem, self.recv_sem = pos, core, send_sem, recv_sem
        self.done = []

    def copy(self, src, dst, sem, axis, by):
        c = pltpu.make_async_remote_copy(
            src_ref=src, dst_ref=dst, send_sem=self.send_sem.at[sem], recv_sem=self.recv_sem.at[sem],
            device_id=(self.core, tile_of(shifted(self.pos, axis, by))), device_id_type=MESH)
        c.start()
        self.done.append(c)
        return c


def at_axis(ref, dims, index, axis, *rest):
    return ref.at[tuple(index if d == axis else slice(None) for d in dims) + rest]


def spread_kernel(wanted, mine_ref, out_ref, own, plane0, plane1, plane2, st0, st1, st2, rl0, rl1, rl2,
                  send_sem, recv_sem, swap_sem, local_sem):
    pos, core = place(), lax.axis_index("vintage")
    planes, stages, relays = (plane0, plane1, plane2), (st0, st1, st2), (rl0, rl1, rl2)
    greet(pos, core)
    swap = pltpu.make_async_remote_copy(
        src_ref=mine_ref, dst_ref=own, send_sem=swap_sem.at[0], recv_sem=swap_sem.at[1],
        device_id=(1 - core, tile_of(pos)), device_id_type=MESH)
    swap.start()
    swap.wait()
    send = Sender(pos, core, send_sem, recv_sem)
    dims = [tuple(sorted(o[:2])) for o in ORDERS]
    local = []

    def line(p, axis):
        return at_axis(planes[p], dims[p], pos[axis], axis)

    def cell(p, a1, i1, a2, i2, *rest):
        return planes[p].at[tuple(i1 if d == a1 else i2 for d in dims[p]) + rest]

    for p, (r0, rows) in enumerate(PIECES):
        a1, a2, a3 = ORDERS[p]
        c = pltpu.make_async_copy(own.at[:, pl.ds(r0, rows), :], cell(p, a1, pos[a1], a2, pos[a2]), local_sem.at[p])
        c.start()
        local.append(c)
    first = []
    for p in range(3):
        a1, a2, a3 = ORDERS[p]
        local[p].wait()
        here = cell(p, a1, pos[a1], a2, pos[a2])
        first.append([send.copy(here, here, p * 12 + i, a1, by) for i, by in enumerate((1, 3))])
    second = []
    for p in range(3):
        a1, a2, a3 = ORDERS[p]
        got = []
        for i, by in enumerate((1, 3)):
            first[p][i].wait_recv()
            part = cell(p, a1, lax.rem(pos[a1] + SIDE - by, SIDE), a2, pos[a2], pl.ds(2 * i, 2))
            got.append(send.copy(part, part, p * 12 + 2 + i, a1, by))
        second.append(got)
    third = []
    for p in range(3):
        a1, a2, a3 = ORDERS[p]
        for c in second[p]:
            c.wait_recv()
        here = line(p, a2)
        third.append([send.copy(here, here, p * 12 + 4 + i, a2, by) for i, by in enumerate((1, 3))])
    fourth = []
    for p in range(3):
        a1, a2, a3 = ORDERS[p]
        got = []
        for i, by in enumerate((1, 3)):
            third[p][i].wait_recv()
            other = lax.rem(pos[a2] + SIDE - by, SIDE)
            part = planes[p].at[tuple(other if d == a2 else pl.ds(2 * i, 2) for d in dims[p])]
            got.append(send.copy(part, part, p * 12 + 6 + i, a2, by))
        fourth.append(got)

    def landing(p, source, half=None):
        a3 = ORDERS[p][2]
        r0, rows = PIECES[p]
        idx = []
        for d in range(3):
            if d == a3:
                idx.append(source)
            elif half is not None and d == dims[p][0]:
                idx.append(pl.ds(2 * half, 2))
            else:
                idx.append(slice(None))
        return out_ref.at[tuple(idx) + (slice(None), pl.ds(r0, rows), slice(None))]

    fifth = []
    for p in range(3):
        a1, a2, a3 = ORDERS[p]
        r0, rows = PIECES[p]
        for c in fourth[p]:
            c.wait_recv()

        def pick(k, by, p=p, a3=a3):
            dest = tile_of(shifted(pos, a3, by))

            def one(j, _):
                hi, lo = lax.div(j, SIDE), lax.rem(j, SIDE)
                source = pos[a3] * STRIDE[a3] + hi * STRIDE[dims[p][0]] + lo * STRIDE[dims[p][1]]
                for s in range(2):
                    blk = jnp.maximum(wanted[dest * 128 + s * 64 + source], 0)
                    stages[p][k, hi, lo, s] = planes[p][hi, lo, blk]
                return 0
            lax.fori_loop(0, SIDE * SIDE, one, 0)

        got = []
        pick(2, 2)
        for i, by in enumerate((1, 3)):
            got.append(send.copy(stages[p].at[2, pl.ds(2 * i, 2)], relays[p].at[i], p * 12 + 8 + i, a3, by))
        for i, by in enumerate((1, 3)):
            pick(i, by)
            send.copy(stages[p].at[i], landing(p, pos[a3]), 36 + p * 2 + i, a3, by)
        pick(3, 0)
        c = pltpu.make_async_copy(stages[p].at[3], landing(p, pos[a3]), local_sem.at[3 + p])
        c.start()
        local.append(c)
        fifth.append(got)
    for p in range(3):
        a3 = ORDERS[p][2]
        for i, by in enumerate((1, 3)):
            fifth[p][i].wait_recv()
            send.copy(relays[p].at[i], landing(p, lax.rem(pos[a3] + SIDE - by, SIDE), i), p * 12 + 10 + i, a3, by)
    for c in local[3:]:
        c.wait()
    for c in send.done:
        c.wait_send()
    waited = set(id(c) for group in (first, second, third, fourth, fifth) for cs in group for c in cs)
    for c in send.done:
        if id(c) not in waited:
            c.wait_recv()


def spread(wanted, mine):
    scratch = [pltpu.VMEM((4, 512, 128), BF16)]
    for make in (lambda r: (4, 4, 4, r, 128), lambda r: (4, 4, 4, 2, r, 128), lambda r: (2, 2, 4, 2, r, 128)):
        scratch += [pltpu.VMEM(make(rows), BF16) for _, rows in PIECES]
    scratch += [pltpu.SemaphoreType.DMA((42,)), pltpu.SemaphoreType.DMA((42,)), pltpu.SemaphoreType.DMA((2,)),
                pltpu.SemaphoreType.DMA((6,))]
    return pl.pallas_call(
        spread_kernel,
        in_specs=[pl.BlockSpec(memory_space=pltpu.SMEM), pl.BlockSpec(memory_space=pl.ANY)],
        out_specs=pl.BlockSpec(memory_space=pl.ANY),
        out_shape=jax.ShapeDtypeStruct((4, 4, 4, 2, 512, 128), BF16),
        scratch_shapes=scratch,
        compiler_params=pltpu.CompilerParams(collective_id=0, has_side_effects=True, vmem_limit_bytes=56 * 2**20),
        name="spread",
    )(wanted, mine)


CUTS = ((48, 48, 32), (48, 32, 48), (32, 48, 48), (48, 48, 32))


def spans(g):
    start = 0
    out = []
    for rows in CUTS[g]:
        out.append((start, rows))
        start += rows
    return out


def return_kernel(wanted, inv, qp_ref, dop_ref, stat_ref, ent_ref, dq_ref, out_ref, rl_ref, yl_ref, xl_ref,
                  kvb, p, t, dqs, parts, stage, rz, sums, gs, ys, hs, xs, total,
                  send_sem, recv_sem, swap_sem, kv_sem):
    pos, core = place(), lax.axis_index("vintage")
    dims = [tuple(sorted(o[:2])) for o in ORDERS]
    send = Sender(pos, core, send_sem, recv_sem)
    nb = qp_ref.shape[0]
    L = kvb.shape[1]
    greet(pos, core, False)

    def turn(axis, by):
        return lax.rem(pos[axis] + by, SIDE)

    def key(g, p, i):
        return (g * 3 + p) * 18 + i

    def load(g, b, slot):
        return pltpu.make_async_copy(ent_ref.at[g, pl.ds(b * L, L)], kvb.at[slot], kv_sem.at[slot])

    load(0, 0, 0).start()

    def backward(g):
        def one(b, _):
            cur = lax.rem(b, 2)
            load(g, b, cur).wait()

            @pl.when(b + 1 < nb)
            def _():
                load(g, b + 1, 1 - cur).start()

            if g < 3:
                @pl.when(b + 1 == nb)
                def _():
                    load(g + 1, 0, 0).start()

            kv = kvb[cur].reshape(L * 128, 128)
            q, do = qp_ref[b, g], dop_ref[b, g]
            m = jnp.broadcast_to(stat_ref[b, g, :, 0:1], (384, 128))
            nrm = jnp.broadcast_to(stat_ref[b, g, :, 64:65], (384, 128))
            s = dot(q, kv, 1, 1)
            dp = dot((do.astype(F32) * 0.125).astype(BF16), kv, 1, 1)
            rd = jnp.zeros((384, 128), F32)
            for i in range(L):
                cols = slice(i * 128, i * 128 + 128)
                pr = jnp.exp2((s[:, cols] - m) * SCALE) * nrm
                x = pr * dp[:, cols]
                p[:, cols] = pr
                t[:, cols] = x
                rd = rd + x
            rd = jnp.broadcast_to(jnp.sum(rd, axis=1, keepdims=True), (384, 128))
            ds_, low = [], []
            for i in range(L):
                cols = slice(i * 128, i * 128 + 128)
                pr = p[:, cols]
                ds_.append((t[:, cols] - pr * rd).astype(BF16))
                low.append(pr.astype(BF16))
            ds_, low = jnp.concatenate(ds_, axis=1), jnp.concatenate(low, axis=1)
            dqs[b, g] = dot(ds_, kv).astype(BF16)
            part = dot(jnp.concatenate([ds_, low], axis=0), jnp.concatenate([q, do], axis=0), 0, 0)
            parts[pl.ds(b * L, L)] = part.astype(BF16).reshape(L, 128, 128)
            return 0
        lax.fori_loop(0, nb, one, 0)

    zr, zd, zf, yr, yd, yf, xr, xd, xf = [{} for _ in range(9)]

    def slots_of(g, p, level, half=None):
        a3 = ORDERS[p][2]
        r0, rows = spans(g)[p]
        idx = []
        for d in range(3):
            if d == a3:
                idx.append(level)
            elif half is not None and d == dims[p][0]:
                idx.append(pl.ds(2 * half, 2))
            else:
                idx.append(slice(None))
        return stage.at[(g % 2,) + tuple(idx) + (slice(None), pl.ds(r0, rows), slice(None))]

    def at_rows(ref, g, p, lead):
        r0, rows = spans(g)[p]
        return ref.at[(g,) + tuple(lead) + (pl.ds(r0, rows), slice(None))]

    W = slice(None)

    def z_send(g):
        if g >= 2:
            for c in zr[g - 2] + zd[g - 2]:
                c.wait_send()

        def place_part(j, _):
            x, y, z = lax.div(j, 16), lax.rem(lax.div(j, 4), 4), lax.rem(j, 4)
            for s in range(2):
                stage[g % 2, x, y, z, s] = parts[inv[j * 2 + s]]
            return 0
        lax.fori_loop(0, 64, place_part, 0)
        if g == 0:
            greet_wait()
        zr[g], zd[g] = [], []
        for p in range(3):
            a3 = ORDERS[p][2]
            for i, by in enumerate((1, 3)):
                zr[g].append(send.copy(slots_of(g, p, turn(a3, 2), i), at_rows(rl_ref, g, p, (i, W, W, W)), key(g, p, i), a3, by))
        for p in range(3):
            a3 = ORDERS[p][2]
            for i, by in enumerate((1, 3)):
                zd[g].append(send.copy(slots_of(g, p, turn(a3, by)), at_rows(rz, g, p, (i, W, W, W)), key(g, p, 2 + i), a3, by))

    def z_relay(g):
        zf[g] = []
        for p in range(3):
            a3 = ORDERS[p][2]
            for i, by in enumerate((1, 3)):
                zr[g][p * 2 + i].wait_recv()
                zf[g].append(send.copy(at_rows(rl_ref, g, p, (i, W, W, W)), at_rows(rz, g, p, (2, pl.ds(2 * i, 2), W, W)),
                                       key(g, p, 4 + i), a3, by))

    def add_up(g, p, k, by, first, last):
        a3 = ORDERS[p][2]
        r0, rows = spans(g)[p]
        source = tile_of(shifted(pos, a3, by))

        def one(j, _):
            hi, lo = lax.div(j, SIDE), lax.rem(j, SIDE)
            holder = pos[a3] * STRIDE[a3] + hi * STRIDE[dims[p][0]] + lo * STRIDE[dims[p][1]]
            where = [None] * 3
            where[a3], where[dims[p][0]], where[dims[p][1]] = pos[a3], hi, lo
            vals = []
            for s in range(2):
                at = (k, hi, lo, s) if k < 3 else tuple(where) + (s,)
                ref, lead = (rz, g) if k < 3 else (stage, g % 2)
                vals.append(ref[(lead,) + at + (pl.ds(r0, rows), slice(None))].astype(F32))
            want = [wanted[source * 128 + s * 64 + holder] for s in range(2)]
            for b in range(4):
                x = jnp.where(want[0] == b, vals[0], 0.0) + jnp.where(want[1] == b, vals[1], 0.0)
                if not first:
                    x = x + sums[hi, lo, b, pl.ds(r0, rows), :]
                if last:
                    gs[g, hi, lo, b, pl.ds(r0, rows), :] = x.astype(BF16)
                else:
                    sums[hi, lo, b, pl.ds(r0, rows), :] = x
            return 0
        lax.fori_loop(0, SIDE * SIDE, one, 0)

    def z_sum(g):
        for p in range(3):
            add_up(g, p, 3, 0, True, False)
        for i, by in enumerate((3, 1)):
            for p in range(3):
                zd[g][p * 2 + i].wait_recv()
                add_up(g, p, i, by, False, False)

    def lines(g, p, axis, index, half=None):
        idx = []
        for d in dims[p]:
            if d == axis:
                idx.append(index)
            else:
                idx.append(slice(None) if half is None else pl.ds(2 * half, 2))
        return at_rows(gs, g, p, tuple(idx) + (W,))

    def y_send(g):
        yr[g], yd[g] = [], []
        for p in range(3):
            a2 = ORDERS[p][1]
            for c in zf[g][p * 2:p * 2 + 2]:
                c.wait_recv()
            add_up(g, p, 2, 2, False, True)
        for p in range(3):
            a2 = ORDERS[p][1]
            for i, by in enumerate((1, 3)):
                yr[g].append(send.copy(lines(g, p, a2, turn(a2, 2), i), at_rows(yl_ref, g, p, (i, W, W)), key(g, p, 6 + i), a2, by))
        for p in range(3):
            a2 = ORDERS[p][1]
            for i, by in enumerate((1, 3)):
                yd[g].append(send.copy(lines(g, p, a2, turn(a2, by)), at_rows(ys, g, p, (i, W, W)), key(g, p, 8 + i), a2, by))

    def y_relay(g):
        yf[g] = []
        for p in range(3):
            a2 = ORDERS[p][1]
            for i, by in enumerate((1, 3)):
                yr[g][p * 2 + i].wait_recv()
                yf[g].append(send.copy(at_rows(yl_ref, g, p, (i, W, W)), at_rows(ys, g, p, (2, pl.ds(2 * i, 2), W)),
                                       key(g, p, 10 + i), a2, by))

    def x_send(g):
        xr[g], xd[g] = [], []
        for p in range(3):
            a1, a2, a3 = ORDERS[p]
            r0, rows = spans(g)[p]
            at = (pl.ds(r0, rows), slice(None))
            for c in yd[g][p * 2:p * 2 + 2] + yf[g][p * 2:p * 2 + 2]:
                c.wait_recv()

            def row(j, _, p=p, a1=a1, a2=a2, at=at):
                i1, b = lax.div(j, 4), lax.rem(j, 4)
                mine = gs[(g,) + tuple(i1 if d == a1 else pos[a2] for d in dims[p]) + (b,) + at].astype(F32)
                for k in range(3):
                    mine = mine + ys[(g, k, i1, b) + at].astype(F32)
                hs[(g, i1, b) + at] = mine.astype(BF16)
                return 0
            lax.fori_loop(0, 16, row, 0)
        for p in range(3):
            a1 = ORDERS[p][0]
            for i, by in enumerate((1, 3)):
                xr[g].append(send.copy(at_rows(hs, g, p, (turn(a1, 2), pl.ds(2 * i, 2))), at_rows(xl_ref, g, p, (i, W)), key(g, p, 12 + i), a1, by))
        for p in range(3):
            a1 = ORDERS[p][0]
            for i, by in enumerate((1, 3)):
                xd[g].append(send.copy(at_rows(hs, g, p, (turn(a1, by), W)), at_rows(xs, g, p, (i, W)), key(g, p, 14 + i), a1, by))

    def x_relay(g):
        xf[g] = []
        for p in range(3):
            a1 = ORDERS[p][0]
            for i, by in enumerate((1, 3)):
                xr[g][p * 2 + i].wait_recv()
                xf[g].append(send.copy(at_rows(xl_ref, g, p, (i, W)), at_rows(xs, g, p, (2, pl.ds(2 * i, 2))),
                                       key(g, p, 16 + i), a1, by))

    swaps = []

    def finish(g):
        for p in range(3):
            a1 = ORDERS[p][0]
            r0, rows = spans(g)[p]
            at = (pl.ds(r0, rows), slice(None))
            for c in xd[g][p * 2:p * 2 + 2] + xf[g][p * 2:p * 2 + 2]:
                c.wait_recv()
            for b in range(4):
                mine = hs[(g, pos[a1], b) + at].astype(F32)
                for k in range(3):
                    mine = mine + xs[(g, k, b) + at].astype(F32)
                total[(g, b) + at] = mine.astype(BF16)
        c = pltpu.make_async_remote_copy(
            src_ref=total.at[g], dst_ref=out_ref.at[g], send_sem=swap_sem.at[0, g], recv_sem=swap_sem.at[1, g],
            device_id=(1 - core, tile_of(pos)), device_id_type=MESH)
        c.start()
        swaps.append(c)

    def queries_out(b):
        for j in range(6):
            dq_ref[b * 128:b * 128 + 128, j * 128:j * 128 + 128] = jnp.concatenate(
                [dqs[b, h // 3, (h % 3) * 128:(h % 3) * 128 + 128, :][:, :64] for h in (2 * j, 2 * j + 1)], axis=1)

    backward(0)
    z_send(0)
    backward(1)
    z_send(1)
    z_relay(0)
    z_sum(0)
    backward(2)
    z_send(2)
    z_relay(1)
    y_send(0)
    z_sum(1)
    backward(3)
    z_send(3)
    z_relay(2)
    y_send(1)
    y_relay(0)
    z_sum(2)
    z_relay(3)
    y_send(2)
    y_relay(1)
    x_send(0)
    z_sum(3)
    y_send(3)
    y_relay(2)
    x_send(1)
    x_relay(0)
    for b in range(4):
        queries_out(b)
    y_relay(3)
    x_send(2)
    x_relay(1)
    finish(0)
    x_send(3)
    x_relay(2)
    finish(1)
    x_relay(3)
    finish(2)
    finish(3)
    for c in swaps:
        c.wait()
    for g in range(4):
        late = zr[g] + zd[g] if g >= 2 else []
        for c in late + zf[g] + yr[g] + yd[g] + yf[g] + xr[g] + xd[g] + xf[g]:
            c.wait_send()


def gather_back(wanted, inv, qp, dop, stat, ent):
    V, A = pl.BlockSpec(memory_space=pltpu.VMEM), pl.BlockSpec(memory_space=pl.ANY)
    S = pl.BlockSpec(memory_space=pltpu.SMEM)
    bf = lambda *shape: jax.ShapeDtypeStruct(shape, BF16)
    vm = lambda *shape: pltpu.VMEM(shape, BF16)
    out = pl.pallas_call(
        return_kernel,
        in_specs=[S, S, V, V, V, A],
        out_specs=[V, A, A, A, A],
        out_shape=[bf(512, 768), bf(4, 4, 128, 128), bf(4, 2, 2, 4, 2, 128, 128), bf(4, 2, 2, 4, 128, 128), bf(4, 2, 2, 128, 128)],
        scratch_shapes=[
            vm(2, 16, 128, 128), pltpu.VMEM((384, 2048), F32), pltpu.VMEM((384, 2048), F32), vm(4, 4, 384, 128),
            vm(64, 128, 128), vm(2, 4, 4, 4, 2, 128, 128), vm(4, 3, 4, 4, 2, 128, 128),
            pltpu.VMEM((4, 4, 4, 128, 128), F32), vm(4, 4, 4, 4, 128, 128), vm(4, 3, 4, 4, 128, 128),
            vm(4, 4, 4, 128, 128), vm(4, 3, 4, 128, 128), vm(4, 4, 128, 128),
            pltpu.SemaphoreType.DMA((216,)), pltpu.SemaphoreType.DMA((216,)), pltpu.SemaphoreType.DMA((2, 4)),
            pltpu.SemaphoreType.DMA((2,))],
        compiler_params=pltpu.CompilerParams(collective_id=1, has_side_effects=True, vmem_limit_bytes=67043328),
        name="collect",
    )(wanted, inv, qp, dop, stat, ent)
    return out[0], out[1]


def shards(patches, out_grad, w_query, w_key, w_value, w_out, key_tiles, key_blocks):
    tokens, grads_in = patches[0], out_grad[0]
    my_tile = lax.axis_index("tile")
    tiles = lax.axis_size("tile")
    named = key_tiles[0].reshape(tiles, -1)
    blocks = key_blocks[0].reshape(tiles, -1)
    entries = named.shape[1]
    earlier = jnp.arange(entries)[None, :] < jnp.arange(entries)[:, None]
    rank = jnp.sum(((named[:, :, None] == named[:, None, :]) & earlier[None]).astype(jnp.int32), axis=2)
    place_of = rank * tiles + named
    hits = place_of[:, :, None] == jnp.arange(CAP * tiles, dtype=jnp.int32)[None, None, :]
    wanted = jnp.max(jnp.where(hits, blocks[:, :, None], -1), axis=1).reshape(-1)
    slots = lax.dynamic_slice_in_dim(named * CAP + rank, my_tile, 1, 0).reshape(-1)

    w_kv = jnp.concatenate([w_key.reshape(-1, 4, 64), w_value.reshape(-1, 4, 64)], axis=2).reshape(-1, 512)
    kv = jnp.dot(tokens, w_kv, preferred_element_type=jnp.float32).astype(jnp.bfloat16)
    mine = kv.reshape(4, 128, 4, 128).transpose(0, 2, 1, 3).reshape(4, 512, 128)
    queries = jnp.dot(tokens, w_query, preferred_element_type=jnp.float32).astype(jnp.bfloat16)
    arrived = spread(wanted, mine)
    layer, qp, dop, stat, inv, ent = attention(slots, queries, grads_in, w_out, arrived.reshape(tiles * CAP, 512, 128))
    query_grad, kv_grad = gather_back(wanted, inv, qp, dop, stat, ent)
    kv_grad = kv_grad.transpose(1, 2, 0, 3).reshape(512, 512)
    lhs = jnp.concatenate([query_grad, kv_grad], axis=1)
    rhs = jnp.concatenate([w_query, w_kv], axis=1)
    total = lax.dot_general(lhs, rhs, (((1,), (1,)), ((), ())), preferred_element_type=jnp.float32)
    return layer[None], total.astype(jnp.bfloat16)[None]


def solution(mesh):
    cubes = P("vintage", "tile", None)
    lists = P("vintage", None, None)
    return jax.shard_map(shards, mesh=mesh, in_specs=(cubes, cubes, P(), P(), P(), P(), lists, lists),
                         out_specs=(cubes, cubes), check_vma=False)
```

```python
import jax
import jax.numpy as jnp
from jax import lax
from jax.experimental import pallas as pl
from jax.experimental.pallas import tpu as pltpu
from jax.sharding import PartitionSpec as P

LOG2E = 1.4426950408889634
EPSILON = 1e-06
F32, BF16 = jnp.float32, jnp.bfloat16


def dot(a, b, ca=1, cb=0):
    return lax.dot_general(a, b, (((ca,), (cb,)), ((), ())), preferred_element_type=F32)


SCALE = 0.125 * LOG2E


def attend_rows(q, kv, e):
    rows, n = q.shape[0], kv.shape[0] // 128
    s = dot(q, kv, 1, 1)
    m = s[:, :128]
    for i in range(1, n):
        m = jnp.maximum(m, s[:, i * 128:i * 128 + 128])
    m = jnp.broadcast_to(jnp.max(m, axis=1, keepdims=True), (rows, 128))
    total = jnp.zeros((rows, 128), F32)
    for i in range(n):
        x = jnp.exp2((s[:, i * 128:i * 128 + 128] - m) * SCALE)
        e[:, i * 128:i * 128 + 128] = x
        total = total + x
    inv = jnp.broadcast_to(1.0 / jnp.sum(total, axis=1, keepdims=True), (rows, 128))
    low = jnp.concatenate([(e[:, i * 128:i * 128 + 128] * inv).astype(BF16) for i in range(n)], axis=1)
    return m, inv, dot(low, kv)


MESH = pl.DeviceIdType.MESH
SIDE = 4
ORDERS = ((0, 1, 2), (1, 2, 0), (2, 0, 1))
STRIDE = (16, 4, 1)


def place():
    tile = lax.axis_index("tile")
    return [lax.rem(lax.div(tile, s), SIDE) for s in STRIDE]


def shifted(pos, axis, by):
    moved = list(pos)
    moved[axis] = lax.rem(pos[axis] + by, SIDE)
    return moved


def tile_of(pos):
    return pos[0] * 16 + pos[1] * 4 + pos[2]


def greet(pos, core, wait=True):
    barrier = pltpu.get_barrier_semaphore()
    for axis in range(3):
        for by in (1, 3):
            pl.semaphore_signal(barrier, inc=1, device_id=(core, tile_of(shifted(pos, axis, by))), device_id_type=MESH)
    pl.semaphore_signal(barrier, inc=1, device_id=(1 - core, tile_of(pos)), device_id_type=MESH)
    if wait:
        greet_wait()


def greet_wait():
    pl.semaphore_wait(pltpu.get_barrier_semaphore(), 7)


class Sender:
    def __init__(self, pos, core, send_sem, recv_sem):
        self.pos, self.core, self.send_sem, self.recv_sem = pos, core, send_sem, recv_sem
        self.done = []

    def copy(self, src, dst, sem, axis, by):
        c = pltpu.make_async_remote_copy(
            src_ref=src, dst_ref=dst, send_sem=self.send_sem.at[sem], recv_sem=self.recv_sem.at[sem],
            device_id=(self.core, tile_of(shifted(self.pos, axis, by))), device_id_type=MESH)
        c.start()
        self.done.append(c)
        return c


def at_axis(ref, dims, index, axis, *rest):
    return ref.at[tuple(index if d == axis else slice(None) for d in dims) + rest]


CUTS = ((48, 48, 32), (48, 32, 48), (32, 48, 48), (48, 48, 32))


def spans(g):
    start = 0
    out = []
    for rows in CUTS[g]:
        out.append((start, rows))
        start += rows
    return out


def offset(g, p):
    return sum(CUTS[i][p] for i in range(g))


def forward_kernel(tok_ref, go_ref, wq_ref, wk_ref, wv_ref, wo_ref, kt_ref, kb_ref,
                   lay_ref, qp_ref, dop_ref, stat_ref, ent_ref, want_ref, inv_ref, rl_ref,
                   mine, own, plane0, plane1, plane2, stage, arr0, arr1, arr2, arr3, e, kvb, qv, dov, stv, att, ng, lay,
                   named, ranks, wtab, itab, stab, want, slot,
                   send_sem, recv_sem, swap_sem, local_sem, tab_sem, ent_sem, out_sem):
    pos, core = place(), lax.axis_index("vintage")
    me = tile_of(pos)
    planes, arr = (plane0, plane1, plane2), (arr0, arr1, arr2, arr3)
    dims = [tuple(sorted(o[:2])) for o in ORDERS]
    send = Sender(pos, core, send_sem, recv_sem)
    nb, L = 4, 16
    greet(pos, core, False)

    k = dot(tok_ref[...], wk_ref[...]).astype(BF16)
    v = dot(tok_ref[...], wv_ref[...]).astype(BF16)
    for g in range(4):
        both = jnp.concatenate([k[:, g * 64:g * 64 + 64], v[:, g * 64:g * 64 + 64]], axis=1)
        for b in range(nb):
            mine[b, g * 128:g * 128 + 128, :] = both[b * 128:b * 128 + 128]

    lane = lax.broadcasted_iota(jnp.int32, (256, 128), 1)
    tile = jnp.where(lane < 64, lane, lane - 64)
    row = lax.broadcasted_iota(jnp.int32, (256, 128), 0)
    quarter = row - (row // 4) * 4
    block, entry = jnp.zeros((256, 128), jnp.int32), jnp.zeros((256, 128), jnp.int32)
    for l in range(L):
        hit = kt_ref[:, l:l + 1] == tile
        block = jnp.where(hit, kb_ref[:, l:l + 1] + 1, block)
        entry = jnp.where(hit, quarter * L + l + 1, entry)
    lane4 = lax.broadcasted_iota(jnp.int32, (64, 128), 1)
    for source, table in ((block, wtab), (entry, itab)):
        named[...] = source
        one, two = jnp.zeros((64, 128), jnp.int32), jnp.zeros((64, 128), jnp.int32)
        for i in range(4):
            x = named[pl.ds(i, 64, stride=4), :]
            ranks[pl.ds(i, 64, stride=4), :] = jnp.where(one > 0, 1, 0)
            two = jnp.where((one > 0) & (x > 0), x, two)
            one = jnp.where(one > 0, one, x)
        table[...] = jnp.where(lane4 < 64, one, two) - 1
    itab[...] = jnp.maximum(itab[...], 0)
    half = pl.ds(pl.multiple_of(lax.div(me, 2) * 8, 8), 8)
    mine_kt, mine_rank = kt_ref[half, :], ranks[half, :]
    lane8 = lax.broadcasted_iota(jnp.int32, (8, 128), 1)
    found = jnp.zeros((8, 128), jnp.int32)
    for l in range(L):
        at = jnp.sum(jnp.where((mine_kt[:, l:l + 1] == lane8) & (lane8 < 64), lane8 * 2 + mine_rank, 0), axis=1, keepdims=True)
        found = jnp.where(lane8 == l, at, found)
    stab[...] = found
    tables = [pltpu.make_async_copy(wtab, want, tab_sem.at[0]), pltpu.make_async_copy(stab, slot, tab_sem.at[1]),
              pltpu.make_async_copy(wtab, want_ref, tab_sem.at[2]), pltpu.make_async_copy(itab, inv_ref, tab_sem.at[3])]
    for c in tables:
        c.start()

    greet_wait()
    swap = pltpu.make_async_remote_copy(
        src_ref=mine, dst_ref=own, send_sem=swap_sem.at[0], recv_sem=swap_sem.at[1],
        device_id=(1 - core, me), device_id_type=MESH)
    swap.start()

    zero = jnp.zeros((128, 64), BF16)
    q = dot(tok_ref[...], wq_ref[...]).astype(BF16)
    for b in range(nb):
        for h in range(12):
            x = q[b * 128:b * 128 + 128, (h // 2) * 128:(h // 2) * 128 + 128][:, (h % 2) * 64:(h % 2) * 64 + 64]
            qv[b, h // 3, (h % 3) * 128:(h % 3) * 128 + 128, :] = jnp.concatenate([x, zero], axis=1)
    outs = [pltpu.make_async_copy(qv, qp_ref, out_sem.at[0])]
    outs[0].start()
    swap.wait()

    def cell(p, a1, i1, a2, i2, *rest):
        return planes[p].at[tuple(i1 if d == a1 else i2 for d in dims[p]) + rest]

    local = []
    for p in range(3):
        a1, a2, a3 = ORDERS[p]
        for g in range(4):
            r0, rows = spans(g)[p]
            c = pltpu.make_async_copy(own.at[:, pl.ds(g * 128 + r0, rows), :],
                                      cell(p, a1, pos[a1], a2, pos[a2], slice(None), pl.ds(offset(g, p), rows), slice(None)),
                                      local_sem.at[p * 4 + g])
            c.start()
            local.append(c)
    first, second, third, fourth = [], [], [], []
    for p in range(3):
        a1, a2, a3 = ORDERS[p]
        for c in local[p * 4:p * 4 + 4]:
            c.wait()
        here = cell(p, a1, pos[a1], a2, pos[a2])
        first.append([send.copy(here, here, p * 8 + i, a1, by) for i, by in enumerate((1, 3))])
    for p in range(3):
        a1, a2, a3 = ORDERS[p]
        got = []
        for i, by in enumerate((1, 3)):
            first[p][i].wait_recv()
            part = cell(p, a1, lax.rem(pos[a1] + SIDE - by, SIDE), a2, pos[a2], pl.ds(2 * i, 2))
            got.append(send.copy(part, part, p * 8 + 2 + i, a1, by))
        second.append(got)
    for p in range(3):
        a1, a2, a3 = ORDERS[p]
        for c in second[p]:
            c.wait_recv()
        here = planes[p].at[tuple(pos[a2] if d == a2 else slice(None) for d in dims[p])]
        third.append([send.copy(here, here, p * 8 + 4 + i, a2, by) for i, by in enumerate((1, 3))])
    ng[...] = dot(go_ref[...], wo_ref[...], 1, 1)
    for p in range(3):
        a1, a2, a3 = ORDERS[p]
        got = []
        for i, by in enumerate((1, 3)):
            third[p][i].wait_recv()
            other = lax.rem(pos[a2] + SIDE - by, SIDE)
            part = planes[p].at[tuple(other if d == a2 else pl.ds(2 * i, 2) for d in dims[p])]
            got.append(send.copy(part, part, p * 8 + 6 + i, a2, by))
        fourth.append(got)

    def landing(g, p, source, half=None):
        a3 = ORDERS[p][2]
        r0, rows = spans(g)[p]
        idx = []
        for d in range(3):
            if d == a3:
                idx.append(source)
            elif half is not None and d == dims[p][0]:
                idx.append(pl.ds(2 * half, 2))
            else:
                idx.append(slice(None))
        return arr[g].at[tuple(idx) + (slice(None), pl.ds(r0, rows), slice(None))]

    def pick(g, p, k, by):
        a3 = ORDERS[p][2]
        r0, rows = spans(g)[p]
        dest = tile_of(shifted(pos, a3, by))

        def one(j, _):
            hi, lo = lax.div(j, SIDE), lax.rem(j, SIDE)
            source = pos[a3] * STRIDE[a3] + hi * STRIDE[dims[p][0]] + lo * STRIDE[dims[p][1]]
            where = [None] * 3
            where[a3], where[dims[p][0]], where[dims[p][1]] = pos[a3], hi, lo
            for s in range(2):
                blk = jnp.maximum(want[dest, s * 64 + source], 0)
                val = planes[p][hi, lo, blk, pl.ds(offset(g, p), rows), :]
                if k < 3:
                    stage[k, hi, lo, s, pl.ds(g * 128 + r0, rows), :] = val
                else:
                    arr[g][tuple(where) + (s, pl.ds(r0, rows), slice(None))] = val
            return 0
        lax.fori_loop(0, SIDE * SIDE, one, 0)

    rows_of = lambda g, p: (slice(None), pl.ds(g * 128 + spans(g)[p][0], spans(g)[p][1]), slice(None))
    W = slice(None)
    zr, zd, zf = {}, {}, {}

    def z_send(g):
        zr[g], zd[g] = [], []
        for p in range(3):
            a3 = ORDERS[p][2]
            if g == 0:
                for c in fourth[p]:
                    c.wait_recv()
            pick(g, p, 2, 2)
            for i, by in enumerate((1, 3)):
                zr[g].append(send.copy(stage.at[(2, pl.ds(2 * i, 2), W) + rows_of(g, p)], rl_ref.at[(i, W, W) + rows_of(g, p)],
                                       24 + (g * 3 + p) * 6 + i, a3, by))
        for p in range(3):
            a3 = ORDERS[p][2]
            for i, by in enumerate((1, 3)):
                pick(g, p, i, by)
                zd[g].append(send.copy(stage.at[(i, W, W) + rows_of(g, p)], landing(g, p, pos[a3]),
                                       24 + (g * 3 + p) * 6 + 2 + i, a3, by))

    def z_own(g):
        for p in range(3):
            pick(g, p, 3, 0)

    def z_relay(g):
        zf[g] = []
        for p in range(3):
            a3 = ORDERS[p][2]
            for i, by in enumerate((1, 3)):
                zr[g][p * 2 + i].wait_recv()
                zf[g].append(send.copy(rl_ref.at[(i, W, W) + rows_of(g, p)], landing(g, p, lax.rem(pos[a3] + SIDE - by, SIDE), i),
                                       24 + (g * 3 + p) * 6 + 4 + i, a3, by))

    def entries(g, b, cur):
        return pltpu.make_async_copy(kvb.at[cur], ent_ref.at[g, pl.ds(b * L, L)], ent_sem.at[cur])

    base = lax.rem(me, 2) * 4

    def forward(g):
        for c in zd[g] + zf[g]:
            c.wait_recv()

        def one(b, _):
            cur = lax.rem(b, 2)
            if g == 0:
                @pl.when(b >= 2)
                def _():
                    entries(g, b, cur).wait()
            else:
                entries(g, b, cur).wait()
            for l in range(L):
                at = slot[base + b, l]
                pair, s = lax.div(at, 2), lax.rem(at, 2)
                x, yz = lax.div(pair, 16), lax.rem(pair, 16)
                kvb[cur, l] = arr[g][x, lax.div(yz, 4), lax.rem(yz, 4), s]
            m, inv, out = attend_rows(qv[b, g], kvb[cur].reshape(L * 128, 128), e)
            entries(g, b, cur).start()
            stv[b, g] = jnp.concatenate([m[:, :64], inv[:, 64:]], axis=1)
            att[b, g] = out.astype(BF16)
            return 0
        lax.fori_loop(0, nb, one, 0)
        c = pltpu.make_async_copy(stv.at[:, g], stat_ref.at[:, g], out_sem.at[1 + g])
        c.start()
        outs.append(c)

    tables[0].wait()
    tables[1].wait()
    z_send(0)
    z_send(1)
    z_own(0)
    z_relay(0)
    z_send(2)
    z_own(1)
    z_relay(1)
    z_send(3)
    forward(0)
    z_own(2)
    z_relay(2)
    forward(1)
    z_own(3)
    z_relay(3)
    forward(2)
    forward(3)

    for b in range(nb):
        rows = slice(b * 128, b * 128 + 128)
        a = []
        for j in range(6):
            a.append(jnp.concatenate([att[b, h // 3, (h % 3) * 128:(h % 3) * 128 + 128, :][:, 64:] for h in (2 * j, 2 * j + 1)], axis=1))
        a = jnp.concatenate(a, axis=1).astype(F32)
        root = jnp.sqrt(jnp.sum(a * a, axis=1, keepdims=True) * (1.0 / 768) + EPSILON)
        normed = a / root
        lay[rows, :] = dot(normed.astype(BF16), wo_ref[...]).astype(BF16)
        n = ng[rows, :]
        a = ((n - normed * (jnp.sum(n * normed, axis=1, keepdims=True) * (1.0 / 768))) / root).astype(BF16)
        for h in range(12):
            x = a[:, (h // 2) * 128:(h // 2) * 128 + 128][:, (h % 2) * 64:(h % 2) * 64 + 64]
            dov[b, h // 3, (h % 3) * 128:(h % 3) * 128 + 128, :] = jnp.concatenate([zero, x], axis=1)
    for i, (src, dst) in enumerate(((dov, dop_ref), (lay, lay_ref))):
        c = pltpu.make_async_copy(src, dst, out_sem.at[5 + i])
        c.start()
        outs.append(c)
    for b in (nb - 2, nb - 1):
        entries(3, b, b % 2).wait()
    for c in outs + tables[2:]:
        c.wait()
    for c in send.done:
        c.wait_send()


def forward_pass(tokens, grads, w_query, w_key, w_value, w_out, named, blocks):
    V, A = pl.BlockSpec(memory_space=pltpu.VMEM), pl.BlockSpec(memory_space=pl.ANY)
    bf = lambda *shape: jax.ShapeDtypeStruct(shape, BF16)
    i32 = lambda *shape: jax.ShapeDtypeStruct(shape, jnp.int32)
    vm = lambda *shape: pltpu.VMEM(shape, BF16)
    vi = lambda *shape: pltpu.VMEM(shape, jnp.int32)
    dma = lambda *shape: pltpu.SemaphoreType.DMA(shape)
    out = pl.pallas_call(
        forward_kernel,
        in_specs=[V] * 8,
        out_specs=[A] * 8,
        out_shape=[bf(512, 768), bf(4, 4, 384, 128), bf(4, 4, 384, 128), jax.ShapeDtypeStruct((4, 4, 384, 128), F32),
                   bf(4, 64, 128, 128), i32(64, 128), i32(64, 128), bf(2, 2, 4, 2, 512, 128)],
        scratch_shapes=[vm(4, 512, 128), vm(4, 512, 128)] + [vm(4, 4, 4, sum(c[p] for c in CUTS), 128) for p in range(3)] + [
            vm(3, 4, 4, 2, 512, 128)] + [vm(4, 4, 4, 2, 128, 128)] * 4 + [pltpu.VMEM((384, 2048), F32), vm(2, 16, 128, 128),
            vm(4, 4, 384, 128), vm(4, 4, 384, 128), pltpu.VMEM((4, 4, 384, 128), F32), vm(4, 4, 384, 128),
            pltpu.VMEM((512, 768), F32), vm(512, 768),
            vi(256, 128), vi(256, 128), vi(64, 128), vi(64, 128), vi(8, 128),
            pltpu.SMEM((64, 128), jnp.int32), pltpu.SMEM((8, 128), jnp.int32),
            dma(96), dma(96), dma(2), dma(12), dma(4), dma(2), dma(7)],
        compiler_params=pltpu.CompilerParams(collective_id=0, has_side_effects=True, vmem_limit_bytes=67043328),
        name="forward",
    )(tokens, grads, w_query, w_key, w_value, w_out, named, blocks)
    return out[:7]


def return_kernel(wanted, inv, qp_ref, dop_ref, stat_ref, ent_ref, dq_ref, out_ref, rl_ref, yl_ref, xl_ref,
                  kvb, qv, dov, stv, p, t, dqs, parts, stage, rz, sums, gs, ys, hs, xs, total,
                  send_sem, recv_sem, swap_sem, kv_sem, in_sem):
    pos, core = place(), lax.axis_index("vintage")
    dims = [tuple(sorted(o[:2])) for o in ORDERS]
    send = Sender(pos, core, send_sem, recv_sem)
    nb = qv.shape[0]
    me = tile_of(pos)
    L = kvb.shape[1]
    greet(pos, core, False)

    def turn(axis, by):
        return lax.rem(pos[axis] + by, SIDE)

    def key(g, p, i):
        return (g * 3 + p) * 18 + i

    def load(g, b, slot):
        return pltpu.make_async_copy(ent_ref.at[g, pl.ds(b * L, L)], kvb.at[slot], kv_sem.at[slot])

    load(0, 0, 0).start()
    rows_in = [[pltpu.make_async_copy(src.at[:, g], dst.at[:, g], in_sem.at[g, i])
                for i, (src, dst) in enumerate(((qp_ref, qv), (dop_ref, dov), (stat_ref, stv)))] for g in range(4)]
    for c in rows_in[0]:
        c.start()

    def backward(g):
        for c in rows_in[g]:
            c.wait()
        if g < 3:
            for c in rows_in[g + 1]:
                c.start()

        def one(b, _):
            cur = lax.rem(b, 2)
            load(g, b, cur).wait()

            @pl.when(b + 1 < nb)
            def _():
                load(g, b + 1, 1 - cur).start()

            if g < 3:
                @pl.when(b + 1 == nb)
                def _():
                    load(g + 1, 0, 0).start()

            kv = kvb[cur].reshape(L * 128, 128)
            q, do = qv[b, g], dov[b, g]
            m = jnp.broadcast_to(stv[b, g, :, 0:1], (384, 128))
            nrm = jnp.broadcast_to(stv[b, g, :, 64:65], (384, 128))
            s = dot(q, kv, 1, 1)
            dp = dot((do.astype(F32) * 0.125).astype(BF16), kv, 1, 1)
            rd = jnp.zeros((384, 128), F32)
            for i in range(L):
                cols = slice(i * 128, i * 128 + 128)
                pr = jnp.exp2((s[:, cols] - m) * SCALE) * nrm
                x = pr * dp[:, cols]
                p[:, cols] = pr
                t[:, cols] = x
                rd = rd + x
            rd = jnp.broadcast_to(jnp.sum(rd, axis=1, keepdims=True), (384, 128))
            ds_, low = [], []
            for i in range(L):
                cols = slice(i * 128, i * 128 + 128)
                pr = p[:, cols]
                ds_.append((t[:, cols] - pr * rd).astype(BF16))
                low.append(pr.astype(BF16))
            ds_, low = jnp.concatenate(ds_, axis=1), jnp.concatenate(low, axis=1)
            dqs[b, g] = dot(ds_, kv).astype(BF16)
            part = dot(jnp.concatenate([ds_, low], axis=0), jnp.concatenate([q, do], axis=0), 0, 0)
            parts[pl.ds(b * L, L)] = part.astype(BF16).reshape(L, 128, 128)
            return 0
        lax.fori_loop(0, nb, one, 0)

    zr, zd, zf, yr, yd, yf, xr, xd, xf = [{} for _ in range(9)]

    def slots_of(g, p, level, half=None):
        a3 = ORDERS[p][2]
        r0, rows = spans(g)[p]
        idx = []
        for d in range(3):
            if d == a3:
                idx.append(level)
            elif half is not None and d == dims[p][0]:
                idx.append(pl.ds(2 * half, 2))
            else:
                idx.append(slice(None))
        return stage.at[(g % 2,) + tuple(idx) + (slice(None), pl.ds(r0, rows), slice(None))]

    def at_rows(ref, g, p, lead):
        r0, rows = spans(g)[p]
        return ref.at[(g,) + tuple(lead) + (pl.ds(r0, rows), slice(None))]

    W = slice(None)

    def z_send(g):
        if g >= 2:
            for c in zr[g - 2] + zd[g - 2]:
                c.wait_send()

        def place_part(j, _):
            x, y, z = lax.div(j, 16), lax.rem(lax.div(j, 4), 4), lax.rem(j, 4)
            for s in range(2):
                stage[g % 2, x, y, z, s] = parts[inv[me, s * 64 + j]]
            return 0
        lax.fori_loop(0, 64, place_part, 0)
        if g == 0:
            greet_wait()
        zr[g], zd[g] = [], []
        for p in range(3):
            a3 = ORDERS[p][2]
            for i, by in enumerate((1, 3)):
                zr[g].append(send.copy(slots_of(g, p, turn(a3, 2), i), at_rows(rl_ref, g, p, (i, W, W, W)), key(g, p, i), a3, by))
        for p in range(3):
            a3 = ORDERS[p][2]
            for i, by in enumerate((1, 3)):
                zd[g].append(send.copy(slots_of(g, p, turn(a3, by)), at_rows(rz, g, p, (i, W, W, W)), key(g, p, 2 + i), a3, by))

    def z_relay(g):
        zf[g] = []
        for p in range(3):
            a3 = ORDERS[p][2]
            for i, by in enumerate((1, 3)):
                zr[g][p * 2 + i].wait_recv()
                zf[g].append(send.copy(at_rows(rl_ref, g, p, (i, W, W, W)), at_rows(rz, g, p, (2, pl.ds(2 * i, 2), W, W)),
                                       key(g, p, 4 + i), a3, by))

    def add_up(g, p, k, by, first, last):
        a3 = ORDERS[p][2]
        r0, rows = spans(g)[p]
        source = tile_of(shifted(pos, a3, by))

        def one(j, _):
            hi, lo = lax.div(j, SIDE), lax.rem(j, SIDE)
            holder = pos[a3] * STRIDE[a3] + hi * STRIDE[dims[p][0]] + lo * STRIDE[dims[p][1]]
            where = [None] * 3
            where[a3], where[dims[p][0]], where[dims[p][1]] = pos[a3], hi, lo
            vals = []
            for s in range(2):
                at = (k, hi, lo, s) if k < 3 else tuple(where) + (s,)
                ref, lead = (rz, g) if k < 3 else (stage, g % 2)
                vals.append(ref[(lead,) + at + (pl.ds(r0, rows), slice(None))].astype(F32))
            want = [wanted[source, s * 64 + holder] for s in range(2)]
            for b in range(4):
                x = jnp.where(want[0] == b, vals[0], 0.0) + jnp.where(want[1] == b, vals[1], 0.0)
                if not first:
                    x = x + sums[hi, lo, b, pl.ds(r0, rows), :]
                if last:
                    gs[g, hi, lo, b, pl.ds(r0, rows), :] = x.astype(BF16)
                else:
                    sums[hi, lo, b, pl.ds(r0, rows), :] = x
            return 0
        lax.fori_loop(0, SIDE * SIDE, one, 0)

    def z_sum(g):
        for p in range(3):
            add_up(g, p, 3, 0, True, False)
        for i, by in enumerate((3, 1)):
            for p in range(3):
                zd[g][p * 2 + i].wait_recv()
                add_up(g, p, i, by, False, False)

    def lines(g, p, axis, index, half=None):
        idx = []
        for d in dims[p]:
            if d == axis:
                idx.append(index)
            else:
                idx.append(slice(None) if half is None else pl.ds(2 * half, 2))
        return at_rows(gs, g, p, tuple(idx) + (W,))

    def y_send(g):
        yr[g], yd[g] = [], []
        for p in range(3):
            a2 = ORDERS[p][1]
            for c in zf[g][p * 2:p * 2 + 2]:
                c.wait_recv()
            add_up(g, p, 2, 2, False, True)
        for p in range(3):
            a2 = ORDERS[p][1]
            for i, by in enumerate((1, 3)):
                yr[g].append(send.copy(lines(g, p, a2, turn(a2, 2), i), at_rows(yl_ref, g, p, (i, W, W)), key(g, p, 6 + i), a2, by))
        for p in range(3):
            a2 = ORDERS[p][1]
            for i, by in enumerate((1, 3)):
                yd[g].append(send.copy(lines(g, p, a2, turn(a2, by)), at_rows(ys, g, p, (i, W, W)), key(g, p, 8 + i), a2, by))

    def y_relay(g):
        yf[g] = []
        for p in range(3):
            a2 = ORDERS[p][1]
            for i, by in enumerate((1, 3)):
                yr[g][p * 2 + i].wait_recv()
                yf[g].append(send.copy(at_rows(yl_ref, g, p, (i, W, W)), at_rows(ys, g, p, (2, pl.ds(2 * i, 2), W)),
                                       key(g, p, 10 + i), a2, by))

    def x_send(g):
        xr[g], xd[g] = [], []
        for p in range(3):
            a1, a2, a3 = ORDERS[p]
            r0, rows = spans(g)[p]
            at = (pl.ds(r0, rows), slice(None))
            for c in yd[g][p * 2:p * 2 + 2] + yf[g][p * 2:p * 2 + 2]:
                c.wait_recv()

            def row(j, _, p=p, a1=a1, a2=a2, at=at):
                i1, b = lax.div(j, 4), lax.rem(j, 4)
                mine = gs[(g,) + tuple(i1 if d == a1 else pos[a2] for d in dims[p]) + (b,) + at].astype(F32)
                for k in range(3):
                    mine = mine + ys[(g, k, i1, b) + at].astype(F32)
                hs[(g, i1, b) + at] = mine.astype(BF16)
                return 0
            lax.fori_loop(0, 16, row, 0)
        for p in range(3):
            a1 = ORDERS[p][0]
            for i, by in enumerate((1, 3)):
                xr[g].append(send.copy(at_rows(hs, g, p, (turn(a1, 2), pl.ds(2 * i, 2))), at_rows(xl_ref, g, p, (i, W)), key(g, p, 12 + i), a1, by))
        for p in range(3):
            a1 = ORDERS[p][0]
            for i, by in enumerate((1, 3)):
                xd[g].append(send.copy(at_rows(hs, g, p, (turn(a1, by), W)), at_rows(xs, g, p, (i, W)), key(g, p, 14 + i), a1, by))

    def x_relay(g):
        xf[g] = []
        for p in range(3):
            a1 = ORDERS[p][0]
            for i, by in enumerate((1, 3)):
                xr[g][p * 2 + i].wait_recv()
                xf[g].append(send.copy(at_rows(xl_ref, g, p, (i, W)), at_rows(xs, g, p, (2, pl.ds(2 * i, 2))),
                                       key(g, p, 16 + i), a1, by))

    swaps = []

    def finish(g):
        for p in range(3):
            a1 = ORDERS[p][0]
            r0, rows = spans(g)[p]
            at = (pl.ds(r0, rows), slice(None))
            for c in xd[g][p * 2:p * 2 + 2] + xf[g][p * 2:p * 2 + 2]:
                c.wait_recv()
            for b in range(4):
                mine = hs[(g, pos[a1], b) + at].astype(F32)
                for k in range(3):
                    mine = mine + xs[(g, k, b) + at].astype(F32)
                total[(g, b) + at] = mine.astype(BF16)
        c = pltpu.make_async_remote_copy(
            src_ref=total.at[g], dst_ref=out_ref.at[g], send_sem=swap_sem.at[0, g], recv_sem=swap_sem.at[1, g],
            device_id=(1 - core, tile_of(pos)), device_id_type=MESH)
        c.start()
        swaps.append(c)

    def queries_out(b):
        for j in range(6):
            dq_ref[b * 128:b * 128 + 128, j * 128:j * 128 + 128] = jnp.concatenate(
                [dqs[b, h // 3, (h % 3) * 128:(h % 3) * 128 + 128, :][:, :64] for h in (2 * j, 2 * j + 1)], axis=1)

    backward(0)
    z_send(0)
    backward(1)
    z_send(1)
    z_relay(0)
    z_sum(0)
    backward(2)
    z_send(2)
    z_relay(1)
    y_send(0)
    z_sum(1)
    backward(3)
    z_send(3)
    z_relay(2)
    y_send(1)
    y_relay(0)
    z_sum(2)
    z_relay(3)
    y_send(2)
    y_relay(1)
    x_send(0)
    z_sum(3)
    y_send(3)
    y_relay(2)
    x_send(1)
    x_relay(0)
    for b in range(4):
        queries_out(b)
    y_relay(3)
    x_send(2)
    x_relay(1)
    finish(0)
    x_send(3)
    x_relay(2)
    finish(1)
    x_relay(3)
    finish(2)
    finish(3)
    for c in swaps:
        c.wait()
    for g in range(4):
        late = zr[g] + zd[g] if g >= 2 else []
        for c in late + zf[g] + yr[g] + yd[g] + yf[g] + xr[g] + xd[g] + xf[g]:
            c.wait_send()


def gather_back(wanted, inv, qp, dop, stat, ent):
    V, A = pl.BlockSpec(memory_space=pltpu.VMEM), pl.BlockSpec(memory_space=pl.ANY)
    S = pl.BlockSpec(memory_space=pltpu.SMEM)
    bf = lambda *shape: jax.ShapeDtypeStruct(shape, BF16)
    vm = lambda *shape: pltpu.VMEM(shape, BF16)
    out = pl.pallas_call(
        return_kernel,
        in_specs=[S, S, A, A, A, A],
        out_specs=[V, A, A, A, A],
        out_shape=[bf(512, 768), bf(4, 4, 128, 128), bf(4, 2, 2, 4, 2, 128, 128), bf(4, 2, 2, 4, 128, 128), bf(4, 2, 2, 128, 128)],
        scratch_shapes=[
            vm(2, 16, 128, 128), vm(4, 4, 384, 128), vm(4, 4, 384, 128), pltpu.VMEM((4, 4, 384, 128), F32),
            pltpu.VMEM((384, 2048), F32), pltpu.VMEM((384, 2048), F32), vm(4, 4, 384, 128),
            vm(64, 128, 128), vm(2, 4, 4, 4, 2, 128, 128), vm(4, 3, 4, 4, 2, 128, 128),
            pltpu.VMEM((4, 4, 4, 128, 128), F32), vm(4, 4, 4, 4, 128, 128), vm(4, 3, 4, 4, 128, 128),
            vm(4, 4, 4, 128, 128), vm(4, 3, 4, 128, 128), vm(4, 4, 128, 128),
            pltpu.SemaphoreType.DMA((216,)), pltpu.SemaphoreType.DMA((216,)), pltpu.SemaphoreType.DMA((2, 4)),
            pltpu.SemaphoreType.DMA((2,)), pltpu.SemaphoreType.DMA((4, 3))],
        compiler_params=pltpu.CompilerParams(collective_id=1, has_side_effects=True, vmem_limit_bytes=67043328),
        name="collect",
    )(wanted, inv, qp, dop, stat, ent)
    return out[0], out[1]


def shards(patches, out_grad, w_query, w_key, w_value, w_out, key_tiles, key_blocks):
    w_kv = jnp.concatenate([w_key.reshape(-1, 4, 64), w_value.reshape(-1, 4, 64)], axis=2).reshape(-1, 512)
    rhs = jnp.concatenate([w_query, w_kv], axis=1)
    layer, qp, dop, stat, ent, wanted, inv = forward_pass(
        patches[0], out_grad[0], w_query, w_key, w_value, w_out, key_tiles[0], key_blocks[0])
    query_grad, kv_grad = gather_back(wanted, inv, qp, dop, stat, ent)
    kv_grad = kv_grad.transpose(1, 2, 0, 3).reshape(512, 512)
    lhs = jnp.concatenate([query_grad, kv_grad], axis=1)
    total = lax.dot_general(lhs, rhs, (((1,), (1,)), ((), ())), preferred_element_type=jnp.float32)
    return layer[None], total.astype(jnp.bfloat16)[None]


def solution(mesh):
    cubes = P("vintage", "tile", None)
    lists = P("vintage", None, None)
    return jax.shard_map(shards, mesh=mesh, in_specs=(cubes, cubes, P(), P(), P(), P(), lists, lists),
                         out_specs=(cubes, cubes), check_vma=False)
```

```python
import jax
import jax.numpy as jnp
from jax import lax
from jax.experimental import pallas as pl
from jax.experimental.pallas import tpu as pltpu
from jax.sharding import PartitionSpec as P

LOG2E = 1.4426950408889634
EPSILON = 1e-06
F32, BF16 = jnp.float32, jnp.bfloat16


def dot(a, b, ca=1, cb=0):
    return lax.dot_general(a, b, (((ca,), (cb,)), ((), ())), preferred_element_type=F32)


SCALE = 0.125 * LOG2E


def attend_rows(q, kv, e):
    rows, n = q.shape[0], kv.shape[0] // 128
    s = dot(q, kv, 1, 1)
    m = s[:, :128]
    for i in range(1, n):
        m = jnp.maximum(m, s[:, i * 128:i * 128 + 128])
    m = jnp.broadcast_to(jnp.max(m, axis=1, keepdims=True), (rows, 128))
    total = jnp.zeros((rows, 128), F32)
    for i in range(n):
        x = jnp.exp2((s[:, i * 128:i * 128 + 128] - m) * SCALE)
        e[:, i * 128:i * 128 + 128] = x
        total = total + x
    inv = jnp.broadcast_to(1.0 / jnp.sum(total, axis=1, keepdims=True), (rows, 128))
    low = jnp.concatenate([(e[:, i * 128:i * 128 + 128] * inv).astype(BF16) for i in range(n)], axis=1)
    return m, inv, dot(low, kv)


MESH = pl.DeviceIdType.MESH
SIDE = 4
ORDERS = ((0, 1, 2), (1, 2, 0), (2, 0, 1))
STRIDE = (16, 4, 1)


def place():
    tile = lax.axis_index("tile")
    return [lax.rem(lax.div(tile, s), SIDE) for s in STRIDE]


def shifted(pos, axis, by):
    moved = list(pos)
    moved[axis] = lax.rem(pos[axis] + by, SIDE)
    return moved


def tile_of(pos):
    return pos[0] * 16 + pos[1] * 4 + pos[2]


def greet(pos, core, wait=True):
    barrier = pltpu.get_barrier_semaphore()
    for axis in range(3):
        for by in (1, 3):
            pl.semaphore_signal(barrier, inc=1, device_id=(core, tile_of(shifted(pos, axis, by))), device_id_type=MESH)
    pl.semaphore_signal(barrier, inc=1, device_id=(1 - core, tile_of(pos)), device_id_type=MESH)
    if wait:
        greet_wait()


def greet_wait():
    pl.semaphore_wait(pltpu.get_barrier_semaphore(), 7)


class Sender:
    def __init__(self, pos, core, send_sem, recv_sem):
        self.pos, self.core, self.send_sem, self.recv_sem = pos, core, send_sem, recv_sem
        self.done = []

    def copy(self, src, dst, sem, axis, by):
        c = pltpu.make_async_remote_copy(
            src_ref=src, dst_ref=dst, send_sem=self.send_sem.at[sem], recv_sem=self.recv_sem.at[sem],
            device_id=(self.core, tile_of(shifted(self.pos, axis, by))), device_id_type=MESH)
        c.start()
        self.done.append(c)
        return c


def at_axis(ref, dims, index, axis, *rest):
    return ref.at[tuple(index if d == axis else slice(None) for d in dims) + rest]


CUTS = ((48, 48, 32), (48, 32, 48), (32, 48, 48), (48, 48, 32))


def spans(g):
    start = 0
    out = []
    for rows in CUTS[g]:
        out.append((start, rows))
        start += rows
    return out


def offset(g, p):
    return sum(CUTS[i][p] for i in range(g - g % 2, g))


def forward_kernel(tok_ref, go_ref, wq_ref, wk_ref, wv_ref, wo_ref, kt_ref, kb_ref,
                   lay_ref, qp_ref, dop_ref, stat_ref, ent_ref, want_ref, inv_ref, rl_ref,
                   mine, own, plane0, plane1, plane2, plane3, plane4, plane5, stage, arr0, arr1, arr2, arr3, e, kvb, qv, dov, stv, att, ng, lay,
                   named, ranks, tiles, wtab, itab, stab, want, slot,
                   send_sem, recv_sem, swap_sem, local_sem, tab_sem, ent_sem, out_sem):
    pos, core = place(), lax.axis_index("vintage")
    me = tile_of(pos)
    planes, arr = ((plane0, plane1), (plane2, plane3), (plane4, plane5)), (arr0, arr1, arr2, arr3)
    dims = [tuple(sorted(o[:2])) for o in ORDERS]
    send = Sender(pos, core, send_sem, recv_sem)
    nb, L = 4, 16
    greet(pos, core, False)

    k = dot(tok_ref[...], wk_ref[...]).astype(BF16)
    v = dot(tok_ref[...], wv_ref[...]).astype(BF16)
    for g in range(4):
        both = jnp.concatenate([k[:, g * 64:g * 64 + 64], v[:, g * 64:g * 64 + 64]], axis=1)
        for b in range(nb):
            mine[b, g * 128:g * 128 + 128, :] = both[b * 128:b * 128 + 128]

    greet_wait()
    swap = pltpu.make_async_remote_copy(
        src_ref=mine, dst_ref=own, send_sem=swap_sem.at[0], recv_sem=swap_sem.at[1],
        device_id=(1 - core, me), device_id_type=MESH)
    swap.start()

    swap.wait()

    def cell(p, h, a1, i1, a2, i2, *rest):
        return planes[p][h].at[tuple(i1 if d == a1 else i2 for d in dims[p]) + rest]

    local = {}
    for h in range(2):
        for p in range(3):
            a1, a2, a3 = ORDERS[p]
            local[p, h] = []
            for g in (2 * h, 2 * h + 1):
                r0, rows = spans(g)[p]
                c = pltpu.make_async_copy(own.at[:, pl.ds(g * 128 + r0, rows), :],
                                          cell(p, h, a1, pos[a1], a2, pos[a2], slice(None), pl.ds(offset(g, p), rows), slice(None)),
                                          local_sem.at[p * 4 + g])
                c.start()
                local[p, h].append(c)
    first, second, third, fourth = {}, {}, {}, {}
    pieces = [(p, h) for h in range(2) for p in range(3)]
    for p, h in pieces:
        a1, a2, a3 = ORDERS[p]
        for c in local[p, h]:
            c.wait()
        here = cell(p, h, a1, pos[a1], a2, pos[a2])
        first[p, h] = [send.copy(here, here, (h * 3 + p) * 8 + i, a1, by) for i, by in enumerate((1, 3))]
    kt, kb = kt_ref[...].T, kb_ref[...].T
    tiles[:, :L] = kt
    lane = lax.broadcasted_iota(jnp.int32, (256, 128), 1)
    tile = jnp.where(lane < 64, lane, lane - 64)
    row = lax.broadcasted_iota(jnp.int32, (256, 128), 0)
    quarter = row - (row // 4) * 4
    block, entry = jnp.zeros((256, 128), jnp.int32), jnp.zeros((256, 128), jnp.int32)
    for l in range(L):
        hit = kt[:, l:l + 1] == tile
        block = jnp.where(hit, kb[:, l:l + 1] + 1, block)
        entry = jnp.where(hit, quarter * L + l + 1, entry)
    lane4 = lax.broadcasted_iota(jnp.int32, (64, 128), 1)
    for source, table in ((block, wtab), (entry, itab)):
        named[...] = source
        one, two = jnp.zeros((64, 128), jnp.int32), jnp.zeros((64, 128), jnp.int32)
        for i in range(4):
            x = named[pl.ds(i, 64, stride=4), :]
            ranks[pl.ds(i, 64, stride=4), :] = jnp.where(one > 0, 1, 0)
            two = jnp.where((one > 0) & (x > 0), x, two)
            one = jnp.where(one > 0, one, x)
        table[...] = jnp.where(lane4 < 64, one, two) - 1
    itab[...] = jnp.maximum(itab[...], 0)
    half = pl.ds(pl.multiple_of(lax.div(me, 2) * 8, 8), 8)
    mine_kt, mine_rank = tiles[half, :], ranks[half, :]
    lane8 = lax.broadcasted_iota(jnp.int32, (8, 128), 1)
    found = jnp.zeros((8, 128), jnp.int32)
    for l in range(L):
        at = jnp.sum(jnp.where((mine_kt[:, l:l + 1] == lane8) & (lane8 < 64), lane8 * 2 + mine_rank, 0), axis=1, keepdims=True)
        found = jnp.where(lane8 == l, at, found)
    stab[...] = found
    tables = [pltpu.make_async_copy(wtab, want, tab_sem.at[0]), pltpu.make_async_copy(stab, slot, tab_sem.at[1]),
              pltpu.make_async_copy(wtab, want_ref, tab_sem.at[2]), pltpu.make_async_copy(itab, inv_ref, tab_sem.at[3])]
    for c in tables:
        c.start()

    for p, h in pieces:
        a1, a2, a3 = ORDERS[p]
        second[p, h] = []
        for i, by in enumerate((1, 3)):
            first[p, h][i].wait_recv()
            part = cell(p, h, a1, lax.rem(pos[a1] + SIDE - by, SIDE), a2, pos[a2], pl.ds(2 * i, 2))
            second[p, h].append(send.copy(part, part, (h * 3 + p) * 8 + 2 + i, a1, by))
    for p, h in pieces:
        a1, a2, a3 = ORDERS[p]
        for c in second[p, h]:
            c.wait_recv()
        here = planes[p][h].at[tuple(pos[a2] if d == a2 else slice(None) for d in dims[p])]
        third[p, h] = [send.copy(here, here, (h * 3 + p) * 8 + 4 + i, a2, by) for i, by in enumerate((1, 3))]
    zero = jnp.zeros((128, 64), BF16)
    q = dot(tok_ref[...], wq_ref[...]).astype(BF16)
    for b in range(nb):
        for h in range(12):
            x = q[b * 128:b * 128 + 128, (h // 2) * 128:(h // 2) * 128 + 128][:, (h % 2) * 64:(h % 2) * 64 + 64]
            qv[b, h // 3, (h % 3) * 128:(h % 3) * 128 + 128, :] = jnp.concatenate([x, zero], axis=1)
    outs = [pltpu.make_async_copy(qv, qp_ref, out_sem.at[0])]
    outs[0].start()
    ng[...] = dot(go_ref[...], wo_ref[...], 1, 1)
    for p, h in pieces:
        a1, a2, a3 = ORDERS[p]
        fourth[p, h] = []
        for i, by in enumerate((1, 3)):
            third[p, h][i].wait_recv()
            other = lax.rem(pos[a2] + SIDE - by, SIDE)
            part = planes[p][h].at[tuple(other if d == a2 else pl.ds(2 * i, 2) for d in dims[p])]
            fourth[p, h].append(send.copy(part, part, (h * 3 + p) * 8 + 6 + i, a2, by))

    def landing(g, p, source, half=None):
        a3 = ORDERS[p][2]
        r0, rows = spans(g)[p]
        idx = []
        for d in range(3):
            if d == a3:
                idx.append(source)
            elif half is not None and d == dims[p][0]:
                idx.append(pl.ds(2 * half, 2))
            else:
                idx.append(slice(None))
        return arr[g].at[tuple(idx) + (slice(None), pl.ds(r0, rows), slice(None))]

    def pick(g, p, k, by):
        a3 = ORDERS[p][2]
        r0, rows = spans(g)[p]
        dest = tile_of(shifted(pos, a3, by))

        def one(j, _):
            hi, lo = lax.div(j, SIDE), lax.rem(j, SIDE)
            source = pos[a3] * STRIDE[a3] + hi * STRIDE[dims[p][0]] + lo * STRIDE[dims[p][1]]
            where = [None] * 3
            where[a3], where[dims[p][0]], where[dims[p][1]] = pos[a3], hi, lo
            for s in range(2):
                blk = jnp.maximum(want[dest, s * 64 + source], 0)
                val = planes[p][g // 2][hi, lo, blk, pl.ds(offset(g, p), rows), :]
                if k < 3:
                    stage[k, hi, lo, s, pl.ds(g * 128 + r0, rows), :] = val
                else:
                    arr[g][tuple(where) + (s, pl.ds(r0, rows), slice(None))] = val
            return 0
        lax.fori_loop(0, SIDE * SIDE, one, 0)

    rows_of = lambda g, p: (slice(None), pl.ds(g * 128 + spans(g)[p][0], spans(g)[p][1]), slice(None))
    W = slice(None)
    zr, zd, zf = {}, {}, {}

    def z_send(g):
        zr[g], zd[g] = [], []
        for p in range(3):
            a3 = ORDERS[p][2]
            if g % 2 == 0:
                for c in fourth[p, g // 2]:
                    c.wait_recv()
            pick(g, p, 2, 2)
            for i, by in enumerate((1, 3)):
                zr[g].append(send.copy(stage.at[(2, pl.ds(2 * i, 2), W) + rows_of(g, p)], rl_ref.at[(i, W, W) + rows_of(g, p)],
                                       48 + (g * 3 + p) * 6 + i, a3, by))
        for p in range(3):
            a3 = ORDERS[p][2]
            for i, by in enumerate((1, 3)):
                pick(g, p, i, by)
                zd[g].append(send.copy(stage.at[(i, W, W) + rows_of(g, p)], landing(g, p, pos[a3]),
                                       48 + (g * 3 + p) * 6 + 2 + i, a3, by))

    def z_own(g):
        for p in range(3):
            pick(g, p, 3, 0)

    def z_relay(g):
        zf[g] = []
        for p in range(3):
            a3 = ORDERS[p][2]
            for i, by in enumerate((1, 3)):
                zr[g][p * 2 + i].wait_recv()
                zf[g].append(send.copy(rl_ref.at[(i, W, W) + rows_of(g, p)], landing(g, p, lax.rem(pos[a3] + SIDE - by, SIDE), i),
                                       48 + (g * 3 + p) * 6 + 4 + i, a3, by))

    def entries(g, b, cur):
        return pltpu.make_async_copy(kvb.at[cur], ent_ref.at[g, pl.ds(b * L, L)], ent_sem.at[cur])

    base = lax.rem(me, 2) * 4

    def forward(g):
        for c in zd[g] + zf[g]:
            c.wait_recv()

        def one(b, _):
            cur = lax.rem(b, 2)
            if g == 0:
                @pl.when(b >= 2)
                def _():
                    entries(g, b, cur).wait()
            else:
                entries(g, b, cur).wait()
            for l in range(L):
                at = slot[base + b, l]
                pair, s = lax.div(at, 2), lax.rem(at, 2)
                x, yz = lax.div(pair, 16), lax.rem(pair, 16)
                kvb[cur, l] = arr[g][x, lax.div(yz, 4), lax.rem(yz, 4), s]
            m, inv, out = attend_rows(qv[b, g], kvb[cur].reshape(L * 128, 128), e)
            entries(g, b, cur).start()
            stv[b, g] = jnp.concatenate([m[:, :64], inv[:, 64:]], axis=1)
            att[b, g] = out.astype(BF16)
            return 0
        lax.fori_loop(0, nb, one, 0)
        c = pltpu.make_async_copy(stv.at[:, g], stat_ref.at[:, g], out_sem.at[1 + g])
        c.start()
        outs.append(c)

    tables[0].wait()
    tables[1].wait()
    z_send(0)
    z_send(1)
    z_own(0)
    z_relay(0)
    z_send(2)
    z_own(1)
    z_relay(1)
    z_send(3)
    forward(0)
    z_own(2)
    z_relay(2)
    forward(1)
    z_own(3)
    z_relay(3)
    forward(2)
    forward(3)

    for b in range(nb):
        rows = slice(b * 128, b * 128 + 128)
        a = []
        for j in range(6):
            a.append(jnp.concatenate([att[b, h // 3, (h % 3) * 128:(h % 3) * 128 + 128, :][:, 64:] for h in (2 * j, 2 * j + 1)], axis=1))
        a = jnp.concatenate(a, axis=1).astype(F32)
        root = jnp.sqrt(jnp.sum(a * a, axis=1, keepdims=True) * (1.0 / 768) + EPSILON)
        normed = a / root
        lay[rows, :] = dot(normed.astype(BF16), wo_ref[...]).astype(BF16)
        n = ng[rows, :]
        a = ((n - normed * (jnp.sum(n * normed, axis=1, keepdims=True) * (1.0 / 768))) / root).astype(BF16)
        for h in range(12):
            x = a[:, (h // 2) * 128:(h // 2) * 128 + 128][:, (h % 2) * 64:(h % 2) * 64 + 64]
            dov[b, h // 3, (h % 3) * 128:(h % 3) * 128 + 128, :] = jnp.concatenate([zero, x], axis=1)
    for i, (src, dst) in enumerate(((dov, dop_ref), (lay, lay_ref))):
        c = pltpu.make_async_copy(src, dst, out_sem.at[5 + i])
        c.start()
        outs.append(c)
    for b in (nb - 2, nb - 1):
        entries(3, b, b % 2).wait()
    for c in outs + tables[2:]:
        c.wait()
    for c in send.done:
        c.wait_send()


def forward_pass(tokens, grads, w_query, w_key, w_value, w_out, named, blocks):
    V, A = pl.BlockSpec(memory_space=pltpu.VMEM), pl.BlockSpec(memory_space=pl.ANY)
    bf = lambda *shape: jax.ShapeDtypeStruct(shape, BF16)
    i32 = lambda *shape: jax.ShapeDtypeStruct(shape, jnp.int32)
    vm = lambda *shape: pltpu.VMEM(shape, BF16)
    vi = lambda *shape: pltpu.VMEM(shape, jnp.int32)
    dma = lambda *shape: pltpu.SemaphoreType.DMA(shape)
    out = pl.pallas_call(
        forward_kernel,
        in_specs=[V] * 8,
        out_specs=[A] * 8,
        out_shape=[bf(512, 768), bf(4, 4, 384, 128), bf(4, 4, 384, 128), jax.ShapeDtypeStruct((4, 4, 384, 128), F32),
                   bf(4, 64, 128, 128), i32(64, 128), i32(64, 128), bf(2, 2, 4, 2, 512, 128)],
        scratch_shapes=[vm(4, 512, 128), vm(4, 512, 128)] + [
            vm(4, 4, 4, CUTS[2 * h][p] + CUTS[2 * h + 1][p], 128) for p in range(3) for h in range(2)] + [
            vm(3, 4, 4, 2, 512, 128)] + [vm(4, 4, 4, 2, 128, 128)] * 4 + [pltpu.VMEM((384, 2048), F32), vm(2, 16, 128, 128),
            vm(4, 4, 384, 128), vm(4, 4, 384, 128), pltpu.VMEM((4, 4, 384, 128), F32), vm(4, 4, 384, 128),
            pltpu.VMEM((512, 768), F32), vm(512, 768),
            vi(256, 128), vi(256, 128), vi(256, 128), vi(64, 128), vi(64, 128), vi(8, 128),
            pltpu.SMEM((64, 128), jnp.int32), pltpu.SMEM((8, 128), jnp.int32),
            dma(120), dma(120), dma(2), dma(12), dma(4), dma(2), dma(7)],
        compiler_params=pltpu.CompilerParams(collective_id=0, has_side_effects=True, vmem_limit_bytes=67043328),
        name="forward",
    )(tokens, grads, w_query, w_key, w_value, w_out, named, blocks)
    return out[:7]


def return_kernel(wanted, inv, qp_ref, dop_ref, stat_ref, ent_ref, wq_ref, wk_ref, wv_ref, out_ref, rl_ref, yl_ref, xl_ref,
                  kvb, qv, dov, stv, p, t, dqs, parts, stage, rz, sums, gs, ys, hs, xs, total, got, wq, flat, wkv,
                  send_sem, recv_sem, swap_sem, kv_sem, in_sem, w_sem):
    pos, core = place(), lax.axis_index("vintage")
    dims = [tuple(sorted(o[:2])) for o in ORDERS]
    send = Sender(pos, core, send_sem, recv_sem)
    nb = qv.shape[0]
    me = tile_of(pos)
    L = kvb.shape[1]
    greet(pos, core, False)

    def turn(axis, by):
        return lax.rem(pos[axis] + by, SIDE)

    def key(g, p, i):
        return (g * 3 + p) * 18 + i

    def load(g, b, slot):
        return pltpu.make_async_copy(ent_ref.at[g, pl.ds(b * L, L)], kvb.at[slot], kv_sem.at[slot])

    load(0, 0, 0).start()
    rows_in = [[pltpu.make_async_copy(src.at[:, g], dst.at[:, g % dst.shape[1]], in_sem.at[g, i])
                for i, (src, dst) in enumerate(((qp_ref, qv), (dop_ref, dov), (stat_ref, stv)))] for g in range(4)]
    for c in rows_in[0]:
        c.start()
    weights = [pltpu.make_async_copy(src, dst, w_sem.at[i]) for i, (src, dst) in enumerate(((wq_ref, wq), (wk_ref, flat.at[0:768]), (wv_ref, flat.at[768:1536])))]
    for c in weights:
        c.start()

    def backward(g):
        for c in rows_in[g]:
            c.wait()
        if g < 3:
            for c in rows_in[g + 1]:
                c.start()

        def one(b, _):
            cur = lax.rem(b, 2)
            load(g, b, cur).wait()

            @pl.when(b + 1 < nb)
            def _():
                load(g, b + 1, 1 - cur).start()

            if g < 3:
                @pl.when(b + 1 == nb)
                def _():
                    load(g + 1, 0, 0).start()

            kv = kvb[cur].reshape(L * 128, 128)
            q, do = qv[b, g % 2], dov[b, g % 2]
            m = jnp.broadcast_to(stv[b, g % 2, :, 0:1], (384, 128))
            nrm = jnp.broadcast_to(stv[b, g % 2, :, 64:65], (384, 128))
            s = dot(q, kv, 1, 1)
            dp = dot((do.astype(F32) * 0.125).astype(BF16), kv, 1, 1)
            rd = jnp.zeros((384, 128), F32)
            for i in range(L):
                cols = slice(i * 128, i * 128 + 128)
                pr = jnp.exp2((s[:, cols] - m) * SCALE) * nrm
                x = pr * dp[:, cols]
                p[:, cols] = pr
                t[:, cols] = x
                rd = rd + x
            rd = jnp.broadcast_to(jnp.sum(rd, axis=1, keepdims=True), (384, 128))
            ds_, low = [], []
            for i in range(L):
                cols = slice(i * 128, i * 128 + 128)
                pr = p[:, cols]
                ds_.append((t[:, cols] - pr * rd).astype(BF16))
                low.append(pr.astype(BF16))
            ds_, low = jnp.concatenate(ds_, axis=1), jnp.concatenate(low, axis=1)
            dqs[b, g] = dot(ds_, kv).astype(BF16)
            part = dot(jnp.concatenate([ds_, low], axis=0), jnp.concatenate([q, do], axis=0), 0, 0)
            parts[pl.ds(b * L, L)] = part.astype(BF16).reshape(L, 128, 128)
            return 0
        lax.fori_loop(0, nb, one, 0)

    zr, zd, zf, yr, yd, yf, xr, xd, xf = [{} for _ in range(9)]

    def slots_of(g, p, level, half=None):
        a3 = ORDERS[p][2]
        r0, rows = spans(g)[p]
        idx = []
        for d in range(3):
            if d == a3:
                idx.append(level)
            elif half is not None and d == dims[p][0]:
                idx.append(pl.ds(2 * half, 2))
            else:
                idx.append(slice(None))
        return stage.at[(g % 2,) + tuple(idx) + (slice(None), pl.ds(r0, rows), slice(None))]

    def at_rows(ref, g, p, lead):
        r0, rows = spans(g)[p]
        return ref.at[(g,) + tuple(lead) + (pl.ds(r0, rows), slice(None))]

    W = slice(None)

    def z_send(g):
        if g >= 2:
            for c in zr[g - 2] + zd[g - 2]:
                c.wait_send()

        def place_part(j, _):
            x, y, z = lax.div(j, 16), lax.rem(lax.div(j, 4), 4), lax.rem(j, 4)
            for s in range(2):
                stage[g % 2, x, y, z, s] = parts[inv[me, s * 64 + j]]
            return 0
        lax.fori_loop(0, 64, place_part, 0)
        if g == 0:
            greet_wait()
        zr[g], zd[g] = [], []
        for p in range(3):
            a3 = ORDERS[p][2]
            for i, by in enumerate((1, 3)):
                zr[g].append(send.copy(slots_of(g, p, turn(a3, 2), i), at_rows(rl_ref, g, p, (i, W, W, W)), key(g, p, i), a3, by))
        for p in range(3):
            a3 = ORDERS[p][2]
            for i, by in enumerate((1, 3)):
                zd[g].append(send.copy(slots_of(g, p, turn(a3, by)), at_rows(rz, g, p, (i, W, W, W)), key(g, p, 2 + i), a3, by))

    def z_relay(g):
        zf[g] = []
        for p in range(3):
            a3 = ORDERS[p][2]
            for i, by in enumerate((1, 3)):
                zr[g][p * 2 + i].wait_recv()
                zf[g].append(send.copy(at_rows(rl_ref, g, p, (i, W, W, W)), at_rows(rz, g, p, (2, pl.ds(2 * i, 2), W, W)),
                                       key(g, p, 4 + i), a3, by))

    def add_up(g, p, k, by, first, last):
        a3 = ORDERS[p][2]
        r0, rows = spans(g)[p]
        source = tile_of(shifted(pos, a3, by))

        def one(j, _):
            hi, lo = lax.div(j, SIDE), lax.rem(j, SIDE)
            holder = pos[a3] * STRIDE[a3] + hi * STRIDE[dims[p][0]] + lo * STRIDE[dims[p][1]]
            where = [None] * 3
            where[a3], where[dims[p][0]], where[dims[p][1]] = pos[a3], hi, lo
            vals = []
            for s in range(2):
                at = (k, hi, lo, s) if k < 3 else tuple(where) + (s,)
                ref, lead = (rz, g) if k < 3 else (stage, g % 2)
                vals.append(ref[(lead,) + at + (pl.ds(r0, rows), slice(None))].astype(F32))
            want = [wanted[source, s * 64 + holder] for s in range(2)]
            for b in range(4):
                x = jnp.where(want[0] == b, vals[0], 0.0) + jnp.where(want[1] == b, vals[1], 0.0)
                if not first:
                    x = x + sums[hi, lo, b, pl.ds(r0, rows), :]
                if last:
                    gs[g, hi, lo, b, pl.ds(r0, rows), :] = x.astype(BF16)
                else:
                    sums[hi, lo, b, pl.ds(r0, rows), :] = x
            return 0
        lax.fori_loop(0, SIDE * SIDE, one, 0)

    def z_sum(g):
        for p in range(3):
            add_up(g, p, 3, 0, True, False)
        for i, by in enumerate((3, 1)):
            for p in range(3):
                zd[g][p * 2 + i].wait_recv()
                add_up(g, p, i, by, False, False)

    def lines(g, p, axis, index, half=None):
        idx = []
        for d in dims[p]:
            if d == axis:
                idx.append(index)
            else:
                idx.append(slice(None) if half is None else pl.ds(2 * half, 2))
        return at_rows(gs, g, p, tuple(idx) + (W,))

    def y_send(g):
        yr[g], yd[g] = [], []
        for p in range(3):
            a2 = ORDERS[p][1]
            for c in zf[g][p * 2:p * 2 + 2]:
                c.wait_recv()
            add_up(g, p, 2, 2, False, True)
        for p in range(3):
            a2 = ORDERS[p][1]
            for i, by in enumerate((1, 3)):
                yr[g].append(send.copy(lines(g, p, a2, turn(a2, 2), i), at_rows(yl_ref, g, p, (i, W, W)), key(g, p, 6 + i), a2, by))
        for p in range(3):
            a2 = ORDERS[p][1]
            for i, by in enumerate((1, 3)):
                yd[g].append(send.copy(lines(g, p, a2, turn(a2, by)), at_rows(ys, g, p, (i, W, W)), key(g, p, 8 + i), a2, by))

    def y_relay(g):
        yf[g] = []
        for p in range(3):
            a2 = ORDERS[p][1]
            for i, by in enumerate((1, 3)):
                yr[g][p * 2 + i].wait_recv()
                yf[g].append(send.copy(at_rows(yl_ref, g, p, (i, W, W)), at_rows(ys, g, p, (2, pl.ds(2 * i, 2), W)),
                                       key(g, p, 10 + i), a2, by))

    def x_send(g):
        xr[g], xd[g] = [], []
        for p in range(3):
            a1, a2, a3 = ORDERS[p]
            r0, rows = spans(g)[p]
            at = (pl.ds(r0, rows), slice(None))
            for c in yd[g][p * 2:p * 2 + 2] + yf[g][p * 2:p * 2 + 2]:
                c.wait_recv()

            def row(j, _, p=p, a1=a1, a2=a2, at=at):
                i1, b = lax.div(j, 4), lax.rem(j, 4)
                mine = gs[(g,) + tuple(i1 if d == a1 else pos[a2] for d in dims[p]) + (b,) + at].astype(F32)
                for k in range(3):
                    mine = mine + ys[(g, k, i1, b) + at].astype(F32)
                hs[(g, i1, b) + at] = mine.astype(BF16)
                return 0
            lax.fori_loop(0, 16, row, 0)
        for p in range(3):
            a1 = ORDERS[p][0]
            for i, by in enumerate((1, 3)):
                xr[g].append(send.copy(at_rows(hs, g, p, (turn(a1, 2), pl.ds(2 * i, 2))), at_rows(xl_ref, g, p, (i, W)), key(g, p, 12 + i), a1, by))
        for p in range(3):
            a1 = ORDERS[p][0]
            for i, by in enumerate((1, 3)):
                xd[g].append(send.copy(at_rows(hs, g, p, (turn(a1, by), W)), at_rows(xs, g, p, (i, W)), key(g, p, 14 + i), a1, by))

    def x_relay(g):
        xf[g] = []
        for p in range(3):
            a1 = ORDERS[p][0]
            for i, by in enumerate((1, 3)):
                xr[g][p * 2 + i].wait_recv()
                xf[g].append(send.copy(at_rows(xl_ref, g, p, (i, W)), at_rows(xs, g, p, (2, pl.ds(2 * i, 2))),
                                       key(g, p, 16 + i), a1, by))

    swaps = []

    def finish(g):
        for p in range(3):
            a1 = ORDERS[p][0]
            r0, rows = spans(g)[p]
            at = (pl.ds(r0, rows), slice(None))
            for c in xd[g][p * 2:p * 2 + 2] + xf[g][p * 2:p * 2 + 2]:
                c.wait_recv()
            for b in range(4):
                mine = hs[(g, pos[a1], b) + at].astype(F32)
                for k in range(3):
                    mine = mine + xs[(g, k, b) + at].astype(F32)
                total[(g, b) + at] = mine.astype(BF16)
        c = pltpu.make_async_remote_copy(
            src_ref=total.at[g], dst_ref=got.at[g], send_sem=swap_sem.at[0, g], recv_sem=swap_sem.at[1, g],
            device_id=(1 - core, tile_of(pos)), device_id_type=MESH)
        c.start()
        swaps.append(c)

    def sums_at(b):
        return slice(b % 3 * 128, b % 3 * 128 + 128), slice(b // 3 * 768, b // 3 * 768 + 768)

    def query_term(b):
        heads = [dqs[b, h // 3, (h % 3) * 128:(h % 3) * 128 + 128, :][:, :64] for h in range(12)]
        p[sums_at(b)] = dot(jnp.concatenate(heads, axis=1), wq[...], 1, 1)

    def key_term(half):
        for g in (2 * half, 2 * half + 1):
            swaps[g].wait()
        for b in range(nb):
            both = jnp.concatenate([got[2 * half, b], got[2 * half + 1, b]], axis=1)
            x = p[sums_at(b)] + dot(both, wkv[:, half * 256:half * 256 + 256], 1, 1)
            if half == 0:
                p[sums_at(b)] = x
            else:
                for i in range(3):
                    flat[i * 512 + b * 128:i * 512 + b * 128 + 128, :] = x[:, i * 256:i * 256 + 256].astype(BF16)

    backward(0)
    z_send(0)
    backward(1)
    z_send(1)
    z_relay(0)
    z_sum(0)
    backward(2)
    z_send(2)
    z_relay(1)
    y_send(0)
    z_sum(1)
    backward(3)
    z_send(3)
    z_relay(2)
    y_send(1)
    y_relay(0)
    z_sum(2)
    z_relay(3)
    y_send(2)
    y_relay(1)
    x_send(0)
    z_sum(3)
    y_send(3)
    y_relay(2)
    x_send(1)
    x_relay(0)
    for c in weights:
        c.wait()
    for g in range(4):
        wkv[:, g * 128:g * 128 + 128] = jnp.concatenate([flat[0:768, g * 64:g * 64 + 64], flat[768:1536, g * 64:g * 64 + 64]], axis=1)
    query_term(0)
    query_term(1)
    y_relay(3)
    x_send(2)
    x_relay(1)
    finish(0)
    query_term(2)
    query_term(3)
    x_send(3)
    x_relay(2)
    finish(1)
    x_relay(3)
    finish(2)
    key_term(0)
    finish(3)
    key_term(1)
    results = [pltpu.make_async_copy(flat.at[i * 512:i * 512 + 512], out_ref.at[:, i * 256:i * 256 + 256], w_sem.at[3 + i]) for i in range(3)]
    for c in results:
        c.start()
    for c in results:
        c.wait()
    for g in range(4):
        late = zr[g] + zd[g] if g >= 2 else []
        for c in late + zf[g] + yr[g] + yd[g] + yf[g] + xr[g] + xd[g] + xf[g]:
            c.wait_send()


def gather_back(wanted, inv, qp, dop, stat, ent, w_query, w_key, w_value):
    V, A = pl.BlockSpec(memory_space=pltpu.VMEM), pl.BlockSpec(memory_space=pl.ANY)
    S = pl.BlockSpec(memory_space=pltpu.SMEM)
    bf = lambda *shape: jax.ShapeDtypeStruct(shape, BF16)
    vm = lambda *shape: pltpu.VMEM(shape, BF16)
    out = pl.pallas_call(
        return_kernel,
        in_specs=[S, S] + [A] * 7,
        out_specs=[A] * 4,
        out_shape=[bf(512, 768), bf(4, 2, 2, 4, 2, 128, 128), bf(4, 2, 2, 4, 128, 128), bf(4, 2, 2, 128, 128)],
        scratch_shapes=[
            vm(2, 16, 128, 128), vm(4, 2, 384, 128), vm(4, 2, 384, 128), pltpu.VMEM((4, 2, 384, 128), F32),
            pltpu.VMEM((384, 2048), F32), pltpu.VMEM((384, 2048), F32), vm(4, 4, 384, 128),
            vm(64, 128, 128), vm(2, 4, 4, 4, 2, 128, 128), vm(4, 3, 4, 4, 2, 128, 128),
            pltpu.VMEM((4, 4, 4, 128, 128), F32), vm(4, 4, 4, 4, 128, 128), vm(4, 3, 4, 4, 128, 128),
            vm(4, 4, 4, 128, 128), vm(4, 3, 4, 128, 128), vm(4, 4, 128, 128), vm(4, 4, 128, 128),
            vm(768, 768), vm(1536, 256), vm(768, 512),
            pltpu.SemaphoreType.DMA((216,)), pltpu.SemaphoreType.DMA((216,)), pltpu.SemaphoreType.DMA((2, 4)),
            pltpu.SemaphoreType.DMA((2,)), pltpu.SemaphoreType.DMA((4, 3)), pltpu.SemaphoreType.DMA((6,))],
        compiler_params=pltpu.CompilerParams(collective_id=1, has_side_effects=True, vmem_limit_bytes=67043328),
        name="collect",
    )(wanted, inv, qp, dop, stat, ent, w_query, w_key, w_value)
    return out[0]


def shards(patches, out_grad, w_query, w_key, w_value, w_out, key_tiles, key_blocks):
    layer, qp, dop, stat, ent, wanted, inv = forward_pass(
        patches[0], out_grad[0], w_query, w_key, w_value, w_out, key_tiles[0].T, key_blocks[0].T)
    total = gather_back(wanted, inv, qp, dop, stat, ent, w_query, w_key, w_value)
    return layer[None], total[None]


def solution(mesh):
    cubes = P("vintage", "tile", None)
    lists = P("vintage", None, None)
    return jax.shard_map(shards, mesh=mesh, in_specs=(cubes, cubes, P(), P(), P(), P(), lists, lists),
                         out_specs=(cubes, cubes), check_vma=False)
```

```python
import jax
import jax.numpy as jnp
from jax import lax
from jax.experimental import pallas as pl
from jax.experimental.pallas import tpu as pltpu
from jax.sharding import PartitionSpec as P

LOG2E = 1.4426950408889634
EPSILON = 1e-06
F32, BF16 = jnp.float32, jnp.bfloat16


def dot(a, b, ca=1, cb=0):
    return lax.dot_general(a, b, (((ca,), (cb,)), ((), ())), preferred_element_type=F32)


SCALE = 0.125 * LOG2E


def attend_rows(q, kv, e):
    rows, n = q.shape[0], kv.shape[0] // 128
    s = dot(q, kv, 1, 1)
    m = s[:, :128]
    for i in range(1, n):
        m = jnp.maximum(m, s[:, i * 128:i * 128 + 128])
    m = jnp.broadcast_to(jnp.max(m, axis=1, keepdims=True), (rows, 128))
    total = jnp.zeros((rows, 128), F32)
    for i in range(n):
        x = jnp.exp2((s[:, i * 128:i * 128 + 128] - m) * SCALE)
        e[:, i * 128:i * 128 + 128] = x
        total = total + x
    inv = jnp.broadcast_to(1.0 / jnp.sum(total, axis=1, keepdims=True), (rows, 128))
    low = jnp.concatenate([(e[:, i * 128:i * 128 + 128] * inv).astype(BF16) for i in range(n)], axis=1)
    return m, inv, dot(low, kv)


MESH = pl.DeviceIdType.MESH
SIDE = 4
ORDERS = ((0, 1, 2), (1, 2, 0), (2, 0, 1))
STRIDE = (16, 4, 1)


def place():
    tile = lax.axis_index("tile")
    return [lax.rem(lax.div(tile, s), SIDE) for s in STRIDE]


def shifted(pos, axis, by):
    moved = list(pos)
    moved[axis] = lax.rem(pos[axis] + by, SIDE)
    return moved


def tile_of(pos):
    return pos[0] * 16 + pos[1] * 4 + pos[2]


def greet(pos, core, wait=True, beside=False):
    barrier = pltpu.get_barrier_semaphore()
    for axis in range(3):
        for by in (1, 3):
            for side in (core, 1 - core) if beside else (core,):
                pl.semaphore_signal(barrier, inc=1, device_id=(side, tile_of(shifted(pos, axis, by))), device_id_type=MESH)
    pl.semaphore_signal(barrier, inc=1, device_id=(1 - core, tile_of(pos)), device_id_type=MESH)
    if wait:
        greet_wait()


def greet_wait(count=7):
    pl.semaphore_wait(pltpu.get_barrier_semaphore(), count)


class Sender:
    def __init__(self, pos, core, send_sem, recv_sem):
        self.pos, self.core, self.send_sem, self.recv_sem = pos, core, send_sem, recv_sem
        self.done = []

    def copy(self, src, dst, sem, axis, by, core=None):
        c = pltpu.make_async_remote_copy(
            src_ref=src, dst_ref=dst, send_sem=self.send_sem.at[sem], recv_sem=self.recv_sem.at[sem],
            device_id=(self.core if core is None else core, tile_of(shifted(self.pos, axis, by))), device_id_type=MESH)
        c.start()
        self.done.append(c)
        return c


def at_axis(ref, dims, index, axis, *rest):
    return ref.at[tuple(index if d == axis else slice(None) for d in dims) + rest]


CUTS = ((48, 48, 32), (48, 32, 48), (32, 48, 48), (48, 48, 32))


def spans(g):
    start = 0
    out = []
    for rows in CUTS[g]:
        out.append((start, rows))
        start += rows
    return out


def offset(g, p):
    return sum(CUTS[i][p] for i in range(g - g % 2, g))


def forward_kernel(tok_ref, go_ref, wq_ref, wk_ref, wv_ref, wo_ref, kt_ref, kb_ref,
                   lay_ref, qp_ref, dop_ref, stat_ref, ent_ref, want_ref, inv_ref, rl_ref,
                   mine0, mine1, mine2, mine3, mine4, mine5, plane0, plane1, plane2, plane3, plane4, plane5, stage, arr0, arr1, arr2, arr3, e, kvb, qv, dov, stv, att, ng, lay,
                   named, ranks, tiles, wtab, itab, stab, want, slot,
                   send_sem, recv_sem, swap_sem, tab_sem, ent_sem, out_sem):
    pos, core = place(), lax.axis_index("vintage")
    me = tile_of(pos)
    planes, arr = ((plane0, plane1), (plane2, plane3), (plane4, plane5)), (arr0, arr1, arr2, arr3)
    dims = [tuple(sorted(o[:2])) for o in ORDERS]
    send = Sender(pos, core, send_sem, recv_sem)
    nb, L = 4, 16
    mine = ((mine0, mine1), (mine2, mine3), (mine4, mine5))
    greet(pos, core, False, True)

    k = dot(tok_ref[...], wk_ref[...]).astype(BF16)
    v = dot(tok_ref[...], wv_ref[...]).astype(BF16)
    for g in range(4):
        both = jnp.concatenate([k[:, g * 64:g * 64 + 64], v[:, g * 64:g * 64 + 64]], axis=1)
        for p in range(3):
            r0, rows = spans(g)[p]
            for b in range(nb):
                mine[p][g // 2][b, offset(g, p):offset(g, p) + rows, :] = both[b * 128 + r0:b * 128 + r0 + rows]

    greet_wait(13)

    def cell(p, h, a1, i1, a2, i2, *rest):
        return planes[p][h].at[tuple(i1 if d == a1 else i2 for d in dims[p]) + rest]

    first, second, third, fourth, swaps = {}, {}, {}, {}, {}
    pieces = [(p, h) for h in range(2) for p in range(3)]
    for p, h in pieces:
        a1, a2, a3 = ORDERS[p]
        here = cell(p, h, a1, pos[a1], a2, pos[a2])
        first[p, h] = [send.copy(mine[p][h], here, (h * 3 + p) * 8 + i, a1, by, 1 - core) for i, by in enumerate((1, 3))]
        c = pltpu.make_async_remote_copy(
            src_ref=mine[p][h], dst_ref=here, send_sem=swap_sem.at[0, h * 3 + p], recv_sem=swap_sem.at[1, h * 3 + p],
            device_id=(1 - core, me), device_id_type=MESH)
        c.start()
        swaps[p, h] = c
    kt, kb = kt_ref[...].T, kb_ref[...].T
    tiles[:, :L] = kt
    lane = lax.broadcasted_iota(jnp.int32, (256, 128), 1)
    tile = jnp.where(lane < 64, lane, lane - 64)
    row = lax.broadcasted_iota(jnp.int32, (256, 128), 0)
    quarter = row - (row // 4) * 4
    block, entry = jnp.zeros((256, 128), jnp.int32), jnp.zeros((256, 128), jnp.int32)
    for l in range(L):
        hit = kt[:, l:l + 1] == tile
        block = jnp.where(hit, kb[:, l:l + 1] + 1, block)
        entry = jnp.where(hit, quarter * L + l + 1, entry)
    lane4 = lax.broadcasted_iota(jnp.int32, (64, 128), 1)
    for source, table in ((block, wtab), (entry, itab)):
        named[...] = source
        one, two = jnp.zeros((64, 128), jnp.int32), jnp.zeros((64, 128), jnp.int32)
        for i in range(4):
            x = named[pl.ds(i, 64, stride=4), :]
            ranks[pl.ds(i, 64, stride=4), :] = jnp.where(one > 0, 1, 0)
            two = jnp.where((one > 0) & (x > 0), x, two)
            one = jnp.where(one > 0, one, x)
        table[...] = jnp.where(lane4 < 64, one, two) - 1
    itab[...] = jnp.maximum(itab[...], 0)
    half = pl.ds(pl.multiple_of(lax.div(me, 2) * 8, 8), 8)
    mine_kt, mine_rank = tiles[half, :], ranks[half, :]
    lane8 = lax.broadcasted_iota(jnp.int32, (8, 128), 1)
    found = jnp.zeros((8, 128), jnp.int32)
    for l in range(L):
        at = jnp.sum(jnp.where((mine_kt[:, l:l + 1] == lane8) & (lane8 < 64), lane8 * 2 + mine_rank, 0), axis=1, keepdims=True)
        found = jnp.where(lane8 == l, at, found)
    stab[...] = found
    tables = [pltpu.make_async_copy(wtab, want, tab_sem.at[0]), pltpu.make_async_copy(stab, slot, tab_sem.at[1]),
              pltpu.make_async_copy(wtab, want_ref, tab_sem.at[2]), pltpu.make_async_copy(itab, inv_ref, tab_sem.at[3])]
    for c in tables:
        c.start()

    for p, h in pieces:
        a1, a2, a3 = ORDERS[p]
        second[p, h] = []
        for i, by in enumerate((1, 3)):
            first[p, h][i].wait_recv()
            part = cell(p, h, a1, lax.rem(pos[a1] + SIDE - by, SIDE), a2, pos[a2], pl.ds(2 * i, 2))
            second[p, h].append(send.copy(part, part, (h * 3 + p) * 8 + 2 + i, a1, by))
    for p, h in pieces:
        a1, a2, a3 = ORDERS[p]
        for c in second[p, h]:
            c.wait_recv()
        swaps[p, h].wait()
        here = planes[p][h].at[tuple(pos[a2] if d == a2 else slice(None) for d in dims[p])]
        third[p, h] = [send.copy(here, here, (h * 3 + p) * 8 + 4 + i, a2, by) for i, by in enumerate((1, 3))]
    zero = jnp.zeros((128, 64), BF16)
    q = dot(tok_ref[...], wq_ref[...]).astype(BF16)
    for b in range(nb):
        for h in range(12):
            x = q[b * 128:b * 128 + 128, (h // 2) * 128:(h // 2) * 128 + 128][:, (h % 2) * 64:(h % 2) * 64 + 64]
            qv[b, h // 3, (h % 3) * 128:(h % 3) * 128 + 128, :] = jnp.concatenate([x, zero], axis=1)
    outs = [pltpu.make_async_copy(qv, qp_ref, out_sem.at[0])]
    outs[0].start()
    ng[...] = dot(go_ref[...], wo_ref[...], 1, 1)
    for p, h in pieces:
        a1, a2, a3 = ORDERS[p]
        fourth[p, h] = []
        for i, by in enumerate((1, 3)):
            third[p, h][i].wait_recv()
            other = lax.rem(pos[a2] + SIDE - by, SIDE)
            part = planes[p][h].at[tuple(other if d == a2 else pl.ds(2 * i, 2) for d in dims[p])]
            fourth[p, h].append(send.copy(part, part, (h * 3 + p) * 8 + 6 + i, a2, by))

    def landing(g, p, source, half=None):
        a3 = ORDERS[p][2]
        r0, rows = spans(g)[p]
        idx = []
        for d in range(3):
            if d == a3:
                idx.append(source)
            elif half is not None and d == dims[p][0]:
                idx.append(pl.ds(2 * half, 2))
            else:
                idx.append(slice(None))
        return arr[g].at[tuple(idx) + (slice(None), pl.ds(r0, rows), slice(None))]

    def pick(g, p, k, by):
        a3 = ORDERS[p][2]
        r0, rows = spans(g)[p]
        dest = tile_of(shifted(pos, a3, by))

        def one(j, _):
            hi, lo = lax.div(j, SIDE), lax.rem(j, SIDE)
            source = pos[a3] * STRIDE[a3] + hi * STRIDE[dims[p][0]] + lo * STRIDE[dims[p][1]]
            where = [None] * 3
            where[a3], where[dims[p][0]], where[dims[p][1]] = pos[a3], hi, lo
            for s in range(2):
                blk = jnp.maximum(want[dest, s * 64 + source], 0)
                val = planes[p][g // 2][hi, lo, blk, pl.ds(offset(g, p), rows), :]
                if k < 3:
                    stage[k, hi, lo, s, pl.ds(g * 128 + r0, rows), :] = val
                else:
                    arr[g][tuple(where) + (s, pl.ds(r0, rows), slice(None))] = val
            return 0
        lax.fori_loop(0, SIDE * SIDE, one, 0)

    rows_of = lambda g, p: (slice(None), pl.ds(g * 128 + spans(g)[p][0], spans(g)[p][1]), slice(None))
    W = slice(None)
    zr, zd, zf = {}, {}, {}

    def z_send(g):
        zr[g], zd[g] = [], []
        for p in range(3):
            a3 = ORDERS[p][2]
            if g % 2 == 0:
                for c in fourth[p, g // 2]:
                    c.wait_recv()
            pick(g, p, 2, 2)
            for i, by in enumerate((1, 3)):
                zr[g].append(send.copy(stage.at[(2, pl.ds(2 * i, 2), W) + rows_of(g, p)], rl_ref.at[(i, W, W) + rows_of(g, p)],
                                       48 + (g * 3 + p) * 6 + i, a3, by))
        for p in range(3):
            a3 = ORDERS[p][2]
            for i, by in enumerate((1, 3)):
                pick(g, p, i, by)
                zd[g].append(send.copy(stage.at[(i, W, W) + rows_of(g, p)], landing(g, p, pos[a3]),
                                       48 + (g * 3 + p) * 6 + 2 + i, a3, by))

    def z_own(g):
        for p in range(3):
            pick(g, p, 3, 0)

    def z_relay(g):
        zf[g] = []
        for p in range(3):
            a3 = ORDERS[p][2]
            for i, by in enumerate((1, 3)):
                zr[g][p * 2 + i].wait_recv()
                zf[g].append(send.copy(rl_ref.at[(i, W, W) + rows_of(g, p)], landing(g, p, lax.rem(pos[a3] + SIDE - by, SIDE), i),
                                       48 + (g * 3 + p) * 6 + 4 + i, a3, by))

    def entries(g, b, cur):
        return pltpu.make_async_copy(kvb.at[cur], ent_ref.at[g, pl.ds(b * L, L)], ent_sem.at[cur])

    base = lax.rem(me, 2) * 4

    def forward(g):
        for c in zd[g] + zf[g]:
            c.wait_recv()

        def one(b, _):
            cur = lax.rem(b, 2)
            if g == 0:
                @pl.when(b >= 2)
                def _():
                    entries(g, b, cur).wait()
            else:
                entries(g, b, cur).wait()
            for l in range(L):
                at = slot[base + b, l]
                pair, s = lax.div(at, 2), lax.rem(at, 2)
                x, yz = lax.div(pair, 16), lax.rem(pair, 16)
                kvb[cur, l] = arr[g][x, lax.div(yz, 4), lax.rem(yz, 4), s]
            m, inv, out = attend_rows(qv[b, g], kvb[cur].reshape(L * 128, 128), e)
            entries(g, b, cur).start()
            stv[b, g] = jnp.concatenate([m[:, :64], inv[:, 64:]], axis=1)
            att[b, g] = out.astype(BF16)
            return 0
        lax.fori_loop(0, nb, one, 0)
        c = pltpu.make_async_copy(stv.at[:, g], stat_ref.at[:, g], out_sem.at[1 + g])
        c.start()
        outs.append(c)

    tables[0].wait()
    tables[1].wait()
    z_send(0)
    z_send(1)
    z_own(0)
    z_relay(0)
    z_send(2)
    z_own(1)
    z_relay(1)
    z_send(3)
    forward(0)
    z_own(2)
    z_relay(2)
    forward(1)
    z_own(3)
    z_relay(3)
    forward(2)
    forward(3)

    for b in range(nb):
        rows = slice(b * 128, b * 128 + 128)
        a = []
        for j in range(6):
            a.append(jnp.concatenate([att[b, h // 3, (h % 3) * 128:(h % 3) * 128 + 128, :][:, 64:] for h in (2 * j, 2 * j + 1)], axis=1))
        a = jnp.concatenate(a, axis=1).astype(F32)
        root = jnp.sqrt(jnp.sum(a * a, axis=1, keepdims=True) * (1.0 / 768) + EPSILON)
        normed = a / root
        lay[rows, :] = dot(normed.astype(BF16), wo_ref[...]).astype(BF16)
        n = ng[rows, :]
        a = ((n - normed * (jnp.sum(n * normed, axis=1, keepdims=True) * (1.0 / 768))) / root).astype(BF16)
        for h in range(12):
            x = a[:, (h // 2) * 128:(h // 2) * 128 + 128][:, (h % 2) * 64:(h % 2) * 64 + 64]
            dov[b, h // 3, (h % 3) * 128:(h % 3) * 128 + 128, :] = jnp.concatenate([zero, x], axis=1)
    for i, (src, dst) in enumerate(((dov, dop_ref), (lay, lay_ref))):
        c = pltpu.make_async_copy(src, dst, out_sem.at[5 + i])
        c.start()
        outs.append(c)
    for b in (nb - 2, nb - 1):
        entries(3, b, b % 2).wait()
    for c in outs + tables[2:]:
        c.wait()
    for c in send.done:
        c.wait_send()


def forward_pass(tokens, grads, w_query, w_key, w_value, w_out, named, blocks):
    V, A = pl.BlockSpec(memory_space=pltpu.VMEM), pl.BlockSpec(memory_space=pl.ANY)
    bf = lambda *shape: jax.ShapeDtypeStruct(shape, BF16)
    i32 = lambda *shape: jax.ShapeDtypeStruct(shape, jnp.int32)
    vm = lambda *shape: pltpu.VMEM(shape, BF16)
    vi = lambda *shape: pltpu.VMEM(shape, jnp.int32)
    dma = lambda *shape: pltpu.SemaphoreType.DMA(shape)
    out = pl.pallas_call(
        forward_kernel,
        in_specs=[V] * 8,
        out_specs=[A] * 8,
        out_shape=[bf(512, 768), bf(4, 4, 384, 128), bf(4, 4, 384, 128), jax.ShapeDtypeStruct((4, 4, 384, 128), F32),
                   bf(4, 64, 128, 128), i32(64, 128), i32(64, 128), bf(2, 2, 4, 2, 512, 128)],
        scratch_shapes=[vm(4, CUTS[2 * h][p] + CUTS[2 * h + 1][p], 128) for p in range(3) for h in range(2)] + [
            vm(4, 4, 4, CUTS[2 * h][p] + CUTS[2 * h + 1][p], 128) for p in range(3) for h in range(2)] + [
            vm(3, 4, 4, 2, 512, 128)] + [vm(4, 4, 4, 2, 128, 128)] * 4 + [pltpu.VMEM((384, 2048), F32), vm(2, 16, 128, 128),
            vm(4, 4, 384, 128), vm(4, 4, 384, 128), pltpu.VMEM((4, 4, 384, 128), F32), vm(4, 4, 384, 128),
            pltpu.VMEM((512, 768), F32), vm(512, 768),
            vi(256, 128), vi(256, 128), vi(256, 128), vi(64, 128), vi(64, 128), vi(8, 128),
            pltpu.SMEM((64, 128), jnp.int32), pltpu.SMEM((8, 128), jnp.int32),
            dma(120), dma(120), dma(2, 6), dma(4), dma(2), dma(7)],
        compiler_params=pltpu.CompilerParams(collective_id=0, has_side_effects=True, vmem_limit_bytes=67043328),
        name="forward",
    )(tokens, grads, w_query, w_key, w_value, w_out, named, blocks)
    return out[:7]


def return_kernel(wanted, inv, qp_ref, dop_ref, stat_ref, ent_ref, wq_ref, wk_ref, wv_ref, out_ref, rl_ref,
                  kvb, qv, dov, stv, p, t, dqs, parts, stage, rz, sums, gs, yl, ys, hs, xl, xs, total, got, wq, flat, wkv,
                  send_sem, recv_sem, swap_sem, kv_sem, in_sem, w_sem):
    pos, core = place(), lax.axis_index("vintage")
    dims = [tuple(sorted(o[:2])) for o in ORDERS]
    send = Sender(pos, core, send_sem, recv_sem)
    nb = qv.shape[0]
    me = tile_of(pos)
    L = kvb.shape[1]
    greet(pos, core, False)

    def turn(axis, by):
        return lax.rem(pos[axis] + by, SIDE)

    def key(g, p, i):
        return (g * 3 + p) * 18 + i

    def load(g, b, slot):
        return pltpu.make_async_copy(ent_ref.at[g, pl.ds(b * L, L)], kvb.at[slot], kv_sem.at[slot])

    load(0, 0, 0).start()
    rows_in = [[pltpu.make_async_copy(src.at[:, g], dst.at[:, g % dst.shape[1]], in_sem.at[g, i])
                for i, (src, dst) in enumerate(((qp_ref, qv), (dop_ref, dov), (stat_ref, stv)))] for g in range(4)]
    for c in rows_in[0]:
        c.start()
    weights = [pltpu.make_async_copy(src, dst, w_sem.at[i]) for i, (src, dst) in enumerate(((wq_ref, wq), (wk_ref, flat.at[0:768]), (wv_ref, flat.at[768:1536])))]
    for c in weights:
        c.start()

    def backward(g):
        for c in rows_in[g]:
            c.wait()
        if g < 3:
            for c in rows_in[g + 1]:
                c.start()

        def one(b, _):
            cur = lax.rem(b, 2)
            load(g, b, cur).wait()

            @pl.when(b + 1 < nb)
            def _():
                load(g, b + 1, 1 - cur).start()

            if g < 3:
                @pl.when(b + 1 == nb)
                def _():
                    load(g + 1, 0, 0).start()

            kv = kvb[cur].reshape(L * 128, 128)
            q, do = qv[b, g % 2], dov[b, g % 2]
            m = jnp.broadcast_to(stv[b, g % 2, :, 0:1], (384, 128))
            nrm = jnp.broadcast_to(stv[b, g % 2, :, 64:65], (384, 128))
            s = dot(q, kv, 1, 1)
            dp = dot((do.astype(F32) * 0.125).astype(BF16), kv, 1, 1)
            rd = jnp.zeros((384, 128), F32)
            for i in range(L):
                cols = slice(i * 128, i * 128 + 128)
                pr = jnp.exp2((s[:, cols] - m) * SCALE) * nrm
                x = pr * dp[:, cols]
                p[:, cols] = pr
                t[:, cols] = x
                rd = rd + x
            rd = jnp.broadcast_to(jnp.sum(rd, axis=1, keepdims=True), (384, 128))
            ds_, low = [], []
            for i in range(L):
                cols = slice(i * 128, i * 128 + 128)
                pr = p[:, cols]
                ds_.append((t[:, cols] - pr * rd).astype(BF16))
                low.append(pr.astype(BF16))
            ds_, low = jnp.concatenate(ds_, axis=1), jnp.concatenate(low, axis=1)
            dqs[b, g] = dot(ds_, kv).astype(BF16)
            part = dot(jnp.concatenate([ds_, low], axis=0), jnp.concatenate([q, do], axis=0), 0, 0)
            parts[pl.ds(b * L, L)] = part.astype(BF16).reshape(L, 128, 128)
            return 0
        lax.fori_loop(0, nb, one, 0)

    zr, zd, zf, yr, yd, xr, xd = [{} for _ in range(7)]

    def slots_of(g, p, level, half=None):
        a3 = ORDERS[p][2]
        r0, rows = spans(g)[p]
        idx = []
        for d in range(3):
            if d == a3:
                idx.append(level)
            elif half is not None and d == dims[p][0]:
                idx.append(pl.ds(2 * half, 2))
            else:
                idx.append(slice(None))
        return stage.at[(g % 2,) + tuple(idx) + (slice(None), pl.ds(r0, rows), slice(None))]

    def at_rows(ref, g, p, lead):
        r0, rows = spans(g)[p]
        return ref.at[(g,) + tuple(lead) + (pl.ds(r0, rows), slice(None))]

    W = slice(None)

    def z_send(g):
        if g >= 2:
            for c in zr[g - 2] + zd[g - 2]:
                c.wait_send()

        def place_part(j, _):
            x, y, z = lax.div(j, 16), lax.rem(lax.div(j, 4), 4), lax.rem(j, 4)
            for s in range(2):
                stage[g % 2, x, y, z, s] = parts[inv[me, s * 64 + j]]
            return 0
        lax.fori_loop(0, 64, place_part, 0)
        if g == 0:
            greet_wait()
        zr[g], zd[g] = [], []
        for p in range(3):
            a3 = ORDERS[p][2]
            for i, by in enumerate((1, 3)):
                zr[g].append(send.copy(slots_of(g, p, turn(a3, 2), i), at_rows(rl_ref, g, p, (i, W, W, W)), key(g, p, i), a3, by))
        for p in range(3):
            a3 = ORDERS[p][2]
            for i, by in enumerate((1, 3)):
                zd[g].append(send.copy(slots_of(g, p, turn(a3, by)), at_rows(rz, g, p, (i, W, W, W)), key(g, p, 2 + i), a3, by))

    def z_relay(g):
        zf[g] = []
        for p in range(3):
            a3 = ORDERS[p][2]
            for i, by in enumerate((1, 3)):
                zr[g][p * 2 + i].wait_recv()
                zf[g].append(send.copy(at_rows(rl_ref, g, p, (i, W, W, W)), at_rows(rz, g, p, (2, pl.ds(2 * i, 2), W, W)),
                                       key(g, p, 4 + i), a3, by))

    def add_up(g, p, k, by, first, last):
        a3 = ORDERS[p][2]
        r0, rows = spans(g)[p]
        source = tile_of(shifted(pos, a3, by))

        def one(j, _):
            hi, lo = lax.div(j, SIDE), lax.rem(j, SIDE)
            holder = pos[a3] * STRIDE[a3] + hi * STRIDE[dims[p][0]] + lo * STRIDE[dims[p][1]]
            where = [None] * 3
            where[a3], where[dims[p][0]], where[dims[p][1]] = pos[a3], hi, lo
            vals = []
            for s in range(2):
                at = (k, hi, lo, s) if k < 3 else tuple(where) + (s,)
                ref, lead = (rz, g) if k < 3 else (stage, g % 2)
                vals.append(ref[(lead,) + at + (pl.ds(r0, rows), slice(None))].astype(F32))
            want = [wanted[source, s * 64 + holder] for s in range(2)]
            for b in range(4):
                x = jnp.where(want[0] == b, vals[0], 0.0) + jnp.where(want[1] == b, vals[1], 0.0)
                if not first:
                    x = x + sums[hi, lo, b, pl.ds(r0, rows), :]
                if last:
                    gs[g, hi, lo, b, pl.ds(r0, rows), :] = x.astype(BF16)
                else:
                    sums[hi, lo, b, pl.ds(r0, rows), :] = x
            return 0
        lax.fori_loop(0, SIDE * SIDE, one, 0)

    def z_sum(g):
        for p in range(3):
            add_up(g, p, 3, 0, True, False)
        for i, by in enumerate((3, 1)):
            for p in range(3):
                zd[g][p * 2 + i].wait_recv()
                add_up(g, p, i, by, False, False)

    def lines(g, p, axis, index, half=None):
        idx = []
        for d in dims[p]:
            if d == axis:
                idx.append(index)
            else:
                idx.append(slice(None) if half is None else pl.ds(2 * half, 2))
        return at_rows(gs, g, p, tuple(idx) + (W,))

    def y_send(g):
        yr[g], yd[g] = [], []
        for p in range(3):
            a2 = ORDERS[p][1]
            for c in zf[g][p * 2:p * 2 + 2]:
                c.wait_recv()
            add_up(g, p, 2, 2, False, True)
            for i, by in enumerate((1, 3)):
                yr[g].append(send.copy(lines(g, p, a2, turn(a2, 2), i), at_rows(yl, g, p, (i, W, W)), key(g, p, 6 + i), a2, by))

    def y_relay(g):
        for p in range(3):
            a1, a2, a3 = ORDERS[p]
            r0, rows = spans(g)[p]
            at = (pl.ds(r0, rows), slice(None))
            for i, by in enumerate((1, 3)):
                yr[g][p * 2 + i].wait_recv()

                def join(j, _, p=p, a1=a1, a2=a2, i=i, by=by, at=at):
                    i1, b = lax.div(j, 4), lax.rem(j, 4)
                    here = (g,) + tuple(2 * i + i1 if d == a1 else turn(a2, by) for d in dims[p]) + (b,) + at
                    gs[here] = (gs[here].astype(F32) + yl[(g, i, i1, b) + at].astype(F32)).astype(BF16)
                    return 0
                lax.fori_loop(0, 8, join, 0)
                yd[g].append(send.copy(lines(g, p, a2, turn(a2, by)), at_rows(ys, g, p, (i, W, W)), key(g, p, 8 + i), a2, by))

    def x_send(g):
        xr[g], xd[g] = [], []
        for p in range(3):
            a1, a2, a3 = ORDERS[p]
            r0, rows = spans(g)[p]
            at = (pl.ds(r0, rows), slice(None))
            for c in yd[g][p * 2:p * 2 + 2]:
                c.wait_recv()

            def row(j, _, p=p, a1=a1, a2=a2, at=at):
                i1, b = lax.div(j, 4), lax.rem(j, 4)
                mine = gs[(g,) + tuple(i1 if d == a1 else pos[a2] for d in dims[p]) + (b,) + at].astype(F32)
                for k in range(2):
                    mine = mine + ys[(g, k, i1, b) + at].astype(F32)
                hs[(g, i1, b) + at] = mine.astype(BF16)
                return 0
            lax.fori_loop(0, 16, row, 0)
        for p in range(3):
            a1 = ORDERS[p][0]
            for i, by in enumerate((1, 3)):
                xr[g].append(send.copy(at_rows(hs, g, p, (turn(a1, 2), pl.ds(2 * i, 2))), at_rows(xl, g, p, (i, W)), key(g, p, 12 + i), a1, by))

    def x_relay(g):
        for p in range(3):
            a1 = ORDERS[p][0]
            r0, rows = spans(g)[p]
            at = (pl.ds(r0, rows), slice(None))
            for i, by in enumerate((1, 3)):
                xr[g][p * 2 + i].wait_recv()
                for b in range(2):
                    here = (g, turn(a1, by), 2 * i + b) + at
                    hs[here] = (hs[here].astype(F32) + xl[(g, i, b) + at].astype(F32)).astype(BF16)
                xd[g].append(send.copy(at_rows(hs, g, p, (turn(a1, by), W)), at_rows(xs, g, p, (i, W)), key(g, p, 14 + i), a1, by))

    swaps = []

    def finish(g):
        for p in range(3):
            a1 = ORDERS[p][0]
            r0, rows = spans(g)[p]
            at = (pl.ds(r0, rows), slice(None))
            for c in xd[g][p * 2:p * 2 + 2]:
                c.wait_recv()
            for b in range(4):
                mine = hs[(g, pos[a1], b) + at].astype(F32)
                for k in range(2):
                    mine = mine + xs[(g, k, b) + at].astype(F32)
                total[(g, b) + at] = mine.astype(BF16)
        c = pltpu.make_async_remote_copy(
            src_ref=total.at[g], dst_ref=got.at[g], send_sem=swap_sem.at[0, g], recv_sem=swap_sem.at[1, g],
            device_id=(1 - core, tile_of(pos)), device_id_type=MESH)
        c.start()
        swaps.append(c)

    def sums_at(b):
        return slice(b % 3 * 128, b % 3 * 128 + 128), slice(b // 3 * 768, b // 3 * 768 + 768)

    def query_term(b):
        heads = [dqs[b, h // 3, (h % 3) * 128:(h % 3) * 128 + 128, :][:, :64] for h in range(12)]
        p[sums_at(b)] = dot(jnp.concatenate(heads, axis=1), wq[...], 1, 1)

    def key_term(half):
        for g in (2 * half, 2 * half + 1):
            swaps[g].wait()
        for b in range(nb):
            both = jnp.concatenate([got[2 * half, b], got[2 * half + 1, b]], axis=1)
            x = p[sums_at(b)] + dot(both, wkv[:, half * 256:half * 256 + 256], 1, 1)
            if half == 0:
                p[sums_at(b)] = x
            else:
                for i in range(3):
                    flat[i * 512 + b * 128:i * 512 + b * 128 + 128, :] = x[:, i * 256:i * 256 + 256].astype(BF16)

    backward(0)
    z_send(0)
    backward(1)
    z_send(1)
    z_relay(0)
    z_sum(0)
    backward(2)
    z_send(2)
    z_relay(1)
    y_send(0)
    z_sum(1)
    backward(3)
    z_send(3)
    z_relay(2)
    y_send(1)
    y_relay(0)
    z_sum(2)
    z_relay(3)
    y_send(2)
    y_relay(1)
    x_send(0)
    z_sum(3)
    y_send(3)
    y_relay(2)
    x_send(1)
    x_relay(0)
    for c in weights:
        c.wait()
    for g in range(4):
        wkv[:, g * 128:g * 128 + 128] = jnp.concatenate([flat[0:768, g * 64:g * 64 + 64], flat[768:1536, g * 64:g * 64 + 64]], axis=1)
    query_term(0)
    query_term(1)
    y_relay(3)
    x_send(2)
    x_relay(1)
    finish(0)
    query_term(2)
    query_term(3)
    x_send(3)
    x_relay(2)
    finish(1)
    x_relay(3)
    finish(2)
    key_term(0)
    finish(3)
    key_term(1)
    results = [pltpu.make_async_copy(flat.at[i * 512:i * 512 + 512], out_ref.at[:, i * 256:i * 256 + 256], w_sem.at[3 + i]) for i in range(3)]
    for c in results:
        c.start()
    for c in results:
        c.wait()
    for g in range(4):
        late = zr[g] + zd[g] if g >= 2 else []
        for c in late + zf[g] + yr[g] + yd[g] + xr[g] + xd[g]:
            c.wait_send()


def gather_back(wanted, inv, qp, dop, stat, ent, w_query, w_key, w_value):
    V, A = pl.BlockSpec(memory_space=pltpu.VMEM), pl.BlockSpec(memory_space=pl.ANY)
    S = pl.BlockSpec(memory_space=pltpu.SMEM)
    bf = lambda *shape: jax.ShapeDtypeStruct(shape, BF16)
    vm = lambda *shape: pltpu.VMEM(shape, BF16)
    out = pl.pallas_call(
        return_kernel,
        in_specs=[S, S] + [A] * 7,
        out_specs=[A] * 2,
        out_shape=[bf(512, 768), bf(4, 2, 2, 4, 2, 128, 128)],
        scratch_shapes=[
            vm(2, 16, 128, 128), vm(4, 2, 384, 128), vm(4, 2, 384, 128), pltpu.VMEM((4, 2, 384, 128), F32),
            pltpu.VMEM((384, 2048), F32), pltpu.VMEM((384, 2048), F32), vm(4, 4, 384, 128),
            vm(64, 128, 128), vm(2, 4, 4, 4, 2, 128, 128), vm(4, 3, 4, 4, 2, 128, 128),
            pltpu.VMEM((4, 4, 4, 128, 128), F32), vm(4, 4, 4, 4, 128, 128), vm(4, 2, 2, 4, 128, 128), vm(4, 2, 4, 4, 128, 128),
            vm(4, 4, 4, 128, 128), vm(4, 2, 2, 128, 128), vm(4, 2, 4, 128, 128), vm(4, 4, 128, 128), vm(4, 4, 128, 128),
            vm(768, 768), vm(1536, 256), vm(768, 512),
            pltpu.SemaphoreType.DMA((216,)), pltpu.SemaphoreType.DMA((216,)), pltpu.SemaphoreType.DMA((2, 4)),
            pltpu.SemaphoreType.DMA((2,)), pltpu.SemaphoreType.DMA((4, 3)), pltpu.SemaphoreType.DMA((6,))],
        compiler_params=pltpu.CompilerParams(collective_id=1, has_side_effects=True, vmem_limit_bytes=67043328),
        name="collect",
    )(wanted, inv, qp, dop, stat, ent, w_query, w_key, w_value)
    return out[0]


def shards(patches, out_grad, w_query, w_key, w_value, w_out, key_tiles, key_blocks):
    layer, qp, dop, stat, ent, wanted, inv = forward_pass(
        patches[0], out_grad[0], w_query, w_key, w_value, w_out, key_tiles[0].T, key_blocks[0].T)
    total = gather_back(wanted, inv, qp, dop, stat, ent, w_query, w_key, w_value)
    return layer[None], total[None]


def solution(mesh):
    cubes = P("vintage", "tile", None)
    lists = P("vintage", None, None)
    return jax.shard_map(shards, mesh=mesh, in_specs=(cubes, cubes, P(), P(), P(), P(), lists, lists),
                         out_specs=(cubes, cubes), check_vma=False)
```

```python
import jax
import jax.numpy as jnp
from jax import lax
from jax.experimental import pallas as pl
from jax.experimental.pallas import tpu as pltpu
from jax.sharding import PartitionSpec as P

LOG2E = 1.4426950408889634
EPSILON = 1e-06
F32, BF16 = jnp.float32, jnp.bfloat16


def dot(a, b, ca=1, cb=0):
    return lax.dot_general(a, b, (((ca,), (cb,)), ((), ())), preferred_element_type=F32)


SCALE = 0.125 * LOG2E


def attend_rows(q, kv, e):
    rows, n = q.shape[0], kv.shape[0] // 128
    s = dot(q, kv, 1, 1)
    m = s[:, :128]
    for i in range(1, n):
        m = jnp.maximum(m, s[:, i * 128:i * 128 + 128])
    m = jnp.broadcast_to(jnp.max(m, axis=1, keepdims=True), (rows, 128))
    total = jnp.zeros((rows, 128), F32)
    for i in range(n):
        x = jnp.exp2((s[:, i * 128:i * 128 + 128] - m) * SCALE)
        e[:, i * 128:i * 128 + 128] = x
        total = total + x
    inv = jnp.broadcast_to(1.0 / jnp.sum(total, axis=1, keepdims=True), (rows, 128))
    low = jnp.concatenate([(e[:, i * 128:i * 128 + 128] * inv).astype(BF16) for i in range(n)], axis=1)
    return m, inv, dot(low, kv)


MESH = pl.DeviceIdType.MESH
SIDE = 4
ORDERS = ((0, 1, 2), (1, 2, 0), (2, 0, 1))
STRIDE = (16, 4, 1)


def place():
    tile = lax.axis_index("tile")
    return [lax.rem(lax.div(tile, s), SIDE) for s in STRIDE]


def shifted(pos, axis, by):
    moved = list(pos)
    moved[axis] = lax.rem(pos[axis] + by, SIDE)
    return moved


def tile_of(pos):
    return pos[0] * 16 + pos[1] * 4 + pos[2]


def greet(pos, core, wait=True, beside=False):
    barrier = pltpu.get_barrier_semaphore()
    for axis in range(3):
        for by in (1, 3):
            for side in (core, 1 - core) if beside else (core,):
                pl.semaphore_signal(barrier, inc=1, device_id=(side, tile_of(shifted(pos, axis, by))), device_id_type=MESH)
    pl.semaphore_signal(barrier, inc=1, device_id=(1 - core, tile_of(pos)), device_id_type=MESH)
    if wait:
        greet_wait()


def greet_wait(count=7):
    pl.semaphore_wait(pltpu.get_barrier_semaphore(), count)


class Sender:
    def __init__(self, pos, core, send_sem, recv_sem):
        self.pos, self.core, self.send_sem, self.recv_sem = pos, core, send_sem, recv_sem
        self.done = []

    def copy(self, src, dst, sem, axis, by, core=None):
        c = pltpu.make_async_remote_copy(
            src_ref=src, dst_ref=dst, send_sem=self.send_sem.at[sem], recv_sem=self.recv_sem.at[sem],
            device_id=(self.core if core is None else core, tile_of(shifted(self.pos, axis, by))), device_id_type=MESH)
        c.start()
        self.done.append(c)
        return c


def at_axis(ref, dims, index, axis, *rest):
    return ref.at[tuple(index if d == axis else slice(None) for d in dims) + rest]


CUTS = ((48, 48, 32), (48, 32, 48), (32, 48, 48), (48, 48, 32))


def spans(g):
    start = 0
    out = []
    for rows in CUTS[g]:
        out.append((start, rows))
        start += rows
    return out


def offset(g, p):
    return sum(CUTS[i][p] for i in range(g - g % 2, g))


def forward_kernel(tok_ref, go_ref, wq_ref, wk_ref, wv_ref, wo_ref, kt_ref, kb_ref,
                   lay_ref, qp_ref, dop_ref, stat_ref, ent_ref, want_ref, inv_ref, rl_ref,
                   mine0, mine1, mine2, mine3, mine4, mine5, plane0, plane1, plane2, plane3, plane4, plane5, stage, arr0, arr1, arr2, arr3, e, kvb, qv, dov, stv, att, ng, lay,
                   named, ranks, tiles, wtab, itab, stab, want, slot,
                   send_sem, recv_sem, swap_sem, tab_sem, ent_sem, out_sem):
    pos, core = place(), lax.axis_index("vintage")
    me = tile_of(pos)
    planes, arr = ((plane0, plane1), (plane2, plane3), (plane4, plane5)), (arr0, arr1, arr2, arr3)
    dims = [tuple(sorted(o[:2])) for o in ORDERS]
    send = Sender(pos, core, send_sem, recv_sem)
    nb, L = 4, 16
    mine = ((mine0, mine1), (mine2, mine3), (mine4, mine5))
    greet(pos, core, False, True)

    k = dot(tok_ref[...], wk_ref[...]).astype(BF16)
    v = dot(tok_ref[...], wv_ref[...]).astype(BF16)
    for g in range(4):
        both = jnp.concatenate([k[:, g * 64:g * 64 + 64], v[:, g * 64:g * 64 + 64]], axis=1)
        for p in range(3):
            r0, rows = spans(g)[p]
            for b in range(nb):
                mine[p][g // 2][b, offset(g, p):offset(g, p) + rows, :] = both[b * 128 + r0:b * 128 + r0 + rows]

    greet_wait(13)

    def cell(p, h, a1, i1, a2, i2, *rest):
        return planes[p][h].at[tuple(i1 if d == a1 else i2 for d in dims[p]) + rest]

    first, second, third, fourth, swaps = {}, {}, {}, {}, {}
    pieces = [(p, h) for h in range(2) for p in range(3)]
    for p, h in pieces:
        a1, a2, a3 = ORDERS[p]
        here = cell(p, h, a1, pos[a1], a2, pos[a2])
        first[p, h] = [send.copy(mine[p][h], here, (h * 3 + p) * 8 + i, a1, by, 1 - core) for i, by in enumerate((1, 3))]
        c = pltpu.make_async_remote_copy(
            src_ref=mine[p][h], dst_ref=here, send_sem=swap_sem.at[0, h * 3 + p], recv_sem=swap_sem.at[1, h * 3 + p],
            device_id=(1 - core, me), device_id_type=MESH)
        c.start()
        swaps[p, h] = c
    kt, kb = kt_ref[...].T, kb_ref[...].T
    tiles[:, :L] = kt
    lane = lax.broadcasted_iota(jnp.int32, (256, 128), 1)
    tile = jnp.where(lane < 64, lane, lane - 64)
    row = lax.broadcasted_iota(jnp.int32, (256, 128), 0)
    quarter = row - (row // 4) * 4
    block, entry = jnp.zeros((256, 128), jnp.int32), jnp.zeros((256, 128), jnp.int32)
    for l in range(L):
        hit = kt[:, l:l + 1] == tile
        block = jnp.where(hit, kb[:, l:l + 1] + 1, block)
        entry = jnp.where(hit, quarter * L + l + 1, entry)
    lane4 = lax.broadcasted_iota(jnp.int32, (64, 128), 1)
    for source, table in ((block, wtab), (entry, itab)):
        named[...] = source
        one, two = jnp.zeros((64, 128), jnp.int32), jnp.zeros((64, 128), jnp.int32)
        for i in range(4):
            x = named[pl.ds(i, 64, stride=4), :]
            ranks[pl.ds(i, 64, stride=4), :] = jnp.where(one > 0, 1, 0)
            two = jnp.where((one > 0) & (x > 0), x, two)
            one = jnp.where(one > 0, one, x)
        table[...] = jnp.where(lane4 < 64, one, two) - 1
    itab[...] = jnp.maximum(itab[...], 0)
    half = pl.ds(pl.multiple_of(lax.div(me, 2) * 8, 8), 8)
    mine_kt, mine_rank = tiles[half, :], ranks[half, :]
    lane8 = lax.broadcasted_iota(jnp.int32, (8, 128), 1)
    found = jnp.zeros((8, 128), jnp.int32)
    for l in range(L):
        at = jnp.sum(jnp.where((mine_kt[:, l:l + 1] == lane8) & (lane8 < 64), lane8 * 2 + mine_rank, 0), axis=1, keepdims=True)
        found = jnp.where(lane8 == l, at, found)
    stab[...] = found
    tables = [pltpu.make_async_copy(wtab, want, tab_sem.at[0]), pltpu.make_async_copy(stab, slot, tab_sem.at[1]),
              pltpu.make_async_copy(wtab, want_ref, tab_sem.at[2]), pltpu.make_async_copy(itab, inv_ref, tab_sem.at[3])]
    for c in tables:
        c.start()

    for p, h in pieces:
        a1, a2, a3 = ORDERS[p]
        second[p, h] = []
        for i, by in enumerate((1, 3)):
            first[p, h][i].wait_recv()
            part = cell(p, h, a1, lax.rem(pos[a1] + SIDE - by, SIDE), a2, pos[a2], pl.ds(2 * i, 2))
            second[p, h].append(send.copy(part, part, (h * 3 + p) * 8 + 2 + i, a1, by))
    for p, h in pieces:
        a1, a2, a3 = ORDERS[p]
        for c in second[p, h]:
            c.wait_recv()
        swaps[p, h].wait()
        here = planes[p][h].at[tuple(pos[a2] if d == a2 else slice(None) for d in dims[p])]
        third[p, h] = [send.copy(here, here, (h * 3 + p) * 8 + 4 + i, a2, by) for i, by in enumerate((1, 3))]
    zero = jnp.zeros((128, 64), BF16)
    q = dot(tok_ref[...], wq_ref[...]).astype(BF16)
    for b in range(nb):
        for h in range(12):
            x = q[b * 128:b * 128 + 128, (h // 2) * 128:(h // 2) * 128 + 128][:, (h % 2) * 64:(h % 2) * 64 + 64]
            qv[b, h // 3, (h % 3) * 128:(h % 3) * 128 + 128, :] = jnp.concatenate([x, zero], axis=1)
    outs = [pltpu.make_async_copy(qv, qp_ref, out_sem.at[0])]
    outs[0].start()
    ng[...] = dot(go_ref[...], wo_ref[...], 1, 1)
    for p, h in pieces:
        a1, a2, a3 = ORDERS[p]
        fourth[p, h] = []
        for i, by in enumerate((1, 3)):
            third[p, h][i].wait_recv()
            other = lax.rem(pos[a2] + SIDE - by, SIDE)
            part = planes[p][h].at[tuple(other if d == a2 else pl.ds(2 * i, 2) for d in dims[p])]
            fourth[p, h].append(send.copy(part, part, (h * 3 + p) * 8 + 6 + i, a2, by))

    def landing(g, p, source, half=None):
        a3 = ORDERS[p][2]
        r0, rows = spans(g)[p]
        idx = []
        for d in range(3):
            if d == a3:
                idx.append(source)
            elif half is not None and d == dims[p][0]:
                idx.append(pl.ds(2 * half, 2))
            else:
                idx.append(slice(None))
        return arr[g].at[tuple(idx) + (slice(None), pl.ds(r0, rows), slice(None))]

    def pick(g, p, k, by):
        a3 = ORDERS[p][2]
        r0, rows = spans(g)[p]
        dest = tile_of(shifted(pos, a3, by))

        def one(j, _):
            hi, lo = lax.div(j, SIDE), lax.rem(j, SIDE)
            source = pos[a3] * STRIDE[a3] + hi * STRIDE[dims[p][0]] + lo * STRIDE[dims[p][1]]
            where = [None] * 3
            where[a3], where[dims[p][0]], where[dims[p][1]] = pos[a3], hi, lo
            for s in range(2):
                blk = jnp.maximum(want[dest, s * 64 + source], 0)
                val = planes[p][g // 2][hi, lo, blk, pl.ds(offset(g, p), rows), :]
                if k < 3:
                    stage[k, hi, lo, s, pl.ds(g * 128 + r0, rows), :] = val
                else:
                    arr[g][tuple(where) + (s, pl.ds(r0, rows), slice(None))] = val
            return 0
        lax.fori_loop(0, SIDE * SIDE, one, 0)

    rows_of = lambda g, p: (slice(None), pl.ds(g * 128 + spans(g)[p][0], spans(g)[p][1]), slice(None))
    W = slice(None)
    zr, zd, zf = {}, {}, {}

    def z_send(g):
        zr[g], zd[g] = [], []
        for p in range(3):
            a3 = ORDERS[p][2]
            if g % 2 == 0:
                for c in fourth[p, g // 2]:
                    c.wait_recv()
            pick(g, p, 2, 2)
            for i, by in enumerate((1, 3)):
                zr[g].append(send.copy(stage.at[(2, pl.ds(2 * i, 2), W) + rows_of(g, p)], rl_ref.at[(i, W, W) + rows_of(g, p)],
                                       48 + (g * 3 + p) * 6 + i, a3, by))
        for p in range(3):
            a3 = ORDERS[p][2]
            for i, by in enumerate((1, 3)):
                pick(g, p, i, by)
                zd[g].append(send.copy(stage.at[(i, W, W) + rows_of(g, p)], landing(g, p, pos[a3]),
                                       48 + (g * 3 + p) * 6 + 2 + i, a3, by))

    def z_own(g):
        for p in range(3):
            pick(g, p, 3, 0)

    def z_relay(g):
        zf[g] = []
        for p in range(3):
            a3 = ORDERS[p][2]
            for i, by in enumerate((1, 3)):
                zr[g][p * 2 + i].wait_recv()
                zf[g].append(send.copy(rl_ref.at[(i, W, W) + rows_of(g, p)], landing(g, p, lax.rem(pos[a3] + SIDE - by, SIDE), i),
                                       48 + (g * 3 + p) * 6 + 4 + i, a3, by))

    def entries(g, b, cur):
        return pltpu.make_async_copy(kvb.at[cur], ent_ref.at[g, pl.ds(b * L, L)], ent_sem.at[cur])

    base = lax.rem(me, 2) * 4

    def forward(g):
        for c in zd[g] + zf[g]:
            c.wait_recv()

        def one(b, _):
            cur = lax.rem(b, 2)
            if g == 0:
                @pl.when(b >= 2)
                def _():
                    entries(g, b, cur).wait()
            else:
                entries(g, b, cur).wait()
            for l in range(L):
                at = slot[base + b, l]
                pair, s = lax.div(at, 2), lax.rem(at, 2)
                x, yz = lax.div(pair, 16), lax.rem(pair, 16)
                kvb[cur, l] = arr[g][x, lax.div(yz, 4), lax.rem(yz, 4), s]
            m, inv, out = attend_rows(qv[b, g], kvb[cur].reshape(L * 128, 128), e)
            entries(g, b, cur).start()
            stv[b, g] = jnp.concatenate([m[:, :64], inv[:, 64:]], axis=1)
            att[b, g] = out.astype(BF16)
            return 0
        lax.fori_loop(0, nb, one, 0)
        c = pltpu.make_async_copy(stv.at[:, g], stat_ref.at[:, g], out_sem.at[1 + g])
        c.start()
        outs.append(c)

    tables[0].wait()
    tables[1].wait()
    z_send(0)
    z_send(1)
    z_own(0)
    z_relay(0)
    z_send(2)
    z_own(1)
    z_relay(1)
    forward(0)
    z_relay(2)
    z_send(3)
    z_own(2)
    z_own(3)
    forward(1)
    forward(2)
    z_relay(3)
    forward(3)

    for b in range(nb):
        rows = slice(b * 128, b * 128 + 128)
        a = []
        for j in range(6):
            a.append(jnp.concatenate([att[b, h // 3, (h % 3) * 128:(h % 3) * 128 + 128, :][:, 64:] for h in (2 * j, 2 * j + 1)], axis=1))
        a = jnp.concatenate(a, axis=1).astype(F32)
        root = jnp.sqrt(jnp.sum(a * a, axis=1, keepdims=True) * (1.0 / 768) + EPSILON)
        normed = a / root
        lay[rows, :] = dot(normed.astype(BF16), wo_ref[...]).astype(BF16)
        n = ng[rows, :]
        a = ((n - normed * (jnp.sum(n * normed, axis=1, keepdims=True) * (1.0 / 768))) / root).astype(BF16)
        for h in range(12):
            x = a[:, (h // 2) * 128:(h // 2) * 128 + 128][:, (h % 2) * 64:(h % 2) * 64 + 64]
            dov[b, h // 3, (h % 3) * 128:(h % 3) * 128 + 128, :] = jnp.concatenate([zero, x], axis=1)
    for i, (src, dst) in enumerate(((dov, dop_ref), (lay, lay_ref))):
        c = pltpu.make_async_copy(src, dst, out_sem.at[5 + i])
        c.start()
        outs.append(c)
    for b in (nb - 2, nb - 1):
        entries(3, b, b % 2).wait()
    for c in outs + tables[2:]:
        c.wait()
    for c in send.done:
        c.wait_send()


def forward_pass(tokens, grads, w_query, w_key, w_value, w_out, named, blocks):
    V, A = pl.BlockSpec(memory_space=pltpu.VMEM), pl.BlockSpec(memory_space=pl.ANY)
    bf = lambda *shape: jax.ShapeDtypeStruct(shape, BF16)
    i32 = lambda *shape: jax.ShapeDtypeStruct(shape, jnp.int32)
    vm = lambda *shape: pltpu.VMEM(shape, BF16)
    vi = lambda *shape: pltpu.VMEM(shape, jnp.int32)
    dma = lambda *shape: pltpu.SemaphoreType.DMA(shape)
    out = pl.pallas_call(
        forward_kernel,
        in_specs=[V] * 8,
        out_specs=[A] * 8,
        out_shape=[bf(512, 768), bf(4, 4, 384, 128), bf(4, 4, 384, 128), jax.ShapeDtypeStruct((4, 4, 384, 128), F32),
                   bf(4, 64, 128, 128), i32(64, 128), i32(64, 128), bf(2, 2, 4, 2, 512, 128)],
        scratch_shapes=[vm(4, CUTS[2 * h][p] + CUTS[2 * h + 1][p], 128) for p in range(3) for h in range(2)] + [
            vm(4, 4, 4, CUTS[2 * h][p] + CUTS[2 * h + 1][p], 128) for p in range(3) for h in range(2)] + [
            vm(3, 4, 4, 2, 512, 128)] + [vm(4, 4, 4, 2, 128, 128)] * 4 + [pltpu.VMEM((384, 2048), F32), vm(2, 16, 128, 128),
            vm(4, 4, 384, 128), vm(4, 4, 384, 128), pltpu.VMEM((4, 4, 384, 128), F32), vm(4, 4, 384, 128),
            pltpu.VMEM((512, 768), F32), vm(512, 768),
            vi(256, 128), vi(256, 128), vi(256, 128), vi(64, 128), vi(64, 128), vi(8, 128),
            pltpu.SMEM((64, 128), jnp.int32), pltpu.SMEM((8, 128), jnp.int32),
            dma(120), dma(120), dma(2, 6), dma(4), dma(2), dma(7)],
        compiler_params=pltpu.CompilerParams(collective_id=0, has_side_effects=True, vmem_limit_bytes=67043328),
        name="forward",
    )(tokens, grads, w_query, w_key, w_value, w_out, named, blocks)
    return out[:7]


def return_kernel(wanted, inv, qp_ref, dop_ref, stat_ref, ent_ref, wq_ref, wk_ref, wv_ref, out_ref, rl_ref,
                  kvb, qv, dov, stv, p, t, dqs, parts, stage, rz, sums, gs, yl, ys, hs, xl, xs, total, got, wq, flat, wkv,
                  send_sem, recv_sem, swap_sem, kv_sem, in_sem, w_sem):
    pos, core = place(), lax.axis_index("vintage")
    dims = [tuple(sorted(o[:2])) for o in ORDERS]
    send = Sender(pos, core, send_sem, recv_sem)
    nb = qv.shape[0]
    me = tile_of(pos)
    L = kvb.shape[1]
    greet(pos, core, False)

    def turn(axis, by):
        return lax.rem(pos[axis] + by, SIDE)

    def key(g, p, i):
        return (g * 3 + p) * 18 + i

    def load(g, b, slot):
        return pltpu.make_async_copy(ent_ref.at[g, pl.ds(b * L, L)], kvb.at[slot], kv_sem.at[slot])

    load(0, 0, 0).start()
    rows_in = [[pltpu.make_async_copy(src.at[:, g], dst.at[:, g % dst.shape[1]], in_sem.at[g, i])
                for i, (src, dst) in enumerate(((qp_ref, qv), (dop_ref, dov), (stat_ref, stv)))] for g in range(4)]
    for c in rows_in[0]:
        c.start()
    weights = [pltpu.make_async_copy(src, dst, w_sem.at[i]) for i, (src, dst) in enumerate(((wq_ref, wq), (wk_ref, flat.at[0:768]), (wv_ref, flat.at[768:1536])))]
    for c in weights:
        c.start()

    def backward(g):
        for c in rows_in[g]:
            c.wait()
        if g < 3:
            for c in rows_in[g + 1]:
                c.start()

        def one(b, _):
            cur = lax.rem(b, 2)
            load(g, b, cur).wait()

            @pl.when(b + 1 < nb)
            def _():
                load(g, b + 1, 1 - cur).start()

            if g < 3:
                @pl.when(b + 1 == nb)
                def _():
                    load(g + 1, 0, 0).start()

            kv = kvb[cur].reshape(L * 128, 128)
            q, do = qv[b, g % 2], dov[b, g % 2]
            m = jnp.broadcast_to(stv[b, g % 2, :, 0:1], (384, 128))
            nrm = jnp.broadcast_to(stv[b, g % 2, :, 64:65], (384, 128))
            s = dot(q, kv, 1, 1)
            dp = dot((do.astype(F32) * 0.125).astype(BF16), kv, 1, 1)
            rd = jnp.zeros((384, 128), F32)
            for i in range(L):
                cols = slice(i * 128, i * 128 + 128)
                pr = jnp.exp2((s[:, cols] - m) * SCALE) * nrm
                x = pr * dp[:, cols]
                p[:, cols] = pr
                t[:, cols] = x
                rd = rd + x
            rd = jnp.broadcast_to(jnp.sum(rd, axis=1, keepdims=True), (384, 128))
            ds_, low = [], []
            for i in range(L):
                cols = slice(i * 128, i * 128 + 128)
                pr = p[:, cols]
                ds_.append((t[:, cols] - pr * rd).astype(BF16))
                low.append(pr.astype(BF16))
            ds_, low = jnp.concatenate(ds_, axis=1), jnp.concatenate(low, axis=1)
            dqs[b, g] = dot(ds_, kv).astype(BF16)
            part = dot(jnp.concatenate([ds_, low], axis=0), jnp.concatenate([q, do], axis=0), 0, 0)
            parts[pl.ds(b * L, L)] = part.astype(BF16).reshape(L, 128, 128)
            return 0
        lax.fori_loop(0, nb, one, 0)

    zr, zd, zf, yr, yd, xr, xd = [{} for _ in range(7)]

    def slots_of(g, p, level, half=None):
        a3 = ORDERS[p][2]
        r0, rows = spans(g)[p]
        idx = []
        for d in range(3):
            if d == a3:
                idx.append(level)
            elif half is not None and d == dims[p][0]:
                idx.append(pl.ds(2 * half, 2))
            else:
                idx.append(slice(None))
        return stage.at[(g % 2,) + tuple(idx) + (slice(None), pl.ds(r0, rows), slice(None))]

    def at_rows(ref, g, p, lead):
        r0, rows = spans(g)[p]
        return ref.at[(g,) + tuple(lead) + (pl.ds(r0, rows), slice(None))]

    W = slice(None)

    def z_send(g):
        if g >= 2:
            for c in zr[g - 2] + zd[g - 2]:
                c.wait_send()

        def place_part(j, _):
            x, y, z = lax.div(j, 16), lax.rem(lax.div(j, 4), 4), lax.rem(j, 4)
            for s in range(2):
                stage[g % 2, x, y, z, s] = parts[inv[me, s * 64 + j]]
            return 0
        lax.fori_loop(0, 64, place_part, 0)
        if g == 0:
            greet_wait()
        zr[g], zd[g] = [], []
        for p in range(3):
            a3 = ORDERS[p][2]
            for i, by in enumerate((1, 3)):
                zr[g].append(send.copy(slots_of(g, p, turn(a3, 2), i), at_rows(rl_ref, g, p, (i, W, W, W)), key(g, p, i), a3, by))
        for p in range(3):
            a3 = ORDERS[p][2]
            for i, by in enumerate((1, 3)):
                zd[g].append(send.copy(slots_of(g, p, turn(a3, by)), at_rows(rz, g, p, (i, W, W, W)), key(g, p, 2 + i), a3, by))

    def z_relay(g):
        zf[g] = []
        for p in range(3):
            a3 = ORDERS[p][2]
            for i, by in enumerate((1, 3)):
                zr[g][p * 2 + i].wait_recv()
                zf[g].append(send.copy(at_rows(rl_ref, g, p, (i, W, W, W)), at_rows(rz, g, p, (2, pl.ds(2 * i, 2), W, W)),
                                       key(g, p, 4 + i), a3, by))

    def add_up(g, p, k, by, first, last):
        a3 = ORDERS[p][2]
        r0, rows = spans(g)[p]
        source = tile_of(shifted(pos, a3, by))

        def one(j, _):
            hi, lo = lax.div(j, SIDE), lax.rem(j, SIDE)
            holder = pos[a3] * STRIDE[a3] + hi * STRIDE[dims[p][0]] + lo * STRIDE[dims[p][1]]
            where = [None] * 3
            where[a3], where[dims[p][0]], where[dims[p][1]] = pos[a3], hi, lo
            vals = []
            for s in range(2):
                at = (k, hi, lo, s) if k < 3 else tuple(where) + (s,)
                ref, lead = (rz, g) if k < 3 else (stage, g % 2)
                vals.append(ref[(lead,) + at + (pl.ds(r0, rows), slice(None))].astype(F32))
            want = [wanted[source, s * 64 + holder] for s in range(2)]
            for b in range(4):
                x = jnp.where(want[0] == b, vals[0], 0.0) + jnp.where(want[1] == b, vals[1], 0.0)
                if not first:
                    x = x + sums[hi, lo, b, pl.ds(r0, rows), :]
                if last:
                    gs[g, hi, lo, b, pl.ds(r0, rows), :] = x.astype(BF16)
                else:
                    sums[hi, lo, b, pl.ds(r0, rows), :] = x
            return 0
        lax.fori_loop(0, SIDE * SIDE, one, 0)

    def z_sum(g):
        for p in range(3):
            add_up(g, p, 3, 0, True, False)
        for i, by in enumerate((3, 1)):
            for p in range(3):
                zd[g][p * 2 + i].wait_recv()
                add_up(g, p, i, by, False, False)

    def lines(g, p, axis, index, half=None):
        idx = []
        for d in dims[p]:
            if d == axis:
                idx.append(index)
            else:
                idx.append(slice(None) if half is None else pl.ds(2 * half, 2))
        return at_rows(gs, g, p, tuple(idx) + (W,))

    def y_send(g):
        yr[g], yd[g] = [], []
        for p in range(3):
            a2 = ORDERS[p][1]
            for c in zf[g][p * 2:p * 2 + 2]:
                c.wait_recv()
            add_up(g, p, 2, 2, False, True)
            for i, by in enumerate((1, 3)):
                yr[g].append(send.copy(lines(g, p, a2, turn(a2, 2), i), at_rows(yl, g, p, (i, W, W)), key(g, p, 6 + i), a2, by))

    def y_relay(g):
        for p in range(3):
            a1, a2, a3 = ORDERS[p]
            r0, rows = spans(g)[p]
            at = (pl.ds(r0, rows), slice(None))
            for i, by in enumerate((1, 3)):
                yr[g][p * 2 + i].wait_recv()

                def join(j, _, p=p, a1=a1, a2=a2, i=i, by=by, at=at):
                    i1, b = lax.div(j, 4), lax.rem(j, 4)
                    here = (g,) + tuple(2 * i + i1 if d == a1 else turn(a2, by) for d in dims[p]) + (b,) + at
                    gs[here] = (gs[here].astype(F32) + yl[(g, i, i1, b) + at].astype(F32)).astype(BF16)
                    return 0
                lax.fori_loop(0, 8, join, 0)
                yd[g].append(send.copy(lines(g, p, a2, turn(a2, by)), at_rows(ys, g, p, (i, W, W)), key(g, p, 8 + i), a2, by))

    def x_send(g):
        xr[g], xd[g] = [], []
        for p in range(3):
            a1, a2, a3 = ORDERS[p]
            r0, rows = spans(g)[p]
            at = (pl.ds(r0, rows), slice(None))
            for c in yd[g][p * 2:p * 2 + 2]:
                c.wait_recv()

            def row(j, _, p=p, a1=a1, a2=a2, at=at):
                i1, b = lax.div(j, 4), lax.rem(j, 4)
                mine = gs[(g,) + tuple(i1 if d == a1 else pos[a2] for d in dims[p]) + (b,) + at].astype(F32)
                for k in range(2):
                    mine = mine + ys[(g, k, i1, b) + at].astype(F32)
                hs[(g, i1, b) + at] = mine.astype(BF16)
                return 0
            lax.fori_loop(0, 16, row, 0)
        for p in range(3):
            a1 = ORDERS[p][0]
            for i, by in enumerate((1, 3)):
                xr[g].append(send.copy(at_rows(hs, g, p, (turn(a1, 2), pl.ds(2 * i, 2))), at_rows(xl, g, p, (i, W)), key(g, p, 12 + i), a1, by))

    def x_relay(g):
        for p in range(3):
            a1 = ORDERS[p][0]
            r0, rows = spans(g)[p]
            at = (pl.ds(r0, rows), slice(None))
            for i, by in enumerate((1, 3)):
                xr[g][p * 2 + i].wait_recv()
                for b in range(2):
                    here = (g, turn(a1, by), 2 * i + b) + at
                    hs[here] = (hs[here].astype(F32) + xl[(g, i, b) + at].astype(F32)).astype(BF16)
                xd[g].append(send.copy(at_rows(hs, g, p, (turn(a1, by), W)), at_rows(xs, g, p, (i, W)), key(g, p, 14 + i), a1, by))

    swaps = []

    def finish(g):
        for p in range(3):
            a1 = ORDERS[p][0]
            r0, rows = spans(g)[p]
            at = (pl.ds(r0, rows), slice(None))
            for c in xd[g][p * 2:p * 2 + 2]:
                c.wait_recv()
            for b in range(4):
                mine = hs[(g, pos[a1], b) + at].astype(F32)
                for k in range(2):
                    mine = mine + xs[(g, k, b) + at].astype(F32)
                total[(g, b) + at] = mine.astype(BF16)
        c = pltpu.make_async_remote_copy(
            src_ref=total.at[g], dst_ref=got.at[g], send_sem=swap_sem.at[0, g], recv_sem=swap_sem.at[1, g],
            device_id=(1 - core, tile_of(pos)), device_id_type=MESH)
        c.start()
        swaps.append(c)

    def sums_at(b):
        return slice(b % 3 * 128, b % 3 * 128 + 128), slice(b // 3 * 768, b // 3 * 768 + 768)

    def query_term(b):
        heads = [dqs[b, h // 3, (h % 3) * 128:(h % 3) * 128 + 128, :][:, :64] for h in range(12)]
        p[sums_at(b)] = dot(jnp.concatenate(heads, axis=1), wq[...], 1, 1)

    def key_term(half):
        for g in (2 * half, 2 * half + 1):
            swaps[g].wait()
        for b in range(nb):
            both = jnp.concatenate([got[2 * half, b], got[2 * half + 1, b]], axis=1)
            x = p[sums_at(b)] + dot(both, wkv[:, half * 256:half * 256 + 256], 1, 1)
            if half == 0:
                p[sums_at(b)] = x
            else:
                for i in range(3):
                    flat[i * 512 + b * 128:i * 512 + b * 128 + 128, :] = x[:, i * 256:i * 256 + 256].astype(BF16)

    backward(0)
    z_send(0)
    backward(1)
    z_relay(0)
    z_send(1)
    z_sum(0)
    backward(2)
    z_relay(1)
    z_send(2)
    y_send(0)
    z_sum(1)
    backward(3)
    z_relay(2)
    z_send(3)
    y_send(1)
    y_relay(0)
    z_sum(2)
    z_relay(3)
    y_send(2)
    y_relay(1)
    x_send(0)
    z_sum(3)
    y_send(3)
    y_relay(2)
    x_send(1)
    x_relay(0)
    for c in weights:
        c.wait()
    for g in range(4):
        wkv[:, g * 128:g * 128 + 128] = jnp.concatenate([flat[0:768, g * 64:g * 64 + 64], flat[768:1536, g * 64:g * 64 + 64]], axis=1)
    query_term(0)
    query_term(1)
    y_relay(3)
    x_send(2)
    x_relay(1)
    finish(0)
    query_term(2)
    query_term(3)
    x_send(3)
    x_relay(2)
    finish(1)
    x_relay(3)
    finish(2)
    key_term(0)
    finish(3)
    key_term(1)
    results = [pltpu.make_async_copy(flat.at[i * 512:i * 512 + 512], out_ref.at[:, i * 256:i * 256 + 256], w_sem.at[3 + i]) for i in range(3)]
    for c in results:
        c.start()
    for c in results:
        c.wait()
    for g in range(4):
        late = zr[g] + zd[g] if g >= 2 else []
        for c in late + zf[g] + yr[g] + yd[g] + xr[g] + xd[g]:
            c.wait_send()


def gather_back(wanted, inv, qp, dop, stat, ent, w_query, w_key, w_value):
    V, A = pl.BlockSpec(memory_space=pltpu.VMEM), pl.BlockSpec(memory_space=pl.ANY)
    S = pl.BlockSpec(memory_space=pltpu.SMEM)
    bf = lambda *shape: jax.ShapeDtypeStruct(shape, BF16)
    vm = lambda *shape: pltpu.VMEM(shape, BF16)
    out = pl.pallas_call(
        return_kernel,
        in_specs=[S, S] + [A] * 7,
        out_specs=[A] * 2,
        out_shape=[bf(512, 768), bf(4, 2, 2, 4, 2, 128, 128)],
        scratch_shapes=[
            vm(2, 16, 128, 128), vm(4, 2, 384, 128), vm(4, 2, 384, 128), pltpu.VMEM((4, 2, 384, 128), F32),
            pltpu.VMEM((384, 2048), F32), pltpu.VMEM((384, 2048), F32), vm(4, 4, 384, 128),
            vm(64, 128, 128), vm(2, 4, 4, 4, 2, 128, 128), vm(4, 3, 4, 4, 2, 128, 128),
            pltpu.VMEM((4, 4, 4, 128, 128), F32), vm(4, 4, 4, 4, 128, 128), vm(4, 2, 2, 4, 128, 128), vm(4, 2, 4, 4, 128, 128),
            vm(4, 4, 4, 128, 128), vm(4, 2, 2, 128, 128), vm(4, 2, 4, 128, 128), vm(4, 4, 128, 128), vm(4, 4, 128, 128),
            vm(768, 768), vm(1536, 256), vm(768, 512),
            pltpu.SemaphoreType.DMA((216,)), pltpu.SemaphoreType.DMA((216,)), pltpu.SemaphoreType.DMA((2, 4)),
            pltpu.SemaphoreType.DMA((2,)), pltpu.SemaphoreType.DMA((4, 3)), pltpu.SemaphoreType.DMA((6,))],
        compiler_params=pltpu.CompilerParams(collective_id=1, has_side_effects=True, vmem_limit_bytes=67043328),
        name="collect",
    )(wanted, inv, qp, dop, stat, ent, w_query, w_key, w_value)
    return out[0]


def finish_kernel(layer_ref, total_ref, layer_out, total_out):
    layer_out[...] = layer_ref[...]
    total_out[...] = total_ref[...]


def finish(layer, total):
    block = pl.BlockSpec((256, 768), lambda i: (i, 0))
    shape = jax.ShapeDtypeStruct((512, 768), BF16)
    return pl.pallas_call(finish_kernel, grid=(2,), in_specs=[block] * 2, out_specs=[block] * 2, out_shape=[shape] * 2,
                          name="finish")(layer, total)


def shards(patches, out_grad, w_query, w_key, w_value, w_out, key_tiles, key_blocks):
    layer, qp, dop, stat, ent, wanted, inv = forward_pass(
        patches[0], out_grad[0], w_query, w_key, w_value, w_out, key_tiles[0].T, key_blocks[0].T)
    total = gather_back(wanted, inv, qp, dop, stat, ent, w_query, w_key, w_value)
    layer, total = finish(layer, total)
    return layer[None], total[None]


def solution(mesh):
    cubes = P("vintage", "tile", None)
    lists = P("vintage", None, None)
    return jax.shard_map(shards, mesh=mesh, in_specs=(cubes, cubes, P(), P(), P(), P(), lists, lists),
                         out_specs=(cubes, cubes), check_vma=False)
```
